32 devices in a mesh: gx: 4 (over z), gy: 8 (over y, x, core).
Axes of the slice: x: 2, y: 2, z: 4, core: 2. Of those that a mesh axis runs over, the one named last changes fastest.
Arguments:
- sample_field: float32 [128, 256, 256], P('gx', 'gy'), may hold values from -4 to 4
- mean_shift: float32 [128, 256, 256], P('gx', 'gy'), may hold values from -18 to 18
- class_map: int32 [128, 256, 256], P('gx', 'gy'), may hold values from 0 to 7
- noise_seed: int32 [128, 256, 256], P('gx', 'gy'), may hold values from 0 to 32703
- diffusion_table: float32 [8], replicated, may hold values from 0.5 to 4
- mass_table: float32 [8], replicated, may hold values from 0.1 to 2
Outputs:
- fine_sample: float32 [128, 256, 256], P('gx', 'gy')
- coarse_sample: float32 [16, 32, 32], P('gx', 'gy')
The draws below stay inside these ranges and needn't reach their ends.
All inputs are finite; a program needn't handle non-finite values.
Results may differ from the reference program's by a relative error of at most 0.0001.
Values sent between devices are 32-bit elements; how exact they have to be, the bound alone decides.
No kernel may reach another device: no remote copies, remote signals or barrier semaphores. Data moves between devices by JAX's collectives and lax.ppermute only.
A program may use at most 192 MiB of HBM per device.

```python
import math
import jax
import jax.numpy as jnp
from jax import lax

SWEEPS = 3
LEVELS = 4
CLASSES = 8
NX = 128
NY = 256
NZ = 256


def with_ends(entries, stream_key, low, top_value):
    longest = entries.shape.index(max(entries.shape))
    spots = []
    for shift in (0, 1):
        where = [jax.random.randint(jax.random.fold_in(stream_key, axis), (), 0, length) for axis, length in enumerate(entries.shape)]
        where[longest] = (where[longest] + shift) % entries.shape[longest]
        spots.append(tuple(where))
    return entries.at[spots[0]].set(low).at[spots[1]].set(top_value)


def levels(rng, extent, split, least, high):
    factor_of, own = 1.0, jax.random.fold_in(rng, 6)
    for dim, parts in split:
        draws = jnp.exp(jax.random.uniform(jax.random.fold_in(own, dim), (parts,), jnp.float32, least / len(split), high / len(split)))
        factor_of = factor_of * jnp.repeat(draws, extent[dim] // parts).reshape([-1 if axis == dim else 1 for axis in range(len(extent))])
    return factor_of


def bell_draw(rng, dims, scale, limit, shards=(), dtype=jnp.bfloat16):
    drawn = jax.random.normal(rng, dims, jnp.float32) * scale
    if len(shards) > 0:
        drawn = levels(rng, dims, shards, -0.22, 0.18) * drawn
    return jnp.clip(drawn, min=-limit, max=limit).astype(dtype)


def setup_inputs(seed: int = 0) -> dict:
    streams_of = jax.random.split(jax.random.key(seed), 7)
    return {
        "sample_field": bell_draw(streams_of[0], (NX, NY, NZ), 0.5, 4.0, ((0, 4), (1, 8)), jnp.float32),
        "mean_shift": bell_draw(streams_of[1], (NX, NY, NZ), 3.0, 18.0, ((0, 4), (1, 8)), jnp.float32),
        "class_map": with_ends(jax.random.randint(streams_of[2], (NX, NY, NZ), 0, CLASSES), jax.random.fold_in(streams_of[2], 1), 0, CLASSES - 1).astype(jnp.int32),
        "noise_seed": with_ends(jax.random.randint(streams_of[3], (NX, NY, NZ), 0, 32704), jax.random.fold_in(streams_of[3], 1), 0, 32703).astype(jnp.int32),
        "diffusion_table": jnp.clip(jnp.exp(jax.random.uniform(streams_of[4], (CLASSES,), jnp.float32, math.log(0.5), math.log(4.0))), 0.5, 4.0),
        "mass_table": jnp.clip(jnp.exp(jax.random.uniform(streams_of[5], (CLASSES,), jnp.float32, math.log(0.1), math.log(2.0))), 0.1, 2.0),
    }


def lookup(class_map, table):
    result = jnp.zeros(class_map.shape, jnp.float32)
    for class_index in range(table.shape[0]):
        result = jnp.where(class_map == class_index, table[class_index], result)
    return result

def coarsen(values):
    rows_x, rows_y, rows_z = values.shape
    return values.reshape(rows_x // 2, 2, rows_y // 2, 2, rows_z // 2, 2).mean(axis=(1, 3, 5))

def gaussian(seed_field, tag_value):
    first_hash = (seed_field * 40503 + (tag_value + 1) * 12347) % 65521
    second_hash = (seed_field * 30011 + (tag_value + 1) * 7919) % 65519
    first_uniform = (first_hash.astype(jnp.float32) + 0.5) / 65521.0
    second_uniform = (second_hash.astype(jnp.float32) + 0.5) / 65519.0
    return jnp.sqrt(-2.0 * jnp.log(first_uniform)) * jnp.cos(6.283185307179586 * second_uniform)

def face_weights(diff_padded, mass_field, grid_scale):
    centre = diff_padded[1:-1, 1:-1]
    column = jnp.pad(centre, ((0, 0), (0, 0), (1, 1)))
    neighbours = [diff_padded[2:, 1:-1], diff_padded[:-2, 1:-1], diff_padded[1:-1, 2:], diff_padded[1:-1, :-2], column[:, :, 2:], column[:, :, :-2]]
    weights = [grid_scale * 0.5 * (centre + neighbour) for neighbour in neighbours]
    diagonal = mass_field
    for weight in weights:
        diagonal = diagonal + weight
    return (weights, diagonal)

def neighbour_sum(field_padded, weights):
    centre = field_padded[1:-1, 1:-1]
    column = jnp.pad(centre, ((0, 0), (0, 0), (1, 1)))
    neighbours = [field_padded[2:, 1:-1], field_padded[:-2, 1:-1], field_padded[1:-1, 2:], field_padded[1:-1, :-2], column[:, :, 2:], column[:, :, :-2]]
    running = weights[0] * neighbours[0]
    for position in range(1, 6):
        running = running + weights[position] * neighbours[position]
    return running

def heat_bath(current, diagonal, beside_sum, right_side, noise_field, chosen):
    updated = (right_side + beside_sum) / diagonal + noise_field * lax.rsqrt(diagonal)
    return jnp.where(chosen, updated, current)

def parity(block_shape, offset_x, offset_y, colour):
    index_x = lax.broadcasted_iota(jnp.int32, block_shape, 0) + offset_x
    index_y = lax.broadcasted_iota(jnp.int32, block_shape, 1) + offset_y
    index_z = lax.broadcasted_iota(jnp.int32, block_shape, 2)
    return (index_x + index_y + index_z) % 2 == colour

def restrict(residual_padded):

    def along_axis(values, axis_number):
        span_length = values.shape[axis_number] - 1
        thirds = [lax.slice_in_dim(values, anchor, anchor + span_length - 1, stride=2, axis=axis_number) for anchor in range(3)]
        return 0.5 * thirds[0] + thirds[1] + 0.5 * thirds[2]
    return 0.25 * along_axis(along_axis(along_axis(residual_padded, 0), 1), 2)

def pad_plane(values, width):
    return jnp.pad(values, ((width, width), (width, width), (0, 0)))

def reference(sample_field, mean_shift, class_map, noise_seed, diffusion_table, mass_table):
    diffusion = lookup(class_map, diffusion_table)
    mass_field = lookup(class_map, mass_table)
    right_side = mean_shift
    current = sample_field
    fine_sample = sample_field
    for level_index in range(LEVELS):
        grid_scale = 0.5 ** level_index
        factor = 2 ** level_index
        if level_index > 0:
            diffusion = coarsen(diffusion)
            mass_field = coarsen(mass_field)
            current = jnp.zeros_like(right_side)
        seed_field = noise_seed[::factor, ::factor, ::factor]
        weights, diagonal = face_weights(pad_plane(diffusion, 1), mass_field, grid_scale)
        for sweep_index in range(SWEEPS):
            noise_field = gaussian(seed_field, level_index * SWEEPS + sweep_index)
            for colour in range(2):
                beside_sum = neighbour_sum(pad_plane(current, 1), weights)
                current = heat_bath(current, diagonal, beside_sum, right_side, noise_field, parity(current.shape, 0, 0, colour))
        if level_index == 0:
            fine_sample = current
        if level_index < LEVELS - 1:
            beside_sum = neighbour_sum(pad_plane(current, 1), weights)
            residual = right_side - (diagonal * current - beside_sum)
            right_side = restrict(jnp.pad(residual, ((1, 0), (1, 0), (1, 0))))
    return (fine_sample, current)
```

```python
import functools

import jax
import jax.numpy as jnp
import numpy as np
from jax import lax
from jax.experimental import pallas as pl
from jax.experimental.pallas import tpu as pltpu
from jax.sharding import PartitionSpec as P

SWEEPS = 3
LEVELS = 4
LANES = 128
HALO = 8
PRIMES = (65521, 65519)
FACTORS = (40503, 30011)
STEPS = (12347, 7919)


def sine_terms(count):
    nodes = 0.25 * np.cos(np.pi * (np.arange(64) + 0.5) / 64)
    design = np.stack([nodes ** (2 * n + 1) for n in range(count)], axis=1)
    fit = np.linalg.lstsq(design, np.sin(2 * np.pi * nodes), rcond=None)[0]
    return [float(c) for c in fit]


SINE = sine_terms(6)


def hash_base(seed, which):
    gap = 65536 - PRIMES[which]
    v = seed * FACTORS[which]
    v = (v >> 16) * gap + (v & 65535)
    v = (v >> 16) * gap + (v & 65535)
    v = jnp.where(v >= PRIMES[which], v - PRIMES[which], v)
    return v.astype(jnp.float32)


def hash_step(base, which, tag):
    prime = float(PRIMES[which])
    h = base + float(((tag + 1) * STEPS[which]) % PRIMES[which])
    return jnp.where(h >= prime, h - prime, h)


def scaled_noise(base1, base2, tag, minus_two_inverse):
    h1 = hash_step(base1, 0, tag)
    h2 = hash_step(base2, 1, tag)
    u1 = h1 * (1.0 / PRIMES[0]) + 0.5 / PRIMES[0]
    v = jnp.log(u1) * minus_two_inverse
    radius = v * lax.rsqrt(jnp.maximum(v, 1e-30))
    z = jnp.abs(h2 - float(PRIMES[1] // 2)) * (1.0 / PRIMES[1]) - 0.25
    zz = z * z
    poly = jnp.full_like(zz, SINE[-1])
    for term in SINE[-2::-1]:
        poly = poly * zz + term
    return radius * (poly * z)


def dot32(a, b):
    return jnp.dot(a, b, preferred_element_type=jnp.float32, precision=lax.Precision.HIGHEST)


def lane_matrix(rows, kind):
    k = lax.broadcasted_iota(jnp.int32, (rows, LANES), 0)
    half = 2 * lax.broadcasted_iota(jnp.int32, (rows, LANES), 1)
    if kind == "pick":
        return (k == half).astype(jnp.float32)
    if kind == "pair":
        return ((k == half) | (k == half + 1)).astype(jnp.float32)
    near = (k == half - 1) | (k == half + 1)
    return jnp.where(k == half, 0.25, jnp.where(near, 0.125, 0.0))


def table_lookup(classes, table_ref, row, count):
    result = jnp.zeros(classes.shape, jnp.float32)
    for n in range(count):
        result = jnp.where(classes == n, table_ref[row, n], result)
    return result


def statics_kernel(shapes, classes, tab_ref, cls_ref, seed_ref, *refs):
    outs, (t_ref, u_ref) = refs[: 3 * (LEVELS - 1)], refs[3 * (LEVELS - 1) :]
    for level in range(1, LEVELS):
        ni, nj, nk = shapes[level - 1]
        rows = ni // 2 * nj
        width = max(nk, LANES)
        for what in range(3):
            for q in range(ni // 2):
                if level == 1:
                    if what < 2:
                        a = table_lookup(cls_ref[2 * q], tab_ref, what, classes)
                        a = a + table_lookup(cls_ref[2 * q + 1], tab_ref, what, classes)
                    else:
                        a = seed_ref[2 * q].astype(jnp.float32)
                else:
                    prev = outs[3 * (level - 2) + what]
                    a = prev[2 * q]
                    if what < 2:
                        a = a + prev[2 * q + 1]
                t_ref[pl.ds(q * nj, nj), :width] = a
            matrix = lane_matrix(width, "pair" if what < 2 else "pick")
            u_ref[pl.ds(0, rows), :] = dot32(t_ref[pl.ds(0, rows), :width], matrix)
            even = u_ref[pl.ds(0, rows // 2, stride=2), :]
            if what < 2:
                even = 0.125 * (even + u_ref[pl.ds(1, rows // 2, stride=2), :])
            outs[3 * (level - 1) + what][...] = even.reshape(ni // 2, nj // 2, LANES)


def coarse_statics(table, class_map, noise_seed):
    ni, nj, nk = class_map.shape
    shapes = [(ni >> n, nj >> n, nk >> n) for n in range(LEVELS)]
    outs = []
    for level in range(1, LEVELS):
        outs += [jax.ShapeDtypeStruct((*shapes[level][:2], LANES), jnp.float32)] * 3
    vmem = pl.BlockSpec(memory_space=pltpu.VMEM)
    got = pl.pallas_call(
        functools.partial(statics_kernel, shapes, table.shape[1]),
        out_shape=tuple(outs),
        in_specs=[pl.BlockSpec(memory_space=pltpu.SMEM), vmem, vmem],
        out_specs=tuple([vmem] * len(outs)),
        scratch_shapes=[
            pltpu.VMEM((ni // 2 * nj, nk), jnp.float32),
            pltpu.VMEM((ni // 2 * nj, LANES), jnp.float32),
        ],
        name="coarse_statics",
    )(table, class_map, noise_seed)
    return [got[3 * n : 3 * n + 3] for n in range(LEVELS - 1)]


def level_kernel(level, dims, classes, *refs):
    ni, nj, nk, w = dims
    first, last = level == 0, level == LEVELS - 1
    count_i, count_j = ni + 2 * w, nj + 2 * w
    pairs = count_i // 2
    refs = list(refs)
    tab_ref = refs.pop(0) if first else None
    arrays = 4 if not first else 4
    own = [refs.pop(0) for _ in range(arrays)]
    if w:
        x_lo, x_hi, y_lo, y_hi = [refs.pop(0) for _ in range(4)]
    outs = [refs.pop(0) for _ in range(2 if first else 1)]
    d_ref, m_ref, s_ref, r_ref, w_ref, x_ref = refs[:6]
    t_ref, u_ref = refs[6:] if not last else (None, None)

    shape = (count_j, nk)
    lane = lax.broadcasted_iota(jnp.int32, shape, 1)
    row = lax.broadcasted_iota(jnp.int32, shape, 0)
    even = ((lane + row) & 1) == 0
    scale = 0.5 * 0.5**level

    def plane(a, e, where):
        if where == 0:
            mid = x_lo[a * w + e]
        elif where == 1:
            mid = own[a][e - w]
        else:
            mid = x_hi[a * w + e - (w + ni)]
        if not w:
            return mid
        at = a * count_i + e
        mid = mid.astype(jnp.float32)
        return jnp.concatenate([mid, y_hi[at], y_lo[at]], axis=0)

    def half_plane(q, where):
        a, h = 3, w // 2
        if where == 0:
            mid = x_lo[a * w + q]
        elif where == 1:
            both = (own[a][2 * q - w], own[a][2 * q - w + 1])
            own_even = even[:nj]
            mid = jnp.where(own_even, both[1], both[0])
        else:
            mid = x_hi[a * w + q - (h + ni // 2)]
        at = a * count_i + q
        return jnp.concatenate([mid, y_hi[at], y_lo[at]], axis=0)

    zero = jnp.zeros(shape, jnp.float32)
    for c in range(2):
        for g in (0, pairs + 1):
            d_ref[c, g] = zero
            x_ref[c, g] = zero

    def split(q, where):
        def put(ref, slot, values):
            ref[0, q + slot] = jnp.where(even, values[0], values[1])
            ref[1, q + slot] = jnp.where(even, values[1], values[0])

        e = (2 * q, 2 * q + 1)
        if first:
            cls = [plane(0, n, where).astype(jnp.int32) for n in e]
            for c in range(2):
                here = jnp.where(even, cls[c], cls[1 - c])
                d_ref[c, q + 1] = table_lookup(here, tab_ref, 0, classes)
                m_ref[c, q] = table_lookup(here, tab_ref, 1, classes)
            put(s_ref, 0, [plane(1, n, where) for n in e])
            put(r_ref.at[0], 0, [plane(2, n, where) for n in e])
            x_ref[1, q + 1] = half_plane(q, where)
        else:
            put(d_ref, 1, [plane(0, n, where) for n in e])
            put(m_ref, 0, [plane(1, n, where) for n in e])
            put(s_ref, 0, [plane(2, n, where) for n in e])
            put(r_ref.at[0], 0, [plane(3, n, where) for n in e])
            x_ref[1, q + 1] = zero

    def loop(start, stop, body):
        def step(q, carry):
            body(q)
            return carry

        lax.fori_loop(start, stop, step, 0)

    h = w // 2
    if w:
        loop(0, h, lambda q: split(q, 0))
    loop(h, h + ni // 2, lambda q: split(q, 1))
    if w:
        loop(h + ni // 2, pairs, lambda q: split(q, 2))

    def around(ref, c, q):
        other = 1 - c
        mid = ref[other, q + 1]
        above, below = ref[other, q + 2], ref[other, q]
        beside = jnp.where(even, below, above) if c == 0 else jnp.where(even, above, below)
        return [
            mid,
            beside,
            pltpu.roll(mid, count_j - 1, 0),
            pltpu.roll(mid, 1, 0),
            pltpu.roll(mid, nk - 1, 1),
            pltpu.roll(mid, 1, 1),
        ]

    def prepare(q):
        for c in range(2):
            d = d_ref[c, q + 1]
            near = around(d_ref, c, q)
            near[4] = jnp.where(lane == nk - 1, 0.0, near[4])
            near[5] = jnp.where(lane == 0, 0.0, near[5])
            total = 6.0 * d
            for v in near:
                total = total + v
            diagonal = jnp.where(d > 0.0, m_ref[c, q] + scale * total, 0.0)
            inverse = jnp.where(d > 0.0, 1.0 / diagonal, 0.0)
            m_ref[c, q] = diagonal
            part = scale * inverse
            near[4] = jnp.where(lane == nk - 1, -d, near[4])
            near[5] = jnp.where(lane == 0, -d, near[5])
            for n in range(6):
                w_ref[n, c, q] = part * (d + near[n])
            r_ref[1, c, q] = inverse

    loop(0, pairs, prepare)

    step = 16 if count_j % 16 == 0 else 8

    def noises(q):
        for c in range(2):
            for at in range(0, count_j, step):
                rows = pl.ds(at, step)
                seed = s_ref[c, q, rows].astype(jnp.int32)
                base1, base2 = hash_base(seed, 0), hash_base(seed, 1)
                inverse = r_ref[1, c, q, rows]
                minus_two = -2.0 * inverse
                b = r_ref[0, c, q, rows] * inverse
                for t in range(SWEEPS):
                    noise = scaled_noise(base1, base2, level * SWEEPS + t, minus_two)
                    r_ref[t, c, q, rows] = b + noise
                s_ref[c, q, rows] = noise

    loop(0, pairs, noises)

    def gathered(c, q):
        total = None
        for n, v in enumerate(around(x_ref, c, q)):
            term = w_ref[n, c, q] * v
            total = term if total is None else total + term
        return total

    for half in range(2 * SWEEPS):
        t, c = half // 2, half % 2

        def update(q, t=t, c=c):
            x_ref[c, q + 1] = r_ref[t, c, q] + gathered(c, q)

        if w:
            loop(half // 2, (ni + w + 2 * SWEEPS - half) // 2 + 1, update)
        else:
            loop(0, pairs, update)

    if last:
        own_even = even[:nj]

        def write(q):
            red, black = x_ref[0, q + 1], x_ref[1, q + 1]
            outs[0][2 * q] = jnp.where(even, red, black)
            outs[0][2 * q + 1] = jnp.where(even, black, red)

        loop(0, pairs, write)
        return

    if first:

        def write(q):
            red, black = x_ref[0, q + h + 1, :nj], x_ref[1, q + h + 1, :nj]
            outs[0][2 * q] = jnp.where(even[:nj], red, black)
            outs[0][2 * q + 1] = jnp.where(even[:nj], black, red)

        loop(0, ni // 2, write)

    def residual(q):
        red = r_ref[SWEEPS - 1, 0, q] - s_ref[0, q] + gathered(0, q) - x_ref[0, q + 1]
        r_ref[0, 0, q] = m_ref[0, q] * red
        r_ref[0, 1, q] = -m_ref[1, q] * s_ref[1, q]

    loop(h - 1, h + ni // 2, residual)

    def restrict(q):
        p = q + h
        red, black = r_ref[0, 0, p], r_ref[0, 1, p]
        red_before, black_before = r_ref[0, 0, p - 1], r_ref[0, 1, p - 1]
        at = jnp.where(even, red, black)
        sides = jnp.where(even, black, red) + jnp.where(even, black_before, red_before)
        v = at + 0.5 * sides
        v = v + 0.5 * (pltpu.roll(v, count_j - 1, 0) + pltpu.roll(v, 1, 0))
        t_ref[pl.ds(pl.multiple_of(q * count_j, 8), count_j), :] = v

    loop(0, ni // 2, restrict)
    u_ref[...] = dot32(t_ref[...], lane_matrix(nk, "restrict"))
    size = ni // 2 * count_j // 2
    coarse = u_ref[pl.ds(0, size, stride=2), :].reshape(ni // 2, count_j // 2, LANES)
    outs[-1][...] = coarse[:, : nj // 2, :]


def run_level(level, own, halos, table=None):
    ni, nj, nk = own[0].shape
    w = HALO if halos else 0
    first, last = level == 0, level == LEVELS - 1
    count_i, count_j = ni + 2 * w, nj + 2 * w
    pairs = count_i // 2
    outs = []
    if first or last:
        outs.append(jax.ShapeDtypeStruct((ni, nj, nk), jnp.float32))
    if not last:
        outs.append(jax.ShapeDtypeStruct((ni // 2, nj // 2, LANES), jnp.float32))
    scratch = [
        pltpu.VMEM((2, pairs + 2, count_j, nk), jnp.float32),
        pltpu.VMEM((2, pairs, count_j, nk), jnp.float32),
        pltpu.VMEM((2, pairs, count_j, nk), jnp.float32),
        pltpu.VMEM((SWEEPS, 2, pairs, count_j, nk), jnp.float32),
        pltpu.VMEM((6, 2, pairs, count_j, nk), jnp.float32),
        pltpu.VMEM((2, pairs + 2, count_j, nk), jnp.float32),
    ]
    if not last:
        scratch += [
            pltpu.VMEM((ni // 2 * count_j, nk), jnp.float32),
            pltpu.VMEM((ni // 2 * count_j, LANES), jnp.float32),
        ]
    vmem = pl.BlockSpec(memory_space=pltpu.VMEM)
    args = list(own) + list(halos)
    specs = [vmem] * len(args)
    if first:
        args = [table] + args
        specs = [pl.BlockSpec(memory_space=pltpu.SMEM)] + specs
    classes = table.shape[1] if first else 0
    got = pl.pallas_call(
        functools.partial(level_kernel, level, (ni, nj, nk, w), classes),
        out_shape=tuple(outs),
        in_specs=specs,
        out_specs=tuple([vmem] * len(outs)),
        scratch_shapes=scratch,
        compiler_params=pltpu.CompilerParams(vmem_limit_bytes=60 * 1024 * 1024),
        name=f"level_{level}",
    )(*args)
    return got


def both_ways(to_next, to_previous, axis):
    size = lax.axis_size(axis)
    up = [(i, i + 1) for i in range(size - 1)]
    down = [(j, i) for i, j in up]
    return lax.ppermute(to_next, axis, up), lax.ppermute(to_previous, axis, down)


def halo_exchange(arrays, black=None):
    w = HALO
    ni, nj, nk = arrays[0].shape
    low = [a[:w] for a in arrays]
    high = [a[ni - w :] for a in arrays]
    if black is not None:
        low.append(black[: w // 2])
        high.append(black[ni // 2 - w // 2 :])
    from_low, from_high = both_ways(jnp.concatenate(high), jnp.concatenate(low), "gx")
    low_rows, high_rows = [], []
    sizes = [w] * len(arrays)
    mids = list(arrays)
    if black is not None:
        sizes.append(w // 2)
        mids.append(black)
    at = 0
    for mid, size in zip(mids, sizes):
        part = slice(at, at + size)
        at += size
        for rows, where in ((slice(0, w), low_rows), (slice(nj - w, nj), high_rows)):
            where += [from_low[part, rows], mid[:, rows], from_high[part, rows]]
    left, right = both_ways(jnp.concatenate(high_rows), jnp.concatenate(low_rows), "gy")
    return (from_low, from_high, left, right)


def per_device(sample_field, mean_shift, class_map, noise_seed, diffusion_table, mass_table):
    zero = jnp.zeros((1,), jnp.float32)
    table = jnp.stack(
        [
            jnp.concatenate([zero, diffusion_table]),
            jnp.concatenate([zero, mass_table]),
        ]
    )
    ni, nj, nk = class_map.shape
    statics = coarse_statics(table[:, 1:], class_map, noise_seed)
    index = lax.broadcasted_iota(jnp.int32, (ni // 2, nj, nk), 1)
    index = index + lax.broadcasted_iota(jnp.int32, (ni // 2, nj, nk), 2)
    planes = sample_field.reshape(ni // 2, 2, nj, nk)
    black = jnp.where((index & 1) == 0, planes[:, 1], planes[:, 0])
    cls = (class_map + 1).astype(jnp.float32)
    seed = noise_seed.astype(jnp.float32)
    arrays = [cls, seed, mean_shift]
    halos = halo_exchange(arrays, black)
    fine, rhs = run_level(0, arrays + [sample_field], halos, table)
    for level in range(1, LEVELS - 1):
        arrays = list(statics[level - 1]) + [rhs]
        (rhs,) = run_level(level, arrays, halo_exchange(arrays))
    lanes = nk >> (LEVELS - 1)
    arrays = list(statics[-1]) + [rhs]
    packed = jnp.concatenate([a[:, :, :lanes] for a in arrays], axis=2)
    gx, gy = lax.axis_size("gx"), lax.axis_size("gy")
    mi, mj, mk = packed.shape
    spread = jnp.broadcast_to(packed[None], (gx * gy, mi, mj, mk))
    all_blocks = lax.all_to_all(spread, ("gx", "gy"), 0, 0, tiled=True)
    grid = all_blocks.reshape(gx, gy, mi, mj, mk).transpose(0, 2, 1, 3, 4)
    grid = grid.reshape(gx * mi, gy * mj, mk)
    pad = ((0, 0), (0, 8), (0, LANES - lanes))
    whole = [jnp.pad(grid[:, :, n * lanes : (n + 1) * lanes], pad) for n in range(4)]
    (coarse,) = run_level(LEVELS - 1, whole, ())
    start = (lax.axis_index("gx") * mi, lax.axis_index("gy") * mj, 0)
    return fine, lax.dynamic_slice(coarse, start, (mi, mj, lanes))


def solution(mesh):
    spec = P("gx", "gy", None)
    return jax.shard_map(
        per_device,
        mesh=mesh,
        in_specs=(spec, spec, spec, spec, P(), P()),
        out_specs=(spec, spec),
        check_vma=False,
    )
```

```python
import functools

import jax
import jax.numpy as jnp
import numpy as np
from jax import lax
from jax.experimental import pallas as pl
from jax.experimental.pallas import tpu as pltpu
from jax.sharding import PartitionSpec as P

SWEEPS = 3
LEVELS = 4
LANES = 128
FINE_HALO = 4
FINE_LIMIT = 40
HALO = 8
PRIMES = (65521, 65519)
FACTORS = (40503, 30011)
STEPS = (12347, 7919)


def sine_terms(count):
    nodes = 0.25 * np.cos(np.pi * (np.arange(64) + 0.5) / 64)
    design = np.stack([nodes ** (2 * n + 1) for n in range(count)], axis=1)
    fit = np.linalg.lstsq(design, np.sin(2 * np.pi * nodes), rcond=None)[0]
    return [float(c) for c in fit]


SINE = sine_terms(6)


def hash_base(seed, which):
    gap = 65536 - PRIMES[which]
    v = seed * FACTORS[which]
    v = (v >> 16) * gap + (v & 65535)
    v = (v >> 16) * gap + (v & 65535)
    v = jnp.where(v >= PRIMES[which], v - PRIMES[which], v)
    return v.astype(jnp.float32)


def hash_step(base, which, tag):
    prime = float(PRIMES[which])
    h = base + float(((tag + 1) * STEPS[which]) % PRIMES[which])
    return jnp.where(h >= prime, h - prime, h)


def raw_noise(base1, base2, tag):
    h1 = hash_step(base1, 0, tag)
    h2 = hash_step(base2, 1, tag)
    u1 = h1 * (1.0 / PRIMES[0]) + 0.5 / PRIMES[0]
    v = -2.0 * jnp.log(u1)
    radius = v * lax.rsqrt(v)
    z = jnp.abs(h2 - float(PRIMES[1] // 2)) * (1.0 / PRIMES[1]) - 0.25
    zz = z * z
    poly = jnp.full_like(zz, SINE[-1])
    for term in SINE[-2::-1]:
        poly = poly * zz + term
    return radius * (poly * z)


def raw_noises(seed, level):
    base1, base2 = hash_base(seed, 0), hash_base(seed, 1)
    return [raw_noise(base1, base2, level * SWEEPS + t) for t in range(SWEEPS)]


def dot32(a, b):
    return jnp.dot(a, b, preferred_element_type=jnp.float32, precision=lax.Precision.HIGHEST)


def lane_matrix(rows, kind):
    k = lax.broadcasted_iota(jnp.int32, (rows, LANES), 0)
    half = 2 * lax.broadcasted_iota(jnp.int32, (rows, LANES), 1)
    if kind == "pick":
        return (k == half).astype(jnp.float32)
    if kind == "pair":
        return ((k == half) | (k == half + 1)).astype(jnp.float32)
    near = (k == half - 1) | (k == half + 1)
    return jnp.where(k == half, 0.25, jnp.where(near, 0.125, 0.0))


def lookups(numbers, tables):
    results = [jnp.zeros(numbers.shape, jnp.float32) for _ in tables]
    for n in range(tables[0].shape[0]):
        hit = numbers == n + 1
        results = [jnp.where(hit, table[n], result) for table, result in zip(tables, results)]
    return results


def loop(start, stop, body, unroll=1):
    if stop - start <= unroll:
        for q in range(start, stop):
            body(q)
        return

    def step(n, carry):
        for u in range(unroll):
            body(start + n * unroll + u)
        return carry

    whole = (stop - start) // unroll
    lax.fori_loop(0, whole, step, 0)
    for q in range(start + whole * unroll, stop):
        body(q)


def checker(shape):
    return ((lax.broadcasted_iota(jnp.int32, shape, 0) + lax.broadcasted_iota(jnp.int32, shape, 1)) & 1) == 0


def has_neighbours(axis):
    at = lax.axis_index(axis)
    last = lax.axis_size(axis) - 1
    return (at > 0).astype(jnp.float32), (at < last).astype(jnp.float32)


VMEM = pl.BlockSpec(memory_space=pltpu.VMEM)
SMEM = pl.BlockSpec(memory_space=pltpu.SMEM)


def f32(*shape):
    return jax.ShapeDtypeStruct(shape, jnp.float32)


def call(kernel, name, outs, args, specs=None, scratch=(), limit=None):
    return pl.pallas_call(
        kernel,
        out_shape=tuple(outs),
        in_specs=specs or [VMEM] * len(args),
        out_specs=tuple([VMEM] * len(outs)),
        scratch_shapes=list(scratch),
        compiler_params=pltpu.CompilerParams(vmem_limit_bytes=(limit or 24) * 1024 * 1024),
        name=name,
    )(*args)


def pack_planes(class_map, noise_seed, mean_shift, sample_field):
    ni, nj, nk = class_map.shape
    w = FINE_HALO
    arrays = (class_map, noise_seed, mean_shift, sample_field)

    def kernel(*refs):
        even = checker((nj, nk))
        for out, ins in ((refs[9], refs[0:8:2]), (refs[8], refs[1:8:2])):
            for e in range(w):
                out[e] = (ins[0][e] + 1).astype(jnp.float32)
                out[w + e] = ins[1][e].astype(jnp.float32)
                out[2 * w + e] = ins[2][e]
            for q in range(w // 2):
                out[3 * w + q] = jnp.where(even, ins[3][2 * q + 1], ins[3][2 * q])

    first = pl.BlockSpec((w, nj, nk), lambda n: (0, 0, 0))
    last = pl.BlockSpec((w, nj, nk), lambda n: (ni // w - 1, 0, 0))
    whole = pl.BlockSpec((3 * w + w // 2, nj, nk), lambda n: (0, 0, 0))
    return pl.pallas_call(
        kernel,
        grid=(1,),
        out_shape=(f32(3 * w + w // 2, nj, nk),) * 2,
        in_specs=[first, last] * 4,
        out_specs=(whole, whole),
        name="pack_planes",
    )(*[a for a in arrays for _ in range(2)])


def edge_specs(shape):
    n, nj, nk = shape
    low = pl.BlockSpec((n, 8, nk), lambda g: (0, 0, 0))
    high = pl.BlockSpec((n, 8, nk), lambda g: (0, nj // 8 - 1, 0))
    return [low, high]


def pack_rows_fine(from_low, from_high, class_map, noise_seed, mean_shift, sample_field):
    ni, nj, nk = class_map.shape
    w = FINE_HALO
    count = ni + 2 * w
    arrays = (from_low, from_high, class_map, noise_seed, mean_shift, sample_field)

    def kernel(*refs):
        to_next, to_previous = refs[12:]
        even = checker((8, nk))
        for out, ins, rows in (
            (to_previous, refs[0:12:2], slice(0, w)),
            (to_next, refs[1:12:2], slice(8 - w, 8)),
        ):
            low, high, own = ins[0], ins[1], ins[2:]
            for a in range(3):
                for e in range(w):
                    out[a * count + e] = low[a * w + e, rows]
                    out[a * count + ni + w + e] = high[a * w + e, rows]
                for e in range(ni):
                    if a == 0:
                        v = (own[0][e, rows] + 1).astype(jnp.float32)
                    else:
                        v = own[a][e, rows].astype(jnp.float32)
                    out[a * count + w + e] = v
            base = 3 * count
            for q in range(w // 2):
                out[base + q] = low[3 * w + q, rows]
                out[base + (ni + w) // 2 + q] = high[3 * w + q, rows]
            for q in range(ni // 2):
                v = jnp.where(even, own[3][2 * q + 1], own[3][2 * q])
                out[base + w // 2 + q] = v[rows]

    total = 3 * count + count // 2
    whole = pl.BlockSpec((total, w, nk), lambda g: (0, 0, 0))
    return pl.pallas_call(
        kernel,
        grid=(1,),
        out_shape=(f32(total, w, nk),) * 2,
        in_specs=[s for a in arrays for s in edge_specs(a.shape)],
        out_specs=(whole, whole),
        name="pack_rows_fine",
    )(*[a for a in arrays for _ in range(2)])


def pack_rows(triples, w, name):
    parts = [a for triple in triples for a in triple]
    nk = parts[0].shape[2]
    total = sum(p.shape[0] for p in parts)

    def kernel(*refs):
        to_next, to_previous = refs[-2:]
        at = 0
        for n, part in enumerate(parts):
            size = part.shape[0]
            for e in range(size):
                to_previous[at + e] = refs[2 * n][e, slice(0, w)]
                to_next[at + e] = refs[2 * n + 1][e, slice(8 - w, 8)]
            at += size

    whole = pl.BlockSpec((total, w, nk), lambda g: (0, 0, 0))
    return pl.pallas_call(
        kernel,
        grid=(1,),
        out_shape=(f32(total, w, nk),) * 2,
        in_specs=[s for a in parts for s in edge_specs(a.shape)],
        out_specs=(whole, whole),
        name=name,
    )(*[a for a in parts for _ in range(2)])


def pack_static_rows(static_planes, statics1, statics2):
    w = HALO
    h = w // 2
    sizes = (statics1[0].shape, statics2[0].shape)
    total = 3 * sum(s[0] + 2 * w for s in sizes)

    def kernel(low, high, *refs):
        to_next, to_previous = refs[-2:]
        at = 0
        for level in range(2):
            ni, nj, _ = sizes[level]
            for a in range(3):
                own = refs[3 * level + a]
                for out, start in ((to_previous, 0), (to_next, nj - w)):
                    for src, base in ((low, 0), (high, w + ni)):
                        for e in range(w):
                            if level == 0:
                                v = src[a * w + e, pl.ds(start, w)]
                            else:
                                v = src[3 * w + a * h + e // 2, pl.ds(e % 2 * nj + start, w)]
                            out[at + base + e] = v
                    for e in range(ni):
                        out[at + w + e] = own[e, pl.ds(start, w)]
                at += ni + 2 * w

    args = (*static_planes, *statics1, *statics2)
    return call(kernel, "pack_rows_static", [f32(total, w, LANES)] * 2, args)


def coarse_statics(tables, class_map, noise_seed):
    ni, nj, nk = class_map.shape
    shapes = [(ni >> n, nj >> n, nk >> n) for n in range(LEVELS)]
    w = HALO

    def kernel(d_tab, m_tab, cls_ref, seed_ref, *refs):
        outs, (to_next, to_previous, packed), (t_ref, u_ref) = refs[:6], refs[6:9], refs[9:]
        for level in range(1, LEVELS):
            mi, mj, mk = shapes[level - 1]
            rows = mi // 2 * mj
            width = max(mk, LANES)
            for what in range(3):

                def gather(q):
                    if level == 1:
                        if what < 2:
                            tab = (d_tab, m_tab)[what]
                            (a,) = lookups(cls_ref[2 * q] + 1, [tab])
                            (b,) = lookups(cls_ref[2 * q + 1] + 1, [tab])
                            a = a + b
                        else:
                            a = seed_ref[2 * q].astype(jnp.float32)
                    else:
                        prev = outs[3 * (level - 2) + what]
                        a = prev[2 * q]
                        if what < 2:
                            a = a + prev[2 * q + 1]
                    t_ref[pl.ds(q * mj, mj), :width] = a

                for q in range(mi // 2):
                    gather(q)
                matrix = lane_matrix(width, "pair" if what < 2 else "pick")
                u_ref[pl.ds(0, rows), :] = dot32(t_ref[pl.ds(0, rows), :width], matrix)
                even = u_ref[pl.ds(0, rows // 2, stride=2), :]
                if what < 2:
                    even = 0.125 * (even + u_ref[pl.ds(1, rows // 2, stride=2), :])
                if level < LEVELS - 1:
                    outs[3 * (level - 1) + what][...] = even.reshape(mi // 2, mj // 2, LANES)
                else:
                    lanes = mk // 2
                    if what:
                        even = pltpu.roll(even, what * lanes, 1)
                    total = even if what == 0 else total + even
        packed[...] = total.reshape(shapes[-1][0], shapes[-1][1], LANES)
        mj = shapes[1][1]
        for what in range(3):
            one, two = outs[what], outs[3 + what]
            for e in range(w):
                to_previous[what * w + e] = one[e]
                to_next[what * w + e] = one[shapes[1][0] - w + e]
                n = what * w + e
                at = (3 * w + n // 2, pl.ds(n % 2 * (mj // 2), mj // 2))
                to_previous[at] = two[e]
                to_next[at] = two[shapes[2][0] - w + e]

    outs = []
    for level in range(1, LEVELS - 1):
        outs += [f32(*shapes[level][:2], LANES)] * 3
    outs += [f32(3 * w + 3 * w // 2, shapes[1][1], LANES)] * 2
    outs += [f32(*shapes[-1][:2], LANES)]
    scratch = [
        pltpu.VMEM((ni // 2 * nj, nk), jnp.float32),
        pltpu.VMEM((ni // 2 * nj, LANES), jnp.float32),
    ]
    args = (*tables, class_map, noise_seed)
    got = call(kernel, "coarse_statics", outs, args, [SMEM, SMEM, VMEM, VMEM], scratch)
    return got[:3], got[3:6], got[6], got[7], got[8]


def around(red_black, c, q, even, roll_rows, roll_lanes):
    ref = red_black[1 - c]
    mid, above, below = ref[q + 1], ref[q + 2], ref[q]
    beside = jnp.where(even, below, above) if c == 0 else jnp.where(even, above, below)
    return [
        mid,
        beside,
        pltpu.roll(mid, roll_rows - 1, 0),
        pltpu.roll(mid, 1, 0),
        pltpu.roll(mid, roll_lanes - 1, 1),
        pltpu.roll(mid, 1, 1),
    ]


class Stencil:
    def __init__(self, level, shape):
        self.rows, self.lanes = shape
        self.scale = 0.5 * 0.5**level
        self.lane = lax.broadcasted_iota(jnp.int32, shape, 1)
        self.even = checker(shape)

    def around(self, refs, c, q):
        return around(refs, c, q, self.even, self.rows, self.lanes)

    def weights(self, d_refs, mass, c, q):
        d = d_refs[c][q + 1]
        near = self.around(d_refs, c, q)
        at_end, at_start = self.lane == self.lanes - 1, self.lane == 0
        near[4] = jnp.where(at_end, 0.0, near[4])
        near[5] = jnp.where(at_start, 0.0, near[5])
        total = 6.0 * d
        for v in near:
            total = total + v
        inside = d > 0.0
        diagonal = jnp.where(inside, mass + self.scale * total, 0.0)
        inverse = jnp.where(inside, 1.0 / diagonal, 0.0)
        part = self.scale * inverse
        near[4] = jnp.where(at_end, -d, near[4])
        near[5] = jnp.where(at_start, -d, near[5])
        return diagonal, inverse, [part * (d + v) for v in near]

    def gathered(self, x_refs, w_ref, c, q):
        total = None
        for n, v in enumerate(self.around(x_refs, c, q)):
            term = w_ref[n, c, q] * v
            total = term if total is None else total + term
        return total

    def whole(self, red, black):
        return jnp.where(self.even, red, black), jnp.where(self.even, black, red)


def restricted(st, res_ref, first_pair, ni, nj, t_ref, u_ref, unroll):
    def gather(q):
        p = q + first_pair
        at, after = st.whole(res_ref[0, p], res_ref[1, p])
        _, before = st.whole(res_ref[0, p - 1], res_ref[1, p - 1])
        v = at + 0.5 * (before + after)
        v = v + 0.5 * (pltpu.roll(v, st.rows - 1, 0) + pltpu.roll(v, 1, 0))
        t_ref[pl.ds(pl.multiple_of(q * st.rows, 8), st.rows), :] = v

    loop(0, ni // 2, gather, unroll)
    u_ref[...] = dot32(t_ref[...], lane_matrix(st.lanes, "restrict"))
    size = ni // 2 * st.rows // 2
    coarse = u_ref[pl.ds(0, size, stride=2), :].reshape(ni // 2, st.rows // 2, LANES)
    return coarse[:, : nj // 2, :]


def restrict_scratch(ni, st_rows, nk):
    return [
        pltpu.VMEM((ni // 2 * st_rows, nk), jnp.float32),
        pltpu.VMEM((ni // 2 * st_rows, LANES), jnp.float32),
    ]


def own_noise(noise_seed):
    ni, nj, nk = noise_seed.shape

    def kernel(seed_ref, out):
        even = checker((nj, nk))

        def body(q):
            for c in range(2):
                for at in range(0, nj, 16):
                    rows = pl.ds(at, 16)
                    mask = even[at : at + 16]
                    seeds = (seed_ref[2 * q, rows], seed_ref[2 * q + 1, rows])
                    seed = jnp.where(mask, seeds[c], seeds[1 - c])
                    for t, g in enumerate(raw_noises(seed, 0)):
                        out[t, c, q, rows] = g

        loop(0, ni // 2, body)

    (out,) = call(kernel, "own_noise", [f32(SWEEPS, 2, ni // 2, nj, nk)], (noise_seed,))
    return out


def halo_noise(from_low, from_high):
    w = FINE_HALO
    nj, nk = from_low.shape[1:]

    def kernel(low, high, out_low, out_high):
        even = checker((nj, nk))
        for src, out in ((low, out_low), (high, out_high)):

            def body(q):
                for c in range(2):
                    for at in range(0, nj, 16):
                        rows = pl.ds(at, 16)
                        mask = even[at : at + 16]
                        seeds = (src[w + 2 * q, rows], src[w + 2 * q + 1, rows])
                        seed = jnp.where(mask, seeds[c], seeds[1 - c]).astype(jnp.int32)
                        for t, g in enumerate(raw_noises(seed, 0)):
                            out[t, c, q, rows] = g

            loop(0, w // 2, body)

    return call(kernel, "halo_noise", [f32(SWEEPS, 2, w // 2, nj, nk)] * 2, (from_low, from_high))


def fine_start(tables, own, noise, planes, plane_noise, rows):
    class_map, mean_shift, sample_field = own
    ni, nj, nk = class_map.shape
    w = FINE_HALO
    h = w // 2
    count = ni + 2 * w
    pairs = count // 2
    count_j = nj + 2 * w

    def kernel(d_tab, m_tab, cls_ref, b_ref, sample, g_own, x_lo, x_hi, g_lo, g_hi, y_lo, y_hi, *refs):
        w_ref, r3_ref, n3_ref, m_ref, xb_ref, to_next, to_previous = refs[:7]
        d0, d1, r_ref, x0, x1 = refs[7:]
        d_refs, x_refs = (d0, d1), (x0, x1)
        shape = (count_j, nk)
        st = Stencil(0, shape)
        even, own_even = st.even, st.even[:nj]
        edge_even = st.even[nj:]
        has_low, has_high = has_neighbours("gy")
        zero = jnp.zeros(shape, jnp.float32)
        for g in (0, pairs + 1):
            for ref in (*d_refs, *x_refs):
                ref[g] = zero

        def edge(at, mask=False):
            hi, lo = y_hi[at], y_lo[at]
            if mask:
                hi, lo = hi * has_high, lo * has_low
            return jnp.concatenate([hi, lo], axis=0)

        def split(q, where):
            e = (2 * q, 2 * q + 1)
            if where == 1:
                mids = [(cls_ref[n - w] + 1).astype(jnp.float32) for n in e]
                bs = [b_ref[n - w] for n in e]
                x = jnp.where(own_even, sample[e[1] - w], sample[e[0] - w])
                g_ref, g_at = g_own, q - h
            else:
                src, g_ref = ((x_lo, g_lo) if where == 0 else (x_hi, g_hi))
                off = 0 if where == 0 else -(w + ni)
                mids = [src[n + off] for n in e]
                bs = [src[2 * w + n + off] for n in e]
                g_at = q + off // 2
                x = src[3 * w + g_at]
            cls = [jnp.concatenate([mids[c], edge(e[c], True)], axis=0) for c in range(2)]
            b = [jnp.concatenate([bs[c], edge(2 * count + e[c])], axis=0) for c in range(2)]
            x1[q + 1] = jnp.concatenate([x, edge(3 * count + q, True)], axis=0)
            seeds = [edge(count + e[c]) for c in range(2)]
            for c in range(2):
                number = jnp.where(even, cls[c], cls[1 - c]).astype(jnp.int32)
                d, m = lookups(number, [d_tab, m_tab])
                d_refs[c][q + 1] = d
                m_ref[c, q] = m
                r_ref[0, c, q] = jnp.where(even, b[c], b[1 - c])
                seed = jnp.where(edge_even, seeds[c], seeds[1 - c]).astype(jnp.int32)
                for t, g in enumerate(raw_noises(seed, 0)):
                    out = n3_ref if t == SWEEPS - 1 else r_ref.at[t + 1]
                    out[c, q] = jnp.concatenate([g_ref[t, c, g_at], g], axis=0)

        loop(0, h, lambda q: split(q, 0))
        loop(h, h + ni // 2, lambda q: split(q, 1))
        loop(h + ni // 2, pairs, lambda q: split(q, 2))

        def prepare(q):
            for c in range(2):
                diagonal, inverse, weights = st.weights(d_refs, m_ref[c, q], c, q)
                m_ref[c, q] = diagonal
                for n in range(6):
                    w_ref[n, c, q] = weights[n]
                root = jnp.where(inverse > 0.0, lax.rsqrt(diagonal), 0.0)
                b = r_ref[0, c, q] * inverse
                noise = n3_ref[c, q] * root
                n3_ref[c, q] = noise
                r3_ref[c, q] = b + noise
                r_ref[0, c, q] = b + r_ref[1, c, q] * root
                r_ref[1, c, q] = b + r_ref[2, c, q] * root

        loop(0, pairs, prepare)

        for half in range(2 * SWEEPS - 2):
            t, c = half // 2, half % 2

            def update(q, t=t, c=c):
                x_refs[c][q + 1] = r_ref[t, c, q] + st.gathered(x_refs, w_ref, c, q)

            loop((half + 1) // 2, pairs - (half + 1) // 2, update)

        def write(q):
            xb_ref[q] = x1[q + h + 1, :nj]

        loop(0, ni // 2, write, 4)
        for q in range(h):
            to_previous[q] = x1[q + h + 1, :nj]
            to_next[q] = x1[ni // 2 + q + 1, :nj]

    state = f32(2, pairs, count_j, nk)
    outs = [f32(6, 2, pairs, count_j, nk), state, state, state]
    outs += [f32(ni // 2, nj, nk), f32(h, nj, nk), f32(h, nj, nk)]
    scratch = [
        pltpu.VMEM((pairs + 2, count_j, nk), jnp.float32),
        pltpu.VMEM((pairs + 2, count_j, nk), jnp.float32),
        pltpu.VMEM((SWEEPS, 2, pairs, count_j, nk), jnp.float32),
        pltpu.VMEM((pairs + 2, count_j, nk), jnp.float32),
        pltpu.VMEM((pairs + 2, count_j, nk), jnp.float32),
    ]
    args = (*tables, class_map, mean_shift, sample_field, noise, *planes, *plane_noise, *rows)
    specs = [SMEM, SMEM] + [VMEM] * (len(args) - 2)
    return call(kernel, "fine_start", outs, args, specs, scratch, FINE_LIMIT)


def fine_finish(state, black, planes, rows):
    ni, nj, nk = black.shape[0] * 2, black.shape[1], black.shape[2]
    w = FINE_HALO
    h = w // 2
    pairs = (ni + 2 * w) // 2
    count_j = nj + 2 * w
    halo = HALO

    def kernel(w_ref, r3_ref, n3_ref, m_ref, xb_ref, x_lo, x_hi, y_lo, y_hi, *refs):
        fine, rhs, to_next, to_previous = refs[:4]
        x0, x1, res_ref, t_ref, u_ref = refs[4:]
        x_refs = (x0, x1)
        shape = (count_j, nk)
        st = Stencil(0, shape)
        has_low, has_high = has_neighbours("gy")
        zero = jnp.zeros(shape, jnp.float32)
        for g in (0, pairs + 1):
            for ref in x_refs:
                ref[g] = zero

        def join(q, mid):
            x1[q + 1] = jnp.concatenate([mid, y_hi[q] * has_high, y_lo[q] * has_low], axis=0)

        for q in range(h):
            join(q, x_lo[q])
            join(h + ni // 2 + q, x_hi[q])
        loop(0, ni // 2, lambda q: join(h + q, xb_ref[q]), 4)

        for c, (start, stop) in enumerate(((0, pairs - 1), (1, pairs - 1))):

            def update(q, c=c):
                x_refs[c][q + 1] = r3_ref[c, q] + st.gathered(x_refs, w_ref, c, q)

            loop(start, stop, update)

        def residual(q):
            red = r3_ref[0, q] - n3_ref[0, q] + st.gathered(x_refs, w_ref, 0, q) - x0[q + 1]
            res_ref[0, q] = m_ref[0, q] * red
            res_ref[1, q] = -m_ref[1, q] * n3_ref[1, q]

        loop(h - 1, h + ni // 2, residual)

        def write(q):
            both = st.whole(x0[q + h + 1], x1[q + h + 1])
            fine[2 * q] = both[0][:nj]
            fine[2 * q + 1] = both[1][:nj]

        loop(0, ni // 2, write, 4)
        coarse = restricted(st, res_ref, h, ni, nj, t_ref, u_ref, 2)
        rhs[...] = coarse
        to_previous[...] = coarse[:halo]
        to_next[...] = coarse[ni // 2 - halo :]

    outs = [f32(ni, nj, nk), f32(ni // 2, nj // 2, LANES)] + [f32(halo, nj // 2, LANES)] * 2
    scratch = [
        pltpu.VMEM((pairs + 2, count_j, nk), jnp.float32),
        pltpu.VMEM((pairs + 2, count_j, nk), jnp.float32),
        pltpu.VMEM((2, pairs, count_j, nk), jnp.float32),
    ] + restrict_scratch(ni, count_j, nk)
    args = (*state, black, *planes, *rows)
    return call(kernel, "fine_finish", outs, args, None, scratch, FINE_LIMIT)


def level_sweeps(st, level, pairs, d_refs, m_ref, s_ref, r_ref, w_ref, x_refs, bounds, unroll):
    def prepare(q):
        for c in range(2):
            diagonal, inverse, weights = st.weights(d_refs, m_ref[c, q], c, q)
            m_ref[c, q] = diagonal
            for n in range(6):
                w_ref[n, c, q] = weights[n]
            root = jnp.where(inverse > 0.0, lax.rsqrt(diagonal), 0.0)
            b = r_ref[0, c, q] * inverse
            for t, g in enumerate(raw_noises(s_ref[c, q].astype(jnp.int32), level)):
                noise = g * root
                r_ref[t, c, q] = b + noise
            s_ref[c, q] = noise

    loop(0, pairs, prepare, min(unroll, 2))
    for half in range(2 * SWEEPS):
        t, c = half // 2, half % 2

        def update(q, t=t, c=c, half=half):
            if half == 0:
                x_refs[c][q + 1] = r_ref[t, c, q]
            else:
                x_refs[c][q + 1] = r_ref[t, c, q] + st.gathered(x_refs, w_ref, c, q)

        loop(*bounds(half), update, unroll)


def level_scratch(pairs, rows, lanes):
    guarded = pltpu.VMEM((pairs + 2, rows, lanes), jnp.float32)
    return [
        guarded,
        guarded,
        pltpu.VMEM((2, pairs, rows, lanes), jnp.float32),
        pltpu.VMEM((2, pairs, rows, lanes), jnp.float32),
        pltpu.VMEM((SWEEPS, 2, pairs, rows, lanes), jnp.float32),
        pltpu.VMEM((6, 2, pairs, rows, lanes), jnp.float32),
        guarded,
        guarded,
    ]


def middle_level(level, statics, static_planes, static_rows, rhs, rhs_planes, rhs_rows, tail=None):
    ni, nj, nk = rhs.shape
    w = HALO
    h = w // 2
    count, count_j = ni + 2 * w, nj + 2 * w
    pairs = count // 2
    to_coarsest = level == LEVELS - 2
    plane_base = 0 if level == 1 else 3 * w
    row_base = 0 if level == 1 else 3 * (2 * ni + 2 * w)
    members = lax.axis_size("gx") * lax.axis_size("gy")

    def kernel(*refs):
        refs = list(refs)
        own = refs[:4]
        sx_lo, sx_hi, sy_lo, sy_hi, bx_lo, bx_hi, by_lo, by_hi = refs[4:12]
        at = 12
        if to_coarsest:
            tail_ref, spread = refs[12:14]
            at = 14
        else:
            out, to_next, to_previous = refs[12:15]
            at = 15
        d0, d1, m_ref, s_ref, r_ref, w_ref, x0, x1, t_ref, u_ref = refs[at:]
        d_refs, x_refs = (d0, d1), (x0, x1)
        shape = (count_j, nk)
        st = Stencil(level, shape)
        x_has = has_neighbours("gx")
        y_has = has_neighbours("gy")
        zero = jnp.zeros(shape, jnp.float32)
        for g in (0, pairs + 1):
            for ref in (*d_refs, *x_refs):
                ref[g] = zero

        def static_plane(src, a, q, k):
            if level == 1:
                return src[a * w + 2 * q + k]
            return src[plane_base + a * h + q, pl.ds(k * nj, nj)]

        def fields(a, q, k, where):
            e = 2 * q + k
            if where == 1:
                mid = own[a][e - w]
            else:
                p = q if where == 0 else q - h - ni // 2
                if a < 3:
                    mid = static_plane((sx_lo, sx_hi)[where // 2], a, p, k)
                else:
                    mid = (bx_lo, bx_hi)[where // 2][2 * p + k]
                if a == 0:
                    mid = mid * x_has[where // 2]
            if a < 3:
                r = row_base + a * count + e
                hi, lo = sy_hi[r], sy_lo[r]
            else:
                hi, lo = by_hi[e], by_lo[e]
            if a == 0:
                hi, lo = hi * y_has[1], lo * y_has[0]
                if where != 1:
                    hi, lo = hi * x_has[where // 2], lo * x_has[where // 2]
            return jnp.concatenate([mid, hi, lo], axis=0)

        def split(q, where):
            for a in range(4):
                v = st.whole(fields(a, q, 0, where), fields(a, q, 1, where))
                for c in range(2):
                    if a == 0:
                        d_refs[c][q + 1] = v[c]
                    else:
                        (m_ref, s_ref, r_ref.at[0])[a - 1][c, q] = v[c]

        loop(0, h, lambda q: split(q, 0), 4)
        loop(h, h + ni // 2, lambda q: split(q, 1), 4)
        loop(h + ni // 2, pairs, lambda q: split(q, 2), 4)

        def bounds(half):
            return half // 2, (ni + w + 2 * SWEEPS - half) // 2 + 1

        level_sweeps(st, level, pairs, d_refs, m_ref, s_ref, r_ref, w_ref, x_refs, bounds, 4)

        def residual(q):
            red = r_ref[SWEEPS - 1, 0, q] - s_ref[0, q] + st.gathered(x_refs, w_ref, 0, q) - x0[q + 1]
            r_ref[0, 0, q] = m_ref[0, q] * red
            r_ref[0, 1, q] = -m_ref[1, q] * s_ref[1, q]

        loop(h - 1, h + ni // 2, residual, 4)
        coarse = restricted(st, r_ref.at[0], h, ni, nj, t_ref, u_ref, 4)
        if to_coarsest:
            lanes = nk // 4
            coarse = jnp.where(lax.broadcasted_iota(jnp.int32, coarse.shape, 2) < lanes, coarse, 0.0)
            block = tail_ref[...] + pltpu.roll(coarse, 3 * lanes, 2)
            for n in range(members):
                spread[n] = block
        else:
            out[...] = coarse
            to_previous[...] = coarse[:w]
            to_next[...] = coarse[ni // 2 - w :]

    args = [*statics, rhs, *static_planes, *static_rows, *rhs_planes, *rhs_rows]
    if to_coarsest:
        args.append(tail)
        outs = [f32(members, ni // 2, nj // 2, LANES)]
    else:
        outs = [f32(ni // 2, nj // 2, LANES)] + [f32(w, nj // 2, LANES)] * 2
    scratch = level_scratch(pairs, count_j, nk) + restrict_scratch(ni, count_j, nk)
    return call(kernel, f"level_{level}", outs, args, None, scratch)


def coarsest_level(blocks, lanes):
    members, mi, mj, _ = blocks.shape
    gx, gy = lax.axis_size("gx"), lax.axis_size("gy")
    pairs = gx * mi // 2
    nj = gy * mj
    count_j = nj + 8
    level = LEVELS - 1

    def kernel(blocks_ref, out, d0, d1, m_ref, s_ref, r_ref, w_ref, x0, x1, t_ref):
        d_refs, x_refs = (d0, d1), (x0, x1)
        shape = (count_j, LANES)
        st = Stencil(level, shape)
        zero = jnp.zeros(shape, jnp.float32)
        for g in (0, pairs + 1):
            for ref in (*d_refs, *x_refs):
                ref[g] = zero
        for i in range(gx * mi):
            for g in range(gy):
                t_ref[i, pl.ds(g * mj, mj), :] = blocks_ref[i // mi * gy + g, i % mi]
            t_ref[i, pl.ds(nj, 8), :] = jnp.zeros((8, LANES), jnp.float32)
        inside = st.lane < lanes

        def split(q):
            both = st.whole(t_ref[2 * q], t_ref[2 * q + 1])
            for a in range(4):
                for c in range(2):
                    v = both[c] if a == 0 else pltpu.roll(both[c], LANES - a * lanes, 1)
                    v = jnp.where(inside, v, 0.0)
                    if a == 0:
                        d_refs[c][q + 1] = v
                    else:
                        (m_ref, s_ref, r_ref.at[0])[a - 1][c, q] = v

        loop(0, pairs, split, 8)
        level_sweeps(
            st, level, pairs, d_refs, m_ref, s_ref, r_ref, w_ref, x_refs, lambda half: (0, pairs), 8
        )
        at_x, at_y = lax.axis_index("gx"), lax.axis_index("gy")
        for n in range(mi // 2):
            p = at_x * (mi // 2) + n + 1
            for k, v in enumerate(st.whole(x0[p], x1[p])):
                out[2 * n + k] = pltpu.roll(v, count_j - at_y * mj, 0)[:mj, :lanes]

    scratch = level_scratch(pairs, count_j, LANES)
    scratch += [pltpu.VMEM((gx * mi, count_j, LANES), jnp.float32)]
    (out,) = call(kernel, f"level_{level}", [f32(mi, mj, lanes)], (blocks,), None, scratch)
    return out


def both_ways(to_next, to_previous, axis, ring=True):
    size = lax.axis_size(axis)
    up = [(i, (i + 1) % size) for i in range(size if ring else size - 1)]
    down = [(j, i) for i, j in up]
    return lax.ppermute(to_next, axis, up), lax.ppermute(to_previous, axis, down)


def tied(first, *others):
    return lax.optimization_barrier((first, *others))[0]


def per_device(sample_field, mean_shift, class_map, noise_seed, diffusion_table, mass_table):
    tables = (diffusion_table, mass_table)
    nk = class_map.shape[2]
    arrays = (class_map, noise_seed, mean_shift, sample_field)

    planes = both_ways(*pack_planes(*arrays), "gx", False)
    noise = own_noise(noise_seed)
    statics1, statics2, static_next, static_previous, tail = coarse_statics(
        tables, class_map, noise_seed
    )
    planes = lax.optimization_barrier((*planes, noise, static_next))[:2]

    rows = both_ways(*pack_rows_fine(*planes, *arrays), "gy")
    plane_noise = halo_noise(*planes)
    rows = lax.optimization_barrier((*rows, *plane_noise))[:2]

    *state, black, to_next, to_previous = fine_start(
        tables, (class_map, mean_shift, sample_field), noise, planes, plane_noise, rows
    )
    planes = both_ways(to_next, to_previous, "gx", False)
    static_planes = both_ways(static_next, static_previous, "gx")
    rows = both_ways(*pack_rows([(planes[0], black, planes[1])], FINE_HALO, "pack_rows_black"), "gy")
    static_rows = both_ways(*pack_static_rows(static_planes, statics1, statics2), "gy")

    fine, rhs, to_next, to_previous = fine_finish(state, black, planes, rows)
    for level in range(1, LEVELS - 1):
        planes = both_ways(to_next, to_previous, "gx")
        rows = both_ways(*pack_rows([(planes[0], rhs, planes[1])], HALO, f"pack_rows_{level}"), "gy")
        statics = (statics1, statics2)[level - 1]
        last = level == LEVELS - 2
        got = middle_level(
            level, statics, static_planes, static_rows, rhs, planes, rows, tail if last else None
        )
        if not last:
            rhs, to_next, to_previous = got
    blocks = lax.all_to_all(got[0], ("gx", "gy"), 0, 0, tiled=True)
    return fine, coarsest_level(blocks, nk >> (LEVELS - 1))


def solution(mesh):
    spec = P("gx", "gy", None)
    return jax.shard_map(
        per_device,
        mesh=mesh,
        in_specs=(spec, spec, spec, spec, P(), P()),
        out_specs=(spec, spec),
        check_vma=False,
    )
```

```python
import functools

import jax
import jax.numpy as jnp
import numpy as np
from jax import lax
from jax.experimental import pallas as pl
from jax.experimental.pallas import tpu as pltpu
from jax.sharding import PartitionSpec as P

SWEEPS = 3
LEVELS = 4
LANES = 128
FINE_HALO = 4
START_LIMIT = 14
FINISH_LIMIT = 8
LEVEL_LIMIT = 12
HALO = 8
PRIMES = (65521, 65519)
FACTORS = (40503, 30011)
STEPS = (12347, 7919)


def sine_terms(count):
    nodes = 0.25 * np.cos(np.pi * (np.arange(64) + 0.5) / 64)
    design = np.stack([nodes ** (2 * n + 1) for n in range(count)], axis=1)
    fit = np.linalg.lstsq(design, np.sin(2 * np.pi * nodes), rcond=None)[0]
    return [float(c) for c in fit]


SINE = sine_terms(6)


def hash_base(seed, which):
    gap = 65536 - PRIMES[which]
    v = seed * FACTORS[which]
    v = (v >> 16) * gap + (v & 65535)
    v = (v >> 16) * gap + (v & 65535)
    v = jnp.where(v >= PRIMES[which], v - PRIMES[which], v)
    return v.astype(jnp.float32)


def hash_step(base, which, tag):
    prime = float(PRIMES[which])
    h = base + float(((tag + 1) * STEPS[which]) % PRIMES[which])
    return jnp.where(h >= prime, h - prime, h)


def raw_noise(base1, base2, tag):
    h1 = hash_step(base1, 0, tag)
    h2 = hash_step(base2, 1, tag)
    u1 = h1 * (1.0 / PRIMES[0]) + 0.5 / PRIMES[0]
    v = -2.0 * jnp.log(u1)
    radius = v * lax.rsqrt(v)
    z = jnp.abs(h2 - float(PRIMES[1] // 2)) * (1.0 / PRIMES[1]) - 0.25
    zz = z * z
    poly = jnp.full_like(zz, SINE[-1])
    for term in SINE[-2::-1]:
        poly = poly * zz + term
    return radius * (poly * z)


def raw_noises(seed, level):
    base1, base2 = hash_base(seed, 0), hash_base(seed, 1)
    return [raw_noise(base1, base2, level * SWEEPS + t) for t in range(SWEEPS)]


def dot32(a, b):
    return jnp.dot(a, b, preferred_element_type=jnp.float32, precision=lax.Precision.HIGHEST)


def lane_matrix(rows, kind):
    k = lax.broadcasted_iota(jnp.int32, (rows, LANES), 0)
    half = 2 * lax.broadcasted_iota(jnp.int32, (rows, LANES), 1)
    if kind == "pick":
        return (k == half).astype(jnp.float32)
    if kind == "pair":
        return ((k == half) | (k == half + 1)).astype(jnp.float32)
    near = (k == half - 1) | (k == half + 1)
    return jnp.where(k == half, 0.25, jnp.where(near, 0.125, 0.0))


def lookups(numbers, tables):
    results = [jnp.zeros(numbers.shape, jnp.float32) for _ in tables]
    for n in range(tables[0].shape[0]):
        hit = numbers == n + 1
        results = [jnp.where(hit, table[n], result) for table, result in zip(tables, results)]
    return results


def loop(start, stop, body, unroll=1):
    if stop - start <= unroll:
        for q in range(start, stop):
            body(q)
        return

    def step(n, carry):
        for u in range(unroll):
            body(start + n * unroll + u)
        return carry

    whole = (stop - start) // unroll
    lax.fori_loop(0, whole, step, 0)
    for q in range(start + whole * unroll, stop):
        body(q)


def checker(shape):
    return ((lax.broadcasted_iota(jnp.int32, shape, 0) + lax.broadcasted_iota(jnp.int32, shape, 1)) & 1) == 0


def has_neighbours(axis):
    at = lax.axis_index(axis)
    last = lax.axis_size(axis) - 1
    return (at > 0).astype(jnp.float32), (at < last).astype(jnp.float32)


VMEM = pl.BlockSpec(memory_space=pltpu.VMEM)
SMEM = pl.BlockSpec(memory_space=pltpu.SMEM)


def f32(*shape):
    return jax.ShapeDtypeStruct(shape, jnp.float32)


def call(kernel, name, outs, args, specs=None, scratch=(), limit=None):
    return pl.pallas_call(
        kernel,
        out_shape=tuple(outs),
        in_specs=specs or [VMEM] * len(args),
        out_specs=tuple([VMEM] * len(outs)),
        scratch_shapes=list(scratch),
        compiler_params=pltpu.CompilerParams(vmem_limit_bytes=(limit or 4) * 1024 * 1024),
        name=name,
    )(*args)


def pack_planes(class_map, noise_seed, mean_shift, sample_field):
    ni, nj, nk = class_map.shape
    w = FINE_HALO
    arrays = (class_map, noise_seed, mean_shift, sample_field)

    def kernel(*refs):
        even = checker((nj, nk))
        for out, ins in ((refs[9], refs[0:8:2]), (refs[8], refs[1:8:2])):
            for e in range(w):
                out[e] = (ins[0][e] + 1).astype(jnp.float32)
                out[w + e] = ins[1][e].astype(jnp.float32)
                out[2 * w + e] = ins[2][e]
            for q in range(w // 2):
                out[3 * w + q] = jnp.where(even, ins[3][2 * q + 1], ins[3][2 * q])

    first = pl.BlockSpec((w, nj, nk), lambda n: (0, 0, 0))
    last = pl.BlockSpec((w, nj, nk), lambda n: (ni // w - 1, 0, 0))
    whole = pl.BlockSpec((3 * w + w // 2, nj, nk), lambda n: (0, 0, 0))
    return pl.pallas_call(
        kernel,
        grid=(1,),
        out_shape=(f32(3 * w + w // 2, nj, nk),) * 2,
        in_specs=[first, last] * 4,
        out_specs=(whole, whole),
        compiler_params=pltpu.CompilerParams(vmem_limit_bytes=8 * 1024 * 1024),
        name="pack_planes",
    )(*[a for a in arrays for _ in range(2)])


def pack_rows_fine(from_low, from_high, class_map, noise_seed, mean_shift, sample_field):
    ni, nj, nk = class_map.shape
    w = FINE_HALO
    count = ni + 2 * w
    arrays = (from_low, from_high, class_map, noise_seed, mean_shift, sample_field)

    def kernel(*refs):
        low, high, *own = refs[:6]
        to_next, to_previous = refs[6:]
        even = checker((nj, nk))
        for out, start in ((to_previous, 0), (to_next, nj - w)):
            rows = pl.ds(start, w)
            mask = even[start : start + w]
            for a in range(3):
                for e in range(w):
                    out[a * count + e] = low[a * w + e, rows]
                    out[a * count + ni + w + e] = high[a * w + e, rows]
                for e in range(ni):
                    if a == 0:
                        v = (own[0][e, rows] + 1).astype(jnp.float32)
                    else:
                        v = own[a][e, rows].astype(jnp.float32)
                    out[a * count + w + e] = v
            base = 3 * count
            for q in range(w // 2):
                out[base + q] = low[3 * w + q, rows]
                out[base + (ni + w) // 2 + q] = high[3 * w + q, rows]
            for q in range(ni // 2):
                v = jnp.where(mask, own[3][2 * q + 1, rows], own[3][2 * q, rows])
                out[base + w // 2 + q] = v

    total = 3 * count + count // 2
    return call(kernel, "pack_rows_fine", [f32(total, w, nk)] * 2, arrays)


def pack_rows(triples, w, name):
    parts = [a for triple in triples for a in triple]
    nk = parts[0].shape[2]
    total = sum(p.shape[0] for p in parts)

    def kernel(*refs):
        to_next, to_previous = refs[-2:]
        at = 0
        for n, part in enumerate(parts):
            size, nj, _ = part.shape
            to_previous[pl.ds(at, size)] = refs[n][:, pl.ds(0, w)]
            to_next[pl.ds(at, size)] = refs[n][:, pl.ds(nj - w, w)]
            at += size

    return call(kernel, name, [f32(total, w, nk)] * 2, parts)


def pack_static_rows(static_planes, statics1, statics2):
    w = HALO
    h = w // 2
    sizes = (statics1[0].shape, statics2[0].shape)
    total = 3 * sum(s[0] + 2 * w for s in sizes)

    def kernel(low, high, *refs):
        to_next, to_previous = refs[-2:]
        at = 0
        for level in range(2):
            ni, nj, _ = sizes[level]
            for a in range(3):
                own = refs[3 * level + a]
                for out, start in ((to_previous, 0), (to_next, nj - w)):
                    for src, base in ((low, 0), (high, w + ni)):
                        for e in range(w):
                            if level == 0:
                                v = src[a * w + e, pl.ds(start, w)]
                            else:
                                v = src[3 * w + a * h + e // 2, pl.ds(e % 2 * nj + start, w)]
                            out[at + base + e] = v
                    for e in range(ni):
                        out[at + w + e] = own[e, pl.ds(start, w)]
                at += ni + 2 * w

    args = (*static_planes, *statics1, *statics2)
    return call(kernel, "pack_rows_static", [f32(total, w, LANES)] * 2, args)


def coarse_statics(tables, class_map, noise_seed):
    ni, nj, nk = class_map.shape
    shapes = [(ni >> n, nj >> n, nk >> n) for n in range(LEVELS)]
    w = HALO

    def kernel(d_tab, m_tab, cls_ref, seed_ref, *refs):
        outs, (to_next, to_previous, packed), (t_ref, u_ref) = refs[:6], refs[6:9], refs[9:]
        for level in range(1, LEVELS):
            mi, mj, mk = shapes[level - 1]
            rows = mi // 2 * mj
            width = max(mk, LANES)
            for what in range(3):

                def gather(q):
                    if level == 1:
                        if what < 2:
                            tab = (d_tab, m_tab)[what]
                            (a,) = lookups(cls_ref[2 * q] + 1, [tab])
                            (b,) = lookups(cls_ref[2 * q + 1] + 1, [tab])
                            a = a + b
                        else:
                            a = seed_ref[2 * q].astype(jnp.float32)
                    else:
                        prev = outs[3 * (level - 2) + what]
                        a = prev[2 * q]
                        if what < 2:
                            a = a + prev[2 * q + 1]
                    t_ref[pl.ds(q * mj, mj), :width] = a

                for q in range(mi // 2):
                    gather(q)
                matrix = lane_matrix(width, "pair" if what < 2 else "pick")
                u_ref[pl.ds(0, rows), :] = dot32(t_ref[pl.ds(0, rows), :width], matrix)
                even = u_ref[pl.ds(0, rows // 2, stride=2), :]
                if what < 2:
                    even = 0.125 * (even + u_ref[pl.ds(1, rows // 2, stride=2), :])
                if level < LEVELS - 1:
                    outs[3 * (level - 1) + what][...] = even.reshape(mi // 2, mj // 2, LANES)
                else:
                    lanes = mk // 2
                    if what:
                        even = pltpu.roll(even, what * lanes, 1)
                    total = even if what == 0 else total + even
        packed[...] = total.reshape(shapes[-1][0], shapes[-1][1], LANES)
        mj = shapes[1][1]
        for what in range(3):
            one, two = outs[what], outs[3 + what]
            for e in range(w):
                to_previous[what * w + e] = one[e]
                to_next[what * w + e] = one[shapes[1][0] - w + e]
                n = what * w + e
                at = (3 * w + n // 2, pl.ds(n % 2 * (mj // 2), mj // 2))
                to_previous[at] = two[e]
                to_next[at] = two[shapes[2][0] - w + e]

    outs = []
    for level in range(1, LEVELS - 1):
        outs += [f32(*shapes[level][:2], LANES)] * 3
    outs += [f32(3 * w + 3 * w // 2, shapes[1][1], LANES)] * 2
    outs += [f32(*shapes[-1][:2], LANES)]
    scratch = [
        pltpu.VMEM((ni // 2 * nj, nk), jnp.float32),
        pltpu.VMEM((ni // 2 * nj, LANES), jnp.float32),
    ]
    args = (*tables, class_map, noise_seed)
    got = call(kernel, "coarse_statics", outs, args, [SMEM, SMEM, VMEM, VMEM], scratch)
    return got[:3], got[3:6], got[6], got[7], got[8]


def around(red_black, c, q, even, roll_rows, roll_lanes):
    ref = red_black[1 - c]
    mid, above, below = ref[q + 1], ref[q + 2], ref[q]
    beside = jnp.where(even, below, above) if c == 0 else jnp.where(even, above, below)
    return [
        mid,
        beside,
        pltpu.roll(mid, roll_rows - 1, 0),
        pltpu.roll(mid, 1, 0),
        pltpu.roll(mid, roll_lanes - 1, 1),
        pltpu.roll(mid, 1, 1),
    ]


class Stencil:
    def __init__(self, level, shape):
        self.rows, self.lanes = shape
        self.scale = 0.5 * 0.5**level
        self.lane = lax.broadcasted_iota(jnp.int32, shape, 1)
        self.even = checker(shape)

    def around(self, refs, c, q):
        return around(refs, c, q, self.even, self.rows, self.lanes)

    def weights(self, d_refs, mass, c, q):
        d = d_refs[c][q + 1]
        near = self.around(d_refs, c, q)
        at_end, at_start = self.lane == self.lanes - 1, self.lane == 0
        near[4] = jnp.where(at_end, 0.0, near[4])
        near[5] = jnp.where(at_start, 0.0, near[5])
        total = 6.0 * d
        for v in near:
            total = total + v
        inside = d > 0.0
        diagonal = jnp.where(inside, mass + self.scale * total, 0.0)
        inverse = jnp.where(inside, 1.0 / diagonal, 0.0)
        part = self.scale * inverse
        near[4] = jnp.where(at_end, -d, near[4])
        near[5] = jnp.where(at_start, -d, near[5])
        return diagonal, inverse, [part * (d + v) for v in near]

    def gathered(self, x_refs, w_ref, c, q):
        total = None
        for n, v in enumerate(self.around(x_refs, c, q)):
            term = w_ref[n, c, q] * v
            total = term if total is None else total + term
        return total

    def whole(self, red, black):
        return jnp.where(self.even, red, black), jnp.where(self.even, black, red)


def restricted(st, res_ref, first_pair, ni, nj, t_ref, u_ref, unroll):
    def gather(q):
        p = q + first_pair
        at, after = st.whole(res_ref[0, p], res_ref[1, p])
        _, before = st.whole(res_ref[0, p - 1], res_ref[1, p - 1])
        v = at + 0.5 * (before + after)
        v = v + 0.5 * (pltpu.roll(v, st.rows - 1, 0) + pltpu.roll(v, 1, 0))
        t_ref[pl.ds(pl.multiple_of(q * st.rows, 8), st.rows), :] = v

    loop(0, ni // 2, gather, unroll)
    u_ref[...] = dot32(t_ref[...], lane_matrix(st.lanes, "restrict"))
    size = ni // 2 * st.rows // 2
    coarse = u_ref[pl.ds(0, size, stride=2), :].reshape(ni // 2, st.rows // 2, LANES)
    return coarse[:, : nj // 2, :]


def restrict_scratch(ni, st_rows, nk):
    return [
        pltpu.VMEM((ni // 2 * st_rows, nk), jnp.float32),
        pltpu.VMEM((ni // 2 * st_rows, LANES), jnp.float32),
    ]


def own_noise(noise_seed):
    ni, nj, nk = noise_seed.shape

    def kernel(seed_ref, out):
        even = checker((nj, nk))

        def body(q):
            for c in range(2):
                for at in range(0, nj, 16):
                    rows = pl.ds(at, 16)
                    mask = even[at : at + 16]
                    seeds = (seed_ref[2 * q, rows], seed_ref[2 * q + 1, rows])
                    seed = jnp.where(mask, seeds[c], seeds[1 - c])
                    for t, g in enumerate(raw_noises(seed, 0)):
                        out[t, c, q, rows] = g

        loop(0, ni // 2, body)

    (out,) = call(kernel, "own_noise", [f32(SWEEPS, 2, ni // 2, nj, nk)], (noise_seed,))
    return out


def halo_noise(from_low, from_high):
    w = FINE_HALO
    nj, nk = from_low.shape[1:]

    def kernel(low, high, out_low, out_high):
        even = checker((nj, nk))
        for src, out in ((low, out_low), (high, out_high)):

            def body(q):
                for c in range(2):
                    for at in range(0, nj, 16):
                        rows = pl.ds(at, 16)
                        mask = even[at : at + 16]
                        seeds = (src[w + 2 * q, rows], src[w + 2 * q + 1, rows])
                        seed = jnp.where(mask, seeds[c], seeds[1 - c]).astype(jnp.int32)
                        for t, g in enumerate(raw_noises(seed, 0)):
                            out[t, c, q, rows] = g

            loop(0, w // 2, body)

    return call(kernel, "halo_noise", [f32(SWEEPS, 2, w // 2, nj, nk)] * 2, (from_low, from_high))


def fine_start(tables, own, noise, planes, plane_noise, rows):
    class_map, mean_shift, sample_field = own
    ni, nj, nk = class_map.shape
    w = FINE_HALO
    h = w // 2
    count = ni + 2 * w
    pairs = count // 2
    count_j = nj + 2 * w

    def kernel(d_tab, m_tab, cls_ref, b_ref, sample, g_own, x_lo, x_hi, g_lo, g_hi, y_lo, y_hi, *refs):
        w_ref, r3_ref, n3_ref, m_ref, xb_ref, to_next, to_previous = refs[:7]
        d0, d1, r_ref, x0, x1 = refs[7:]
        d_refs, x_refs = (d0, d1), (x0, x1)
        shape = (count_j, nk)
        st = Stencil(0, shape)
        even, own_even = st.even, st.even[:nj]
        edge_even = st.even[nj:]
        has_low, has_high = has_neighbours("gy")
        zero = jnp.zeros(shape, jnp.float32)
        for g in (0, pairs + 1):
            for ref in (*d_refs, *x_refs):
                ref[g] = zero

        def edge(at, mask=False):
            hi, lo = y_hi[at], y_lo[at]
            if mask:
                hi, lo = hi * has_high, lo * has_low
            return jnp.concatenate([hi, lo], axis=0)

        def split(q, where):
            e = (2 * q, 2 * q + 1)
            if where == 1:
                mids = [(cls_ref[n - w] + 1).astype(jnp.float32) for n in e]
                bs = [b_ref[n - w] for n in e]
                x = jnp.where(own_even, sample[e[1] - w], sample[e[0] - w])
                g_ref, g_at = g_own, q - h
            else:
                src, g_ref = ((x_lo, g_lo) if where == 0 else (x_hi, g_hi))
                off = 0 if where == 0 else -(w + ni)
                mids = [src[n + off] for n in e]
                bs = [src[2 * w + n + off] for n in e]
                g_at = q + off // 2
                x = src[3 * w + g_at]
            cls = [jnp.concatenate([mids[c], edge(e[c], True)], axis=0) for c in range(2)]
            b = [jnp.concatenate([bs[c], edge(2 * count + e[c])], axis=0) for c in range(2)]
            x1[q + 1] = jnp.concatenate([x, edge(3 * count + q, True)], axis=0)
            seeds = [edge(count + e[c]) for c in range(2)]
            for c in range(2):
                number = jnp.where(even, cls[c], cls[1 - c]).astype(jnp.int32)
                d, m = lookups(number, [d_tab, m_tab])
                d_refs[c][q + 1] = d
                m_ref[c, q] = m
                r_ref[0, c, q] = jnp.where(even, b[c], b[1 - c])
                seed = jnp.where(edge_even, seeds[c], seeds[1 - c]).astype(jnp.int32)
                for t, g in enumerate(raw_noises(seed, 0)):
                    out = n3_ref if t == SWEEPS - 1 else r_ref.at[t + 1]
                    out[c, q] = jnp.concatenate([g_ref[t, c, g_at], g], axis=0)

        loop(0, h, lambda q: split(q, 0))
        loop(h, h + ni // 2, lambda q: split(q, 1))
        loop(h + ni // 2, pairs, lambda q: split(q, 2))

        def prepare(q):
            for c in range(2):
                diagonal, inverse, weights = st.weights(d_refs, m_ref[c, q], c, q)
                m_ref[c, q] = diagonal
                for n in range(6):
                    w_ref[n, c, q] = weights[n]
                root = jnp.where(inverse > 0.0, lax.rsqrt(diagonal), 0.0)
                b = r_ref[0, c, q] * inverse
                noise = n3_ref[c, q] * root
                n3_ref[c, q] = noise
                r3_ref[c, q] = b + noise
                r_ref[0, c, q] = b + r_ref[1, c, q] * root
                r_ref[1, c, q] = b + r_ref[2, c, q] * root

        loop(0, pairs, prepare)

        for half in range(2 * SWEEPS - 2):
            t, c = half // 2, half % 2

            def update(q, t=t, c=c):
                x_refs[c][q + 1] = r_ref[t, c, q] + st.gathered(x_refs, w_ref, c, q)

            loop((half + 1) // 2, pairs - (half + 1) // 2, update)

        def write(q):
            xb_ref[q] = x1[q + h + 1, :nj]

        loop(0, ni // 2, write, 4)
        for q in range(h):
            to_previous[q] = x1[q + h + 1, :nj]
            to_next[q] = x1[ni // 2 + q + 1, :nj]

    state = f32(2, pairs, count_j, nk)
    outs = [f32(6, 2, pairs, count_j, nk), state, state, state]
    outs += [f32(ni // 2, nj, nk), f32(h, nj, nk), f32(h, nj, nk)]
    scratch = [
        pltpu.VMEM((pairs + 2, count_j, nk), jnp.float32),
        pltpu.VMEM((pairs + 2, count_j, nk), jnp.float32),
        pltpu.VMEM((SWEEPS, 2, pairs, count_j, nk), jnp.float32),
        pltpu.VMEM((pairs + 2, count_j, nk), jnp.float32),
        pltpu.VMEM((pairs + 2, count_j, nk), jnp.float32),
    ]
    args = (*tables, class_map, mean_shift, sample_field, noise, *planes, *plane_noise, *rows)
    specs = [SMEM, SMEM] + [VMEM] * (len(args) - 2)
    return call(kernel, "fine_start", outs, args, specs, scratch, START_LIMIT)


def fine_finish(state, black, planes, rows):
    ni, nj, nk = black.shape[0] * 2, black.shape[1], black.shape[2]
    w = FINE_HALO
    h = w // 2
    pairs = (ni + 2 * w) // 2
    count_j = nj + 2 * w
    halo = HALO

    def kernel(w_ref, r3_ref, n3_ref, m_ref, xb_ref, x_lo, x_hi, y_lo, y_hi, *refs):
        fine, rhs, to_next, to_previous = refs[:4]
        x0, x1, res_ref, t_ref, u_ref = refs[4:]
        x_refs = (x0, x1)
        shape = (count_j, nk)
        st = Stencil(0, shape)
        has_low, has_high = has_neighbours("gy")
        zero = jnp.zeros(shape, jnp.float32)
        for g in (0, pairs + 1):
            for ref in x_refs:
                ref[g] = zero

        def join(q, mid):
            x1[q + 1] = jnp.concatenate([mid, y_hi[q] * has_high, y_lo[q] * has_low], axis=0)

        for q in range(h):
            join(q, x_lo[q])
            join(h + ni // 2 + q, x_hi[q])
        loop(0, ni // 2, lambda q: join(h + q, xb_ref[q]), 4)

        for c, (start, stop) in enumerate(((0, pairs - 1), (1, pairs - 1))):

            def update(q, c=c):
                x_refs[c][q + 1] = r3_ref[c, q] + st.gathered(x_refs, w_ref, c, q)

            loop(start, stop, update)

        def residual(q):
            red = r3_ref[0, q] - n3_ref[0, q] + st.gathered(x_refs, w_ref, 0, q) - x0[q + 1]
            res_ref[0, q] = m_ref[0, q] * red
            res_ref[1, q] = -m_ref[1, q] * n3_ref[1, q]

        loop(h - 1, h + ni // 2, residual)

        def write(q):
            both = st.whole(x0[q + h + 1], x1[q + h + 1])
            fine[2 * q] = both[0][:nj]
            fine[2 * q + 1] = both[1][:nj]

        loop(0, ni // 2, write, 4)
        coarse = restricted(st, res_ref, h, ni, nj, t_ref, u_ref, 2)
        rhs[...] = coarse
        to_previous[...] = coarse[:halo]
        to_next[...] = coarse[ni // 2 - halo :]

    outs = [f32(ni, nj, nk), f32(ni // 2, nj // 2, LANES)] + [f32(halo, nj // 2, LANES)] * 2
    scratch = [
        pltpu.VMEM((pairs + 2, count_j, nk), jnp.float32),
        pltpu.VMEM((pairs + 2, count_j, nk), jnp.float32),
        pltpu.VMEM((2, pairs, count_j, nk), jnp.float32),
    ] + restrict_scratch(ni, count_j, nk)
    args = (*state, black, *planes, *rows)
    return call(kernel, "fine_finish", outs, args, None, scratch, FINISH_LIMIT)


def level_sweeps(st, level, pairs, d_refs, m_ref, s_ref, r_ref, w_ref, x_refs, bounds, unroll):
    def prepare(q):
        for c in range(2):
            diagonal, inverse, weights = st.weights(d_refs, m_ref[c, q], c, q)
            m_ref[c, q] = diagonal
            for n in range(6):
                w_ref[n, c, q] = weights[n]
            root = jnp.where(inverse > 0.0, lax.rsqrt(diagonal), 0.0)
            b = r_ref[0, c, q] * inverse
            for t, g in enumerate(raw_noises(s_ref[c, q].astype(jnp.int32), level)):
                noise = g * root
                r_ref[t, c, q] = b + noise
            s_ref[c, q] = noise

    loop(0, pairs, prepare, min(unroll, 2))
    for half in range(2 * SWEEPS):
        t, c = half // 2, half % 2

        def update(q, t=t, c=c, half=half):
            if half == 0:
                x_refs[c][q + 1] = r_ref[t, c, q]
            else:
                x_refs[c][q + 1] = r_ref[t, c, q] + st.gathered(x_refs, w_ref, c, q)

        loop(*bounds(half), update, unroll)


def level_scratch(pairs, rows, lanes):
    guarded = pltpu.VMEM((pairs + 2, rows, lanes), jnp.float32)
    return [
        guarded,
        guarded,
        pltpu.VMEM((2, pairs, rows, lanes), jnp.float32),
        pltpu.VMEM((2, pairs, rows, lanes), jnp.float32),
        pltpu.VMEM((SWEEPS, 2, pairs, rows, lanes), jnp.float32),
        pltpu.VMEM((6, 2, pairs, rows, lanes), jnp.float32),
        guarded,
        guarded,
    ]


def middle_level(level, statics, static_planes, static_rows, rhs, rhs_planes, rhs_rows, tail=None):
    ni, nj, nk = rhs.shape
    w = HALO
    h = w // 2
    count, count_j = ni + 2 * w, nj + 2 * w
    pairs = count // 2
    to_coarsest = level == LEVELS - 2
    plane_base = 0 if level == 1 else 3 * w
    row_base = 0 if level == 1 else 3 * (2 * ni + 2 * w)

    def kernel(*refs):
        refs = list(refs)
        own = refs[:4]
        sx_lo, sx_hi, sy_lo, sy_hi, bx_lo, bx_hi, by_lo, by_hi = refs[4:12]
        at = 12
        if to_coarsest:
            tail_ref, out = refs[12:14]
            at = 14
        else:
            out, to_next, to_previous = refs[12:15]
            at = 15
        d0, d1, m_ref, s_ref, r_ref, w_ref, x0, x1, t_ref, u_ref = refs[at:]
        d_refs, x_refs = (d0, d1), (x0, x1)
        shape = (count_j, nk)
        st = Stencil(level, shape)
        x_has = has_neighbours("gx")
        y_has = has_neighbours("gy")
        zero = jnp.zeros(shape, jnp.float32)
        for g in (0, pairs + 1):
            for ref in (*d_refs, *x_refs):
                ref[g] = zero

        def static_plane(src, a, q, k):
            if level == 1:
                return src[a * w + 2 * q + k]
            return src[plane_base + a * h + q, pl.ds(k * nj, nj)]

        def fields(a, q, k, where):
            e = 2 * q + k
            if where == 1:
                mid = own[a][e - w]
            else:
                p = q if where == 0 else q - h - ni // 2
                if a < 3:
                    mid = static_plane((sx_lo, sx_hi)[where // 2], a, p, k)
                else:
                    mid = (bx_lo, bx_hi)[where // 2][2 * p + k]
                if a == 0:
                    mid = mid * x_has[where // 2]
            if a < 3:
                r = row_base + a * count + e
                hi, lo = sy_hi[r], sy_lo[r]
            else:
                hi, lo = by_hi[e], by_lo[e]
            if a == 0:
                hi, lo = hi * y_has[1], lo * y_has[0]
                if where != 1:
                    hi, lo = hi * x_has[where // 2], lo * x_has[where // 2]
            return jnp.concatenate([mid, hi, lo], axis=0)

        def split(q, where):
            for a in range(4):
                v = st.whole(fields(a, q, 0, where), fields(a, q, 1, where))
                for c in range(2):
                    if a == 0:
                        d_refs[c][q + 1] = v[c]
                    else:
                        (m_ref, s_ref, r_ref.at[0])[a - 1][c, q] = v[c]

        loop(0, h, lambda q: split(q, 0), 4)
        loop(h, h + ni // 2, lambda q: split(q, 1), 4)
        loop(h + ni // 2, pairs, lambda q: split(q, 2), 4)

        def bounds(half):
            return half // 2, (ni + w + 2 * SWEEPS - half) // 2 + 1

        level_sweeps(st, level, pairs, d_refs, m_ref, s_ref, r_ref, w_ref, x_refs, bounds, 4)

        def residual(q):
            red = r_ref[SWEEPS - 1, 0, q] - s_ref[0, q] + st.gathered(x_refs, w_ref, 0, q) - x0[q + 1]
            r_ref[0, 0, q] = m_ref[0, q] * red
            r_ref[0, 1, q] = -m_ref[1, q] * s_ref[1, q]

        loop(h - 1, h + ni // 2, residual, 4)
        coarse = restricted(st, r_ref.at[0], h, ni, nj, t_ref, u_ref, 4)
        if to_coarsest:
            lanes = nk // 4
            coarse = jnp.where(lax.broadcasted_iota(jnp.int32, coarse.shape, 2) < lanes, coarse, 0.0)
            out[...] = tail_ref[...] + pltpu.roll(coarse, 3 * lanes, 2)
        else:
            out[...] = coarse
            to_previous[...] = coarse[:w]
            to_next[...] = coarse[ni // 2 - w :]

    args = [*statics, rhs, *static_planes, *static_rows, *rhs_planes, *rhs_rows]
    if to_coarsest:
        args.append(tail)
        outs = [f32(ni // 2, nj // 2, LANES)]
    else:
        outs = [f32(ni // 2, nj // 2, LANES)] + [f32(w, nj // 2, LANES)] * 2
    scratch = level_scratch(pairs, count_j, nk) + restrict_scratch(ni, count_j, nk)
    return call(kernel, f"level_{level}", outs, args, None, scratch, LEVEL_LIMIT)


def coarsest_level(columns, reach, mi, lanes):
    mj = columns[0].shape[1]
    planes = columns[0].shape[0]
    pairs = planes // 2
    count_j = -(-len(columns) * mj // 8) * 8
    level = LEVELS - 1

    def kernel(*refs):
        blocks = refs[: len(columns)]
        out, d0, d1, m_ref, s_ref, r_ref, w_ref, x0, x1, t_ref = refs[len(columns) :]
        d_refs, x_refs = (d0, d1), (x0, x1)
        shape = (count_j, LANES)
        st = Stencil(level, shape)
        zero = jnp.zeros(shape, jnp.float32)
        for g in (0, pairs + 1):
            for ref in (*d_refs, *x_refs):
                ref[g] = zero
        t_ref[:, pl.ds(count_j - 8, 8), :] = jnp.zeros((planes, 8, LANES), jnp.float32)
        for g, block in enumerate(blocks):
            t_ref[:, pl.ds(g * mj, mj), :] = block[...]
        inside = st.lane < lanes
        first_i = (lax.axis_index("gx") - reach) * mi
        row = lax.broadcasted_iota(jnp.int32, shape, 0)
        j = row + (lax.axis_index("gy") - reach) * mj
        known = (j >= 0) & (j < lax.axis_size("gy") * mj) & (row < len(columns) * mj) & inside
        known = known.astype(jnp.float32)

        def split(q):
            i = first_i + 2 * q
            here = ((i >= 0) & (i < lax.axis_size("gx") * mi)).astype(jnp.float32)
            both = st.whole(t_ref[2 * q], t_ref[2 * q + 1])
            for c in range(2):
                d_refs[c][q + 1] = both[c] * (known * here)
                for a in range(1, 4):
                    v = pltpu.roll(both[c], LANES - a * lanes, 1)
                    (m_ref, s_ref, r_ref.at[0])[a - 1][c, q] = jnp.where(inside, v, 0.0)

        loop(0, pairs, split, pairs)

        def bounds(half):
            more = 2 * SWEEPS - 1 - half
            return (reach * mi - more) // 2, (reach * mi + mi - 1 + more) // 2 + 1

        level_sweeps(st, level, pairs, d_refs, m_ref, s_ref, r_ref, w_ref, x_refs, bounds, pairs)
        for n in range(mi // 2):
            p = reach * mi // 2 + n + 1
            for k, v in enumerate(st.whole(x0[p], x1[p])):
                out[2 * n + k] = v[reach * mj : reach * mj + mj, :lanes]

    scratch = level_scratch(pairs, count_j, LANES)
    scratch += [pltpu.VMEM((planes, count_j, LANES), jnp.float32)]
    outs = [f32(mi, mj, lanes)]
    (out,) = call(kernel, f"level_{level}", outs, columns, None, scratch, LEVEL_LIMIT)
    return out


def both_ways(to_next, to_previous, axis, ring=True):
    size = lax.axis_size(axis)
    up = [(i, (i + 1) % size) for i in range(size if ring else size - 1)]
    down = [(j, i) for i, j in up]
    return lax.ppermute(to_next, axis, up), lax.ppermute(to_previous, axis, down)


def window(block, axis, reach):
    size = lax.axis_size(axis)
    got = {0: block}
    for off in range(-reach, reach + 1):
        if off % size not in got:
            got[off % size] = lax.ppermute(block, axis, [(i, (i - off) % size) for i in range(size)])
    return [got[off % size] for off in range(-reach, reach + 1)]


def per_device(sample_field, mean_shift, class_map, noise_seed, diffusion_table, mass_table):
    tables = (diffusion_table, mass_table)
    nk = class_map.shape[2]
    arrays = (class_map, noise_seed, mean_shift, sample_field)

    planes = both_ways(*pack_planes(*arrays), "gx", False)
    noise = own_noise(noise_seed)
    statics1, statics2, static_next, static_previous, tail = coarse_statics(
        tables, class_map, noise_seed
    )
    planes = lax.optimization_barrier((*planes, noise, static_next))[:2]

    rows = both_ways(*pack_rows_fine(*planes, *arrays), "gy")
    plane_noise = halo_noise(*planes)
    rows = lax.optimization_barrier((*rows, *plane_noise))[:2]

    *state, black, to_next, to_previous = fine_start(
        tables, (class_map, mean_shift, sample_field), noise, planes, plane_noise, rows
    )
    planes = both_ways(to_next, to_previous, "gx", False)
    static_planes = both_ways(static_next, static_previous, "gx")
    rows = both_ways(*pack_rows([(planes[0], black, planes[1])], FINE_HALO, "pack_rows_black"), "gy")
    static_rows = both_ways(*pack_static_rows(static_planes, statics1, statics2), "gy")

    fine, rhs, to_next, to_previous = fine_finish(state, black, planes, rows)
    for level in range(1, LEVELS - 1):
        planes = both_ways(to_next, to_previous, "gx")
        rows = both_ways(*pack_rows([(planes[0], rhs, planes[1])], HALO, f"pack_rows_{level}"), "gy")
        statics = (statics1, statics2)[level - 1]
        last = level == LEVELS - 2
        got = middle_level(
            level, statics, static_planes, static_rows, rhs, planes, rows, tail if last else None
        )
        if not last:
            rhs, to_next, to_previous = got
    (block,) = got
    mi, mj, _ = block.shape
    reach = -(-2 * SWEEPS // min(mi, mj))
    column = jnp.concatenate(window(block, "gx", reach))
    columns = window(column, "gy", reach)
    return fine, coarsest_level(columns, reach, mi, nk >> (LEVELS - 1))


def solution(mesh):
    spec = P("gx", "gy", None)
    return jax.shard_map(
        per_device,
        mesh=mesh,
        in_specs=(spec, spec, spec, spec, P(), P()),
        out_specs=(spec, spec),
        check_vma=False,
    )
```

```python
import functools

import jax
import jax.numpy as jnp
import numpy as np
from jax import lax
from jax.experimental import pallas as pl
from jax.experimental.pallas import tpu as pltpu
from jax.sharding import PartitionSpec as P

SWEEPS = 3
LEVELS = 4
LANES = 128
FINE_HALO = 4
PACK_LIMIT = 58
START_LIMIT = 14
FINISH_LIMIT = 8
LEVEL_LIMIT = 12
UNROLL = 4
HALO = 8
PRIMES = (65521, 65519)
FACTORS = (40503, 30011)
STEPS = (12347, 7919)


def sine_terms(count):
    nodes = 0.25 * np.cos(np.pi * (np.arange(64) + 0.5) / 64)
    design = np.stack([nodes ** (2 * n + 1) for n in range(count)], axis=1)
    fit = np.linalg.lstsq(design, np.sin(2 * np.pi * nodes), rcond=None)[0]
    return [float(c) for c in fit]


SINE = sine_terms(6)


def hash_base(seed, which):
    gap = 65536 - PRIMES[which]
    v = seed * FACTORS[which]
    v = (v >> 16) * gap + (v & 65535)
    v = (v >> 16) * gap + (v & 65535)
    v = jnp.where(v >= PRIMES[which], v - PRIMES[which], v)
    return v.astype(jnp.float32)


def hash_step(base, which, tag):
    prime = float(PRIMES[which])
    h = base + float(((tag + 1) * STEPS[which]) % PRIMES[which])
    return jnp.where(h >= prime, h - prime, h)


def raw_noise(base1, base2, tag):
    h1 = hash_step(base1, 0, tag)
    h2 = hash_step(base2, 1, tag)
    u1 = h1 * (1.0 / PRIMES[0]) + 0.5 / PRIMES[0]
    v = -2.0 * jnp.log(u1)
    radius = v * lax.rsqrt(v)
    z = jnp.abs(h2 - float(PRIMES[1] // 2)) * (1.0 / PRIMES[1]) - 0.25
    zz = z * z
    poly = jnp.full_like(zz, SINE[-1])
    for term in SINE[-2::-1]:
        poly = poly * zz + term
    return radius * (poly * z)


def raw_noises(seed, level):
    base1, base2 = hash_base(seed, 0), hash_base(seed, 1)
    return [raw_noise(base1, base2, level * SWEEPS + t) for t in range(SWEEPS)]


def dot32(a, b):
    return jnp.dot(a, b, preferred_element_type=jnp.float32, precision=lax.Precision.HIGHEST)


def lane_matrix(rows, kind):
    k = lax.broadcasted_iota(jnp.int32, (rows, LANES), 0)
    half = 2 * lax.broadcasted_iota(jnp.int32, (rows, LANES), 1)
    if kind == "pick":
        return (k == half).astype(jnp.float32)
    if kind == "pair":
        return ((k == half) | (k == half + 1)).astype(jnp.float32)
    near = (k == half - 1) | (k == half + 1)
    return jnp.where(k == half, 0.25, jnp.where(near, 0.125, 0.0))


def lookups(numbers, tables):
    results = [jnp.zeros(numbers.shape, jnp.float32) for _ in tables]
    for n in range(tables[0].shape[0]):
        hit = numbers == n + 1
        results = [jnp.where(hit, table[n], result) for table, result in zip(tables, results)]
    return results


def loop(start, stop, body, unroll=1):
    if stop - start <= unroll:
        for q in range(start, stop):
            body(q)
        return

    def step(n, carry):
        for u in range(unroll):
            body(start + n * unroll + u)
        return carry

    whole = (stop - start) // unroll
    lax.fori_loop(0, whole, step, 0)
    for q in range(start + whole * unroll, stop):
        body(q)


def checker(shape):
    return ((lax.broadcasted_iota(jnp.int32, shape, 0) + lax.broadcasted_iota(jnp.int32, shape, 1)) & 1) == 0


def has_neighbours(axis):
    at = lax.axis_index(axis)
    last = lax.axis_size(axis) - 1
    return (at > 0).astype(jnp.float32), (at < last).astype(jnp.float32)


VMEM = pl.BlockSpec(memory_space=pltpu.VMEM)
SMEM = pl.BlockSpec(memory_space=pltpu.SMEM)


def f32(*shape):
    return jax.ShapeDtypeStruct(shape, jnp.float32)


def call(kernel, name, outs, args, specs=None, scratch=(), limit=None):
    return pl.pallas_call(
        kernel,
        out_shape=tuple(outs),
        in_specs=specs or [VMEM] * len(args),
        out_specs=tuple([VMEM] * len(outs)),
        scratch_shapes=list(scratch),
        compiler_params=pltpu.CompilerParams(vmem_limit_bytes=(limit or 4) * 1024 * 1024),
        name=name,
    )(*args)


def pack_planes(class_map, noise_seed, mean_shift, sample_field):
    ni, nj, nk = class_map.shape
    w = FINE_HALO
    arrays = (class_map, noise_seed, mean_shift, sample_field)

    def kernel(*refs):
        sources, outs, (whole_ref, real_ref, sems) = refs[:4], refs[4:6], refs[6:]
        copies = []
        for side, start in enumerate((ni - w, 0)):
            for a, source in enumerate(sources):
                target = (whole_ref, real_ref)[a // 2].at[side, a % 2]
                copy = pltpu.make_async_copy(source.at[pl.ds(start, w)], target, sems.at[side, a])
                copy.start()
                copies.append(copy)
        for copy in copies:
            copy.wait()
        even = checker((nj, nk))
        for side, out in enumerate(outs):
            for e in range(w):
                out[e] = (whole_ref[side, 0, e] + 1).astype(jnp.float32)
                out[w + e] = whole_ref[side, 1, e].astype(jnp.float32)
                out[2 * w + e] = real_ref[side, 0, e]
            for q in range(w // 2):
                out[3 * w + q] = jnp.where(even, real_ref[side, 1, 2 * q + 1], real_ref[side, 1, 2 * q])

    scratch = [
        pltpu.VMEM((2, 2, w, nj, nk), jnp.int32),
        pltpu.VMEM((2, 2, w, nj, nk), jnp.float32),
        pltpu.SemaphoreType.DMA((2, 4)),
    ]
    outs = [f32(3 * w + w // 2, nj, nk)] * 2
    specs = [pl.BlockSpec(memory_space=pltpu.HBM)] * 4
    return call(kernel, "pack_planes", outs, arrays, specs, scratch, PACK_LIMIT)


def pack_rows_fine(from_low, from_high, class_map, noise_seed, mean_shift, sample_field):
    ni, nj, nk = class_map.shape
    w = FINE_HALO
    count = ni + 2 * w
    arrays = (from_low, from_high, class_map, noise_seed, mean_shift, sample_field)

    def kernel(*refs):
        low, high, *own = refs[:6]
        to_next, to_previous = refs[6:]
        even = checker((nj, nk))
        for out, start in ((to_previous, 0), (to_next, nj - w)):
            rows = pl.ds(start, w)
            mask = even[start : start + w]
            for a in range(3):
                for e in range(w):
                    out[a * count + e] = low[a * w + e, rows]
                    out[a * count + ni + w + e] = high[a * w + e, rows]
                for e in range(ni):
                    if a == 0:
                        v = (own[0][e, rows] + 1).astype(jnp.float32)
                    else:
                        v = own[a][e, rows].astype(jnp.float32)
                    out[a * count + w + e] = v
            base = 3 * count
            for q in range(w // 2):
                out[base + q] = low[3 * w + q, rows]
                out[base + (ni + w) // 2 + q] = high[3 * w + q, rows]
            for q in range(ni // 2):
                v = jnp.where(mask, own[3][2 * q + 1, rows], own[3][2 * q, rows])
                out[base + w // 2 + q] = v

    total = 3 * count + count // 2
    return call(kernel, "pack_rows_fine", [f32(total, w, nk)] * 2, arrays)


def pack_rows(triples, w, name):
    parts = [a for triple in triples for a in triple]
    nk = parts[0].shape[2]
    total = sum(p.shape[0] for p in parts)

    def kernel(*refs):
        to_next, to_previous = refs[-2:]
        at = 0
        for n, part in enumerate(parts):
            size, nj, _ = part.shape
            to_previous[pl.ds(at, size)] = refs[n][:, pl.ds(0, w)]
            to_next[pl.ds(at, size)] = refs[n][:, pl.ds(nj - w, w)]
            at += size

    return call(kernel, name, [f32(total, w, nk)] * 2, parts)


def pack_static_rows(static_planes, statics1, statics2):
    w = HALO
    h = w // 2
    sizes = (statics1[0].shape, statics2[0].shape)
    total = 3 * sum(s[0] + 2 * w for s in sizes)

    def kernel(low, high, *refs):
        to_next, to_previous = refs[-2:]
        at = 0
        for level in range(2):
            ni, nj, _ = sizes[level]
            for a in range(3):
                own = refs[3 * level + a]
                for out, start in ((to_previous, 0), (to_next, nj - w)):
                    for src, base in ((low, 0), (high, w + ni)):
                        for e in range(w):
                            if level == 0:
                                v = src[a * w + e, pl.ds(start, w)]
                            else:
                                v = src[3 * w + a * h + e // 2, pl.ds(e % 2 * nj + start, w)]
                            out[at + base + e] = v
                    for e in range(ni):
                        out[at + w + e] = own[e, pl.ds(start, w)]
                at += ni + 2 * w

    args = (*static_planes, *statics1, *statics2)
    return call(kernel, "pack_rows_static", [f32(total, w, LANES)] * 2, args)


def coarse_statics(tables, class_map, noise_seed):
    ni, nj, nk = class_map.shape
    shapes = [(ni >> n, nj >> n, nk >> n) for n in range(LEVELS)]
    w = HALO

    def kernel(d_tab, m_tab, cls_ref, seed_ref, *refs):
        outs, (to_next, to_previous, packed), (t_ref, u_ref) = refs[:6], refs[6:9], refs[9:]
        for level in range(1, LEVELS):
            mi, mj, mk = shapes[level - 1]
            rows = mi // 2 * mj
            width = max(mk, LANES)
            for what in range(3):

                def gather(q):
                    if level == 1:
                        if what < 2:
                            tab = (d_tab, m_tab)[what]
                            (a,) = lookups(cls_ref[2 * q] + 1, [tab])
                            (b,) = lookups(cls_ref[2 * q + 1] + 1, [tab])
                            a = a + b
                        else:
                            a = seed_ref[2 * q].astype(jnp.float32)
                    else:
                        prev = outs[3 * (level - 2) + what]
                        a = prev[2 * q]
                        if what < 2:
                            a = a + prev[2 * q + 1]
                    t_ref[pl.ds(q * mj, mj), :width] = a

                for q in range(mi // 2):
                    gather(q)
                matrix = lane_matrix(width, "pair" if what < 2 else "pick")
                u_ref[pl.ds(0, rows), :] = dot32(t_ref[pl.ds(0, rows), :width], matrix)
                even = u_ref[pl.ds(0, rows // 2, stride=2), :]
                if what < 2:
                    even = 0.125 * (even + u_ref[pl.ds(1, rows // 2, stride=2), :])
                if level < LEVELS - 1:
                    outs[3 * (level - 1) + what][...] = even.reshape(mi // 2, mj // 2, LANES)
                else:
                    lanes = mk // 2
                    if what:
                        even = pltpu.roll(even, what * lanes, 1)
                    total = even if what == 0 else total + even
        packed[...] = total.reshape(shapes[-1][0], shapes[-1][1], LANES)
        mj = shapes[1][1]
        for what in range(3):
            one, two = outs[what], outs[3 + what]
            for e in range(w):
                to_previous[what * w + e] = one[e]
                to_next[what * w + e] = one[shapes[1][0] - w + e]
                n = what * w + e
                at = (3 * w + n // 2, pl.ds(n % 2 * (mj // 2), mj // 2))
                to_previous[at] = two[e]
                to_next[at] = two[shapes[2][0] - w + e]

    outs = []
    for level in range(1, LEVELS - 1):
        outs += [f32(*shapes[level][:2], LANES)] * 3
    outs += [f32(3 * w + 3 * w // 2, shapes[1][1], LANES)] * 2
    outs += [f32(*shapes[-1][:2], LANES)]
    scratch = [
        pltpu.VMEM((ni // 2 * nj, nk), jnp.float32),
        pltpu.VMEM((ni // 2 * nj, LANES), jnp.float32),
    ]
    args = (*tables, class_map, noise_seed)
    got = call(kernel, "coarse_statics", outs, args, [SMEM, SMEM, VMEM, VMEM], scratch)
    return got[:3], got[3:6], got[6], got[7], got[8]


def around(red_black, c, q, even, roll_rows, roll_lanes):
    ref = red_black[1 - c]
    mid, above, below = ref[q + 1], ref[q + 2], ref[q]
    beside = jnp.where(even, below, above) if c == 0 else jnp.where(even, above, below)
    return [
        mid,
        beside,
        pltpu.roll(mid, roll_rows - 1, 0),
        pltpu.roll(mid, 1, 0),
        pltpu.roll(mid, roll_lanes - 1, 1),
        pltpu.roll(mid, 1, 1),
    ]


class Stencil:
    def __init__(self, level, shape):
        self.rows, self.lanes = shape
        self.scale = 0.5 * 0.5**level
        self.lane = lax.broadcasted_iota(jnp.int32, shape, 1)
        self.even = checker(shape)

    def around(self, refs, c, q):
        return around(refs, c, q, self.even, self.rows, self.lanes)

    def weights(self, d_refs, mass, c, q):
        d = d_refs[c][q + 1]
        near = self.around(d_refs, c, q)
        at_end, at_start = self.lane == self.lanes - 1, self.lane == 0
        near[4] = jnp.where(at_end, 0.0, near[4])
        near[5] = jnp.where(at_start, 0.0, near[5])
        total = 6.0 * d
        for v in near:
            total = total + v
        inside = d > 0.0
        diagonal = jnp.where(inside, mass + self.scale * total, 0.0)
        inverse = jnp.where(inside, 1.0 / diagonal, 0.0)
        part = self.scale * inverse
        near[4] = jnp.where(at_end, -d, near[4])
        near[5] = jnp.where(at_start, -d, near[5])
        return diagonal, inverse, [part * (d + v) for v in near]

    def gathered(self, x_refs, w_ref, c, q):
        total = None
        for n, v in enumerate(self.around(x_refs, c, q)):
            term = w_ref[n, c, q] * v
            total = term if total is None else total + term
        return total

    def whole(self, red, black):
        return jnp.where(self.even, red, black), jnp.where(self.even, black, red)


def restricted(st, res_ref, first_pair, ni, nj, t_ref, u_ref, unroll):
    def gather(q):
        p = q + first_pair
        at, after = st.whole(res_ref[0, p], res_ref[1, p])
        _, before = st.whole(res_ref[0, p - 1], res_ref[1, p - 1])
        v = at + 0.5 * (before + after)
        v = v + 0.5 * (pltpu.roll(v, st.rows - 1, 0) + pltpu.roll(v, 1, 0))
        t_ref[pl.ds(pl.multiple_of(q * st.rows, 8), st.rows), :] = v

    loop(0, ni // 2, gather, unroll)
    u_ref[...] = dot32(t_ref[...], lane_matrix(st.lanes, "restrict"))
    size = ni // 2 * st.rows // 2
    coarse = u_ref[pl.ds(0, size, stride=2), :].reshape(ni // 2, st.rows // 2, LANES)
    return coarse[:, : nj // 2, :]


def restrict_scratch(ni, st_rows, nk):
    return [
        pltpu.VMEM((ni // 2 * st_rows, nk), jnp.float32),
        pltpu.VMEM((ni // 2 * st_rows, LANES), jnp.float32),
    ]


def own_noise(noise_seed):
    ni, nj, nk = noise_seed.shape

    def kernel(seed_ref, out):
        even = checker((nj, nk))

        def body(q):
            for c in range(2):
                for at in range(0, nj, 16):
                    rows = pl.ds(at, 16)
                    mask = even[at : at + 16]
                    seeds = (seed_ref[2 * q, rows], seed_ref[2 * q + 1, rows])
                    seed = jnp.where(mask, seeds[c], seeds[1 - c])
                    for t, g in enumerate(raw_noises(seed, 0)):
                        out[t, c, q, rows] = g

        loop(0, ni // 2, body)

    (out,) = call(kernel, "own_noise", [f32(SWEEPS, 2, ni // 2, nj, nk)], (noise_seed,))
    return out


def halo_noise(from_low, from_high):
    w = FINE_HALO
    nj, nk = from_low.shape[1:]

    def kernel(low, high, out_low, out_high):
        even = checker((nj, nk))
        for src, out in ((low, out_low), (high, out_high)):

            def body(q):
                for c in range(2):
                    for at in range(0, nj, 16):
                        rows = pl.ds(at, 16)
                        mask = even[at : at + 16]
                        seeds = (src[w + 2 * q, rows], src[w + 2 * q + 1, rows])
                        seed = jnp.where(mask, seeds[c], seeds[1 - c]).astype(jnp.int32)
                        for t, g in enumerate(raw_noises(seed, 0)):
                            out[t, c, q, rows] = g

            loop(0, w // 2, body)

    return call(kernel, "halo_noise", [f32(SWEEPS, 2, w // 2, nj, nk)] * 2, (from_low, from_high))


def fine_start(tables, own, noise, planes, plane_noise, rows):
    class_map, mean_shift, sample_field = own
    ni, nj, nk = class_map.shape
    w = FINE_HALO
    h = w // 2
    count = ni + 2 * w
    pairs = count // 2
    count_j = nj + 2 * w

    def kernel(d_tab, m_tab, cls_ref, b_ref, sample, g_own, x_lo, x_hi, g_lo, g_hi, y_lo, y_hi, *refs):
        w_ref, r3_ref, n3_ref, m_ref, xb_ref, to_next, to_previous = refs[:7]
        d0, d1, r_ref, x0, x1 = refs[7:]
        d_refs, x_refs = (d0, d1), (x0, x1)
        shape = (count_j, nk)
        st = Stencil(0, shape)
        even, own_even = st.even, st.even[:nj]
        edge_even = st.even[nj:]
        has_low, has_high = has_neighbours("gy")
        zero = jnp.zeros(shape, jnp.float32)
        for g in (0, pairs + 1):
            for ref in (*d_refs, *x_refs):
                ref[g] = zero

        def edge(at, mask=False):
            hi, lo = y_hi[at], y_lo[at]
            if mask:
                hi, lo = hi * has_high, lo * has_low
            return jnp.concatenate([hi, lo], axis=0)

        def split(q, where):
            e = (2 * q, 2 * q + 1)
            if where == 1:
                mids = [(cls_ref[n - w] + 1).astype(jnp.float32) for n in e]
                bs = [b_ref[n - w] for n in e]
                x = jnp.where(own_even, sample[e[1] - w], sample[e[0] - w])
                g_ref, g_at = g_own, q - h
            else:
                src, g_ref = ((x_lo, g_lo) if where == 0 else (x_hi, g_hi))
                off = 0 if where == 0 else -(w + ni)
                mids = [src[n + off] for n in e]
                bs = [src[2 * w + n + off] for n in e]
                g_at = q + off // 2
                x = src[3 * w + g_at]
            cls = [jnp.concatenate([mids[c], edge(e[c], True)], axis=0) for c in range(2)]
            b = [jnp.concatenate([bs[c], edge(2 * count + e[c])], axis=0) for c in range(2)]
            x1[q + 1] = jnp.concatenate([x, edge(3 * count + q, True)], axis=0)
            seeds = [edge(count + e[c]) for c in range(2)]
            for c in range(2):
                number = jnp.where(even, cls[c], cls[1 - c]).astype(jnp.int32)
                d, m = lookups(number, [d_tab, m_tab])
                d_refs[c][q + 1] = d
                m_ref[c, q] = m
                r_ref[0, c, q] = jnp.where(even, b[c], b[1 - c])
                seed = jnp.where(edge_even, seeds[c], seeds[1 - c]).astype(jnp.int32)
                for t, g in enumerate(raw_noises(seed, 0)):
                    out = n3_ref if t == SWEEPS - 1 else r_ref.at[t + 1]
                    out[c, q] = jnp.concatenate([g_ref[t, c, g_at], g], axis=0)

        loop(0, h, lambda q: split(q, 0))
        loop(h, h + ni // 2, lambda q: split(q, 1))
        loop(h + ni // 2, pairs, lambda q: split(q, 2))

        def prepare(q):
            for c in range(2):
                diagonal, inverse, weights = st.weights(d_refs, m_ref[c, q], c, q)
                m_ref[c, q] = diagonal
                for n in range(6):
                    w_ref[n, c, q] = weights[n]
                root = jnp.where(inverse > 0.0, lax.rsqrt(diagonal), 0.0)
                b = r_ref[0, c, q] * inverse
                noise = n3_ref[c, q] * root
                n3_ref[c, q] = noise
                r3_ref[c, q] = b + noise
                r_ref[0, c, q] = b + r_ref[1, c, q] * root
                r_ref[1, c, q] = b + r_ref[2, c, q] * root

        loop(0, pairs, prepare, 2)

        for half in range(2 * SWEEPS - 2):
            t, c = half // 2, half % 2

            def update(q, t=t, c=c):
                x_refs[c][q + 1] = r_ref[t, c, q] + st.gathered(x_refs, w_ref, c, q)

            loop((half + 1) // 2, pairs - (half + 1) // 2, update, UNROLL)

        def write(q):
            xb_ref[q] = x1[q + h + 1, :nj]

        loop(0, ni // 2, write, 4)
        for q in range(h):
            to_previous[q] = x1[q + h + 1, :nj]
            to_next[q] = x1[ni // 2 + q + 1, :nj]

    state = f32(2, pairs, count_j, nk)
    outs = [f32(6, 2, pairs, count_j, nk), state, state, state]
    outs += [f32(ni // 2, nj, nk), f32(h, nj, nk), f32(h, nj, nk)]
    scratch = [
        pltpu.VMEM((pairs + 2, count_j, nk), jnp.float32),
        pltpu.VMEM((pairs + 2, count_j, nk), jnp.float32),
        pltpu.VMEM((SWEEPS, 2, pairs, count_j, nk), jnp.float32),
        pltpu.VMEM((pairs + 2, count_j, nk), jnp.float32),
        pltpu.VMEM((pairs + 2, count_j, nk), jnp.float32),
    ]
    args = (*tables, class_map, mean_shift, sample_field, noise, *planes, *plane_noise, *rows)
    specs = [SMEM, SMEM] + [VMEM] * (len(args) - 2)
    return call(kernel, "fine_start", outs, args, specs, scratch, START_LIMIT)


def fine_finish(state, black, planes, rows):
    ni, nj, nk = black.shape[0] * 2, black.shape[1], black.shape[2]
    w = FINE_HALO
    h = w // 2
    pairs = (ni + 2 * w) // 2
    count_j = nj + 2 * w
    halo = HALO

    def kernel(w_ref, r3_ref, n3_ref, m_ref, xb_ref, x_lo, x_hi, y_lo, y_hi, *refs):
        fine, rhs, to_next, to_previous = refs[:4]
        x0, x1, res_ref, t_ref, u_ref = refs[4:]
        x_refs = (x0, x1)
        shape = (count_j, nk)
        st = Stencil(0, shape)
        has_low, has_high = has_neighbours("gy")
        has_x = has_neighbours("gx")
        zero = jnp.zeros(shape, jnp.float32)
        for g in (0, pairs + 1):
            for ref in x_refs:
                ref[g] = zero

        def join(q, mid, here=1.0):
            hi, lo = y_hi[q] * (has_high * here), y_lo[q] * (has_low * here)
            x1[q + 1] = jnp.concatenate([mid * here, hi, lo], axis=0)

        for q in range(h):
            join(q, x_lo[q], has_x[0])
            join(h + ni // 2 + q, x_hi[q], has_x[1])
        loop(0, ni // 2, lambda q: join(h + q, xb_ref[q]), 4)

        for c, (start, stop) in enumerate(((0, pairs - 1), (1, pairs - 1))):

            def update(q, c=c):
                x_refs[c][q + 1] = r3_ref[c, q] + st.gathered(x_refs, w_ref, c, q)

            loop(start, stop, update, UNROLL)

        def residual(q):
            red = r3_ref[0, q] - n3_ref[0, q] + st.gathered(x_refs, w_ref, 0, q) - x0[q + 1]
            res_ref[0, q] = m_ref[0, q] * red
            res_ref[1, q] = -m_ref[1, q] * n3_ref[1, q]

        loop(h - 1, h + ni // 2, residual, UNROLL)

        def write(q):
            both = st.whole(x0[q + h + 1], x1[q + h + 1])
            fine[2 * q] = both[0][:nj]
            fine[2 * q + 1] = both[1][:nj]

        loop(0, ni // 2, write, 4)
        coarse = restricted(st, res_ref, h, ni, nj, t_ref, u_ref, 2)
        rhs[...] = coarse
        to_previous[...] = coarse[:halo]
        to_next[...] = coarse[ni // 2 - halo :]

    outs = [f32(ni, nj, nk), f32(ni // 2, nj // 2, LANES)] + [f32(halo, nj // 2, LANES)] * 2
    scratch = [
        pltpu.VMEM((pairs + 2, count_j, nk), jnp.float32),
        pltpu.VMEM((pairs + 2, count_j, nk), jnp.float32),
        pltpu.VMEM((2, pairs, count_j, nk), jnp.float32),
    ] + restrict_scratch(ni, count_j, nk)
    args = (*state, black, *planes, *rows)
    return call(kernel, "fine_finish", outs, args, None, scratch, FINISH_LIMIT)


def level_sweeps(st, level, pairs, d_refs, m_ref, s_ref, r_ref, w_ref, x_refs, bounds, unroll):
    def prepare(q):
        for c in range(2):
            diagonal, inverse, weights = st.weights(d_refs, m_ref[c, q], c, q)
            m_ref[c, q] = diagonal
            for n in range(6):
                w_ref[n, c, q] = weights[n]
            root = jnp.where(inverse > 0.0, lax.rsqrt(diagonal), 0.0)
            b = r_ref[0, c, q] * inverse
            for t, g in enumerate(raw_noises(s_ref[c, q].astype(jnp.int32), level)):
                noise = g * root
                r_ref[t, c, q] = b + noise
            s_ref[c, q] = noise

    loop(0, pairs, prepare, min(unroll, 2))
    for half in range(2 * SWEEPS):
        t, c = half // 2, half % 2

        def update(q, t=t, c=c, half=half):
            if half == 0:
                x_refs[c][q + 1] = r_ref[t, c, q]
            else:
                x_refs[c][q + 1] = r_ref[t, c, q] + st.gathered(x_refs, w_ref, c, q)

        loop(*bounds(half), update, unroll)


def level_scratch(pairs, rows, lanes):
    guarded = pltpu.VMEM((pairs + 2, rows, lanes), jnp.float32)
    return [
        guarded,
        guarded,
        pltpu.VMEM((2, pairs, rows, lanes), jnp.float32),
        pltpu.VMEM((2, pairs, rows, lanes), jnp.float32),
        pltpu.VMEM((SWEEPS, 2, pairs, rows, lanes), jnp.float32),
        pltpu.VMEM((6, 2, pairs, rows, lanes), jnp.float32),
        guarded,
        guarded,
    ]


def middle_level(level, statics, static_planes, static_rows, rhs, rhs_planes, rhs_rows, tail=None):
    ni, nj, nk = rhs.shape
    w = HALO
    h = w // 2
    count, count_j = ni + 2 * w, nj + 2 * w
    pairs = count // 2
    to_coarsest = level == LEVELS - 2
    plane_base = 0 if level == 1 else 3 * w
    row_base = 0 if level == 1 else 3 * (2 * ni + 2 * w)

    def kernel(*refs):
        refs = list(refs)
        own = refs[:4]
        sx_lo, sx_hi, sy_lo, sy_hi, bx_lo, bx_hi, by_lo, by_hi = refs[4:12]
        at = 12
        if to_coarsest:
            tail_ref, out = refs[12:14]
            at = 14
        else:
            out, to_next, to_previous = refs[12:15]
            at = 15
        d0, d1, m_ref, s_ref, r_ref, w_ref, x0, x1, t_ref, u_ref = refs[at:]
        d_refs, x_refs = (d0, d1), (x0, x1)
        shape = (count_j, nk)
        st = Stencil(level, shape)
        x_has = has_neighbours("gx")
        y_has = has_neighbours("gy")
        zero = jnp.zeros(shape, jnp.float32)
        for g in (0, pairs + 1):
            for ref in (*d_refs, *x_refs):
                ref[g] = zero

        def static_plane(src, a, q, k):
            if level == 1:
                return src[a * w + 2 * q + k]
            return src[plane_base + a * h + q, pl.ds(k * nj, nj)]

        def fields(a, q, k, where):
            e = 2 * q + k
            if where == 1:
                mid = own[a][e - w]
            else:
                p = q if where == 0 else q - h - ni // 2
                if a < 3:
                    mid = static_plane((sx_lo, sx_hi)[where // 2], a, p, k)
                else:
                    mid = (bx_lo, bx_hi)[where // 2][2 * p + k]
                if a == 0:
                    mid = mid * x_has[where // 2]
            if a < 3:
                r = row_base + a * count + e
                hi, lo = sy_hi[r], sy_lo[r]
            else:
                hi, lo = by_hi[e], by_lo[e]
            if a == 0:
                hi, lo = hi * y_has[1], lo * y_has[0]
                if where != 1:
                    hi, lo = hi * x_has[where // 2], lo * x_has[where // 2]
            return jnp.concatenate([mid, hi, lo], axis=0)

        def split(q, where):
            for a in range(4):
                v = st.whole(fields(a, q, 0, where), fields(a, q, 1, where))
                for c in range(2):
                    if a == 0:
                        d_refs[c][q + 1] = v[c]
                    else:
                        (m_ref, s_ref, r_ref.at[0])[a - 1][c, q] = v[c]

        loop(0, h, lambda q: split(q, 0), 4)
        loop(h, h + ni // 2, lambda q: split(q, 1), 4)
        loop(h + ni // 2, pairs, lambda q: split(q, 2), 4)

        def bounds(half):
            return half // 2, (ni + w + 2 * SWEEPS - half) // 2 + 1

        level_sweeps(st, level, pairs, d_refs, m_ref, s_ref, r_ref, w_ref, x_refs, bounds, 4)

        def residual(q):
            red = r_ref[SWEEPS - 1, 0, q] - s_ref[0, q] + st.gathered(x_refs, w_ref, 0, q) - x0[q + 1]
            r_ref[0, 0, q] = m_ref[0, q] * red
            r_ref[0, 1, q] = -m_ref[1, q] * s_ref[1, q]

        loop(h - 1, h + ni // 2, residual, 4)
        coarse = restricted(st, r_ref.at[0], h, ni, nj, t_ref, u_ref, 4)
        if to_coarsest:
            lanes = nk // 4
            coarse = jnp.where(lax.broadcasted_iota(jnp.int32, coarse.shape, 2) < lanes, coarse, 0.0)
            out[...] = tail_ref[...] + pltpu.roll(coarse, 3 * lanes, 2)
        else:
            out[...] = coarse
            to_previous[...] = coarse[:w]
            to_next[...] = coarse[ni // 2 - w :]

    args = [*statics, rhs, *static_planes, *static_rows, *rhs_planes, *rhs_rows]
    if to_coarsest:
        args.append(tail)
        outs = [f32(ni // 2, nj // 2, LANES)]
    else:
        outs = [f32(ni // 2, nj // 2, LANES)] + [f32(w, nj // 2, LANES)] * 2
    scratch = level_scratch(pairs, count_j, nk) + restrict_scratch(ni, count_j, nk)
    return call(kernel, f"level_{level}", outs, args, None, scratch, LEVEL_LIMIT)


def coarsest_level(columns, reach, mi, lanes):
    mj = columns[0].shape[1]
    planes = columns[0].shape[0]
    pairs = planes // 2
    count_j = -(-len(columns) * mj // 8) * 8
    level = LEVELS - 1

    def kernel(*refs):
        blocks = refs[: len(columns)]
        out, d0, d1, m_ref, s_ref, r_ref, w_ref, x0, x1, t_ref = refs[len(columns) :]
        d_refs, x_refs = (d0, d1), (x0, x1)
        shape = (count_j, LANES)
        st = Stencil(level, shape)
        zero = jnp.zeros(shape, jnp.float32)
        for g in (0, pairs + 1):
            for ref in (*d_refs, *x_refs):
                ref[g] = zero
        t_ref[:, pl.ds(count_j - 8, 8), :] = jnp.zeros((planes, 8, LANES), jnp.float32)
        for g, block in enumerate(blocks):
            t_ref[:, pl.ds(g * mj, mj), :] = block[...]
        inside = st.lane < lanes
        first_i = (lax.axis_index("gx") - reach) * mi
        row = lax.broadcasted_iota(jnp.int32, shape, 0)
        j = row + (lax.axis_index("gy") - reach) * mj
        known = (j >= 0) & (j < lax.axis_size("gy") * mj) & (row < len(columns) * mj) & inside
        known = known.astype(jnp.float32)

        def split(q):
            i = first_i + 2 * q
            here = ((i >= 0) & (i < lax.axis_size("gx") * mi)).astype(jnp.float32)
            both = st.whole(t_ref[2 * q], t_ref[2 * q + 1])
            for c in range(2):
                d_refs[c][q + 1] = both[c] * (known * here)
                for a in range(1, 4):
                    v = pltpu.roll(both[c], LANES - a * lanes, 1)
                    (m_ref, s_ref, r_ref.at[0])[a - 1][c, q] = jnp.where(inside, v, 0.0)

        loop(0, pairs, split, pairs)

        def bounds(half):
            more = 2 * SWEEPS - 1 - half
            return (reach * mi - more) // 2, (reach * mi + mi - 1 + more) // 2 + 1

        level_sweeps(st, level, pairs, d_refs, m_ref, s_ref, r_ref, w_ref, x_refs, bounds, pairs)
        for n in range(mi // 2):
            p = reach * mi // 2 + n + 1
            for k, v in enumerate(st.whole(x0[p], x1[p])):
                out[2 * n + k] = v[reach * mj : reach * mj + mj, :lanes]

    scratch = level_scratch(pairs, count_j, LANES)
    scratch += [pltpu.VMEM((planes, count_j, LANES), jnp.float32)]
    outs = [f32(mi, mj, lanes)]
    (out,) = call(kernel, f"level_{level}", outs, columns, None, scratch, LEVEL_LIMIT)
    return out


def both_ways(to_next, to_previous, axis, ring=True):
    size = lax.axis_size(axis)
    up = [(i, (i + 1) % size) for i in range(size if ring else size - 1)]
    down = [(j, i) for i, j in up]
    return lax.ppermute(to_next, axis, up), lax.ppermute(to_previous, axis, down)


def window(block, axis, reach):
    size = lax.axis_size(axis)
    got = {0: block}
    for off in range(-reach, reach + 1):
        if off % size not in got:
            got[off % size] = lax.ppermute(block, axis, [(i, (i - off) % size) for i in range(size)])
    return [got[off % size] for off in range(-reach, reach + 1)]


def per_device(sample_field, mean_shift, class_map, noise_seed, diffusion_table, mass_table):
    tables = (diffusion_table, mass_table)
    nk = class_map.shape[2]
    arrays = (class_map, noise_seed, mean_shift, sample_field)

    planes = both_ways(*pack_planes(*arrays), "gx", False)
    noise = own_noise(noise_seed)
    statics1, statics2, static_next, static_previous, tail = coarse_statics(
        tables, class_map, noise_seed
    )
    *planes, noise, static_next, static_previous = lax.optimization_barrier(
        (*planes, noise, static_next, static_previous)
    )
    static_planes = both_ways(static_next, static_previous, "gx", False)

    rows = both_ways(*pack_rows_fine(*planes, *arrays), "gy")
    plane_noise = halo_noise(*planes)
    *rows, low_noise, high_noise, static_low, static_high = lax.optimization_barrier(
        (*rows, *plane_noise, *static_planes)
    )
    static_planes = (static_low, static_high)
    static_next, static_previous = pack_static_rows(static_planes, statics1, statics2)
    *rows, static_next, static_previous = lax.optimization_barrier(
        (*rows, static_next, static_previous)
    )
    static_rows = both_ways(static_next, static_previous, "gy")

    *state, black, to_next, to_previous = fine_start(
        tables, (class_map, mean_shift, sample_field), noise, planes, (low_noise, high_noise), rows
    )
    planes = both_ways(to_next, to_previous, "gx")
    rows = both_ways(*pack_rows([(planes[0], black, planes[1])], FINE_HALO, "pack_rows_black"), "gy")

    fine, rhs, to_next, to_previous = fine_finish(state, black, planes, rows)
    for level in range(1, LEVELS - 1):
        planes = both_ways(to_next, to_previous, "gx")
        rows = both_ways(*pack_rows([(planes[0], rhs, planes[1])], HALO, f"pack_rows_{level}"), "gy")
        statics = (statics1, statics2)[level - 1]
        last = level == LEVELS - 2
        got = middle_level(
            level, statics, static_planes, static_rows, rhs, planes, rows, tail if last else None
        )
        if not last:
            rhs, to_next, to_previous = got
    (block,) = got
    mi, mj, _ = block.shape
    reach = -(-2 * SWEEPS // min(mi, mj))
    column = jnp.concatenate(window(block, "gx", reach))
    columns = window(column, "gy", reach)
    return fine, coarsest_level(columns, reach, mi, nk >> (LEVELS - 1))


def solution(mesh):
    spec = P("gx", "gy", None)
    return jax.shard_map(
        per_device,
        mesh=mesh,
        in_specs=(spec, spec, spec, spec, P(), P()),
        out_specs=(spec, spec),
        check_vma=False,
    )
```

```python
import functools

import jax
import jax.numpy as jnp
import numpy as np
from jax import lax
from jax.experimental import pallas as pl
from jax.experimental.pallas import tpu as pltpu
from jax.sharding import PartitionSpec as P

SWEEPS = 3
LEVELS = 4
LANES = 128
FINE_HALO = 4
PACK_LIMIT = 58
START_LIMIT = 14
FINISH_LIMIT = 8
LEVEL_LIMIT = 12
UNROLL = 4
HALO = 8
PRIMES = (65521, 65519)
FACTORS = (40503, 30011)
STEPS = (12347, 7919)


def sine_terms(count):
    nodes = 0.25 * np.cos(np.pi * (np.arange(64) + 0.5) / 64)
    design = np.stack([nodes ** (2 * n + 1) for n in range(count)], axis=1)
    fit = np.linalg.lstsq(design, np.sin(2 * np.pi * nodes), rcond=None)[0]
    return [float(c) for c in fit]


SINE = sine_terms(6)


def hash_base(seed, which):
    gap = 65536 - PRIMES[which]
    v = seed * FACTORS[which]
    v = (v >> 16) * gap + (v & 65535)
    v = (v >> 16) * gap + (v & 65535)
    v = jnp.where(v >= PRIMES[which], v - PRIMES[which], v)
    return v.astype(jnp.float32)


def hash_step(base, which, tag):
    prime = float(PRIMES[which])
    h = base + float(((tag + 1) * STEPS[which]) % PRIMES[which])
    return jnp.where(h >= prime, h - prime, h)


def raw_noise(base1, base2, tag):
    h1 = hash_step(base1, 0, tag)
    h2 = hash_step(base2, 1, tag)
    u1 = h1 * (1.0 / PRIMES[0]) + 0.5 / PRIMES[0]
    v = -2.0 * jnp.log(u1)
    radius = v * lax.rsqrt(v)
    z = jnp.abs(h2 - float(PRIMES[1] // 2)) * (1.0 / PRIMES[1]) - 0.25
    zz = z * z
    poly = jnp.full_like(zz, SINE[-1])
    for term in SINE[-2::-1]:
        poly = poly * zz + term
    return radius * (poly * z)


def raw_noises(seed, level):
    base1, base2 = hash_base(seed, 0), hash_base(seed, 1)
    return [raw_noise(base1, base2, level * SWEEPS + t) for t in range(SWEEPS)]


def dot32(a, b):
    return jnp.dot(a, b, preferred_element_type=jnp.float32, precision=lax.Precision.HIGHEST)


def lane_matrix(rows, kind):
    k = lax.broadcasted_iota(jnp.int32, (rows, LANES), 0)
    half = 2 * lax.broadcasted_iota(jnp.int32, (rows, LANES), 1)
    if kind == "pick":
        return (k == half).astype(jnp.float32)
    if kind == "pair":
        return ((k == half) | (k == half + 1)).astype(jnp.float32)
    near = (k == half - 1) | (k == half + 1)
    return jnp.where(k == half, 0.25, jnp.where(near, 0.125, 0.0))


def lookups(numbers, tables):
    results = [jnp.zeros(numbers.shape, jnp.float32) for _ in tables]
    for n in range(tables[0].shape[0]):
        hit = numbers == n + 1
        results = [jnp.where(hit, table[n], result) for table, result in zip(tables, results)]
    return results


def loop(start, stop, body, unroll=1):
    if stop - start <= unroll:
        for q in range(start, stop):
            body(q)
        return

    def step(n, carry):
        for u in range(unroll):
            body(start + n * unroll + u)
        return carry

    whole = (stop - start) // unroll
    lax.fori_loop(0, whole, step, 0)
    for q in range(start + whole * unroll, stop):
        body(q)


def checker(shape):
    return ((lax.broadcasted_iota(jnp.int32, shape, 0) + lax.broadcasted_iota(jnp.int32, shape, 1)) & 1) == 0


def has_neighbours(axis):
    at = lax.axis_index(axis)
    last = lax.axis_size(axis) - 1
    return (at > 0).astype(jnp.float32), (at < last).astype(jnp.float32)


VMEM = pl.BlockSpec(memory_space=pltpu.VMEM)
SMEM = pl.BlockSpec(memory_space=pltpu.SMEM)


def f32(*shape):
    return jax.ShapeDtypeStruct(shape, jnp.float32)


def call(kernel, name, outs, args, specs=None, scratch=(), limit=None):
    return pl.pallas_call(
        kernel,
        out_shape=tuple(outs),
        in_specs=specs or [VMEM] * len(args),
        out_specs=tuple([VMEM] * len(outs)),
        scratch_shapes=list(scratch),
        compiler_params=pltpu.CompilerParams(vmem_limit_bytes=(limit or 4) * 1024 * 1024),
        name=name,
    )(*args)


def pack_planes(class_map, noise_seed, mean_shift, sample_field):
    ni, nj, nk = class_map.shape
    w = FINE_HALO
    arrays = (class_map, noise_seed, mean_shift, sample_field)

    def kernel(*refs):
        sources, outs, (whole_ref, real_ref, sems) = refs[:4], refs[4:6], refs[6:]
        copies = []
        for side, start in enumerate((ni - w, 0)):
            for a, source in enumerate(sources):
                target = (whole_ref, real_ref)[a // 2].at[side, a % 2]
                copy = pltpu.make_async_copy(source.at[pl.ds(start, w)], target, sems.at[side, a])
                copy.start()
                copies.append(copy)
        for copy in copies:
            copy.wait()
        even = checker((nj, nk))
        for side, out in enumerate(outs):
            for e in range(w):
                out[e] = (whole_ref[side, 0, e] + 1).astype(jnp.float32)
                out[w + e] = whole_ref[side, 1, e].astype(jnp.float32)
                out[2 * w + e] = real_ref[side, 0, e]
            for q in range(w // 2):
                out[3 * w + q] = jnp.where(even, real_ref[side, 1, 2 * q + 1], real_ref[side, 1, 2 * q])

    scratch = [
        pltpu.VMEM((2, 2, w, nj, nk), jnp.int32),
        pltpu.VMEM((2, 2, w, nj, nk), jnp.float32),
        pltpu.SemaphoreType.DMA((2, 4)),
    ]
    outs = [f32(3 * w + w // 2, nj, nk)] * 2
    specs = [pl.BlockSpec(memory_space=pltpu.HBM)] * 4
    return call(kernel, "pack_planes", outs, arrays, specs, scratch, PACK_LIMIT)


def pack_rows_fine(class_map, noise_seed, mean_shift, sample_field):
    ni, nj, nk = class_map.shape
    w = FINE_HALO

    def kernel(*refs):
        own, (to_next, to_previous) = refs[:4], refs[4:]
        even = checker((nj, nk))
        for out, start in ((to_previous, 0), (to_next, nj - w)):
            rows = pl.ds(start, w)
            mask = even[start : start + w]
            for e in range(ni):
                out[e] = (own[0][e, rows] + 1).astype(jnp.float32)
                out[ni + e] = own[1][e, rows].astype(jnp.float32)
                out[2 * ni + e] = own[2][e, rows]
            for q in range(ni // 2):
                out[3 * ni + q] = jnp.where(mask, own[3][2 * q + 1, rows], own[3][2 * q, rows])

    args = (class_map, noise_seed, mean_shift, sample_field)
    return call(kernel, "pack_rows_fine", [f32(3 * ni + ni // 2, w, nk)] * 2, args)


def pack_rows(triples, w, name):
    parts = [a for triple in triples for a in triple]
    nk = parts[0].shape[2]
    total = sum(p.shape[0] for p in parts)

    def kernel(*refs):
        to_next, to_previous = refs[-2:]
        at = 0
        for n, part in enumerate(parts):
            size, nj, _ = part.shape
            to_previous[pl.ds(at, size)] = refs[n][:, pl.ds(0, w)]
            to_next[pl.ds(at, size)] = refs[n][:, pl.ds(nj - w, w)]
            at += size

    return call(kernel, name, [f32(total, w, nk)] * 2, parts)


def pack_static_rows(static_planes, statics1, statics2):
    w = HALO
    h = w // 2
    sizes = (statics1[0].shape, statics2[0].shape)
    total = 3 * sum(s[0] + 2 * w for s in sizes)

    def kernel(low, high, *refs):
        to_next, to_previous = refs[-2:]
        at = 0
        for level in range(2):
            ni, nj, _ = sizes[level]
            for a in range(3):
                own = refs[3 * level + a]
                for out, start in ((to_previous, 0), (to_next, nj - w)):
                    for src, base in ((low, 0), (high, w + ni)):
                        for e in range(w):
                            if level == 0:
                                v = src[a * w + e, pl.ds(start, w)]
                            else:
                                v = src[3 * w + a * h + e // 2, pl.ds(e % 2 * nj + start, w)]
                            out[at + base + e] = v
                    for e in range(ni):
                        out[at + w + e] = own[e, pl.ds(start, w)]
                at += ni + 2 * w

    args = (*static_planes, *statics1, *statics2)
    return call(kernel, "pack_rows_static", [f32(total, w, LANES)] * 2, args)


def coarse_statics(tables, class_map, noise_seed):
    ni, nj, nk = class_map.shape
    shapes = [(ni >> n, nj >> n, nk >> n) for n in range(LEVELS)]
    w = HALO

    def kernel(d_tab, m_tab, cls_ref, seed_ref, *refs):
        outs, (to_next, to_previous, packed), (t_ref, u_ref) = refs[:6], refs[6:9], refs[9:]
        for level in range(1, LEVELS):
            mi, mj, mk = shapes[level - 1]
            rows = mi // 2 * mj
            width = max(mk, LANES)
            for what in range(3):

                def gather(q):
                    if level == 1:
                        if what < 2:
                            tab = (d_tab, m_tab)[what]
                            (a,) = lookups(cls_ref[2 * q] + 1, [tab])
                            (b,) = lookups(cls_ref[2 * q + 1] + 1, [tab])
                            a = a + b
                        else:
                            a = seed_ref[2 * q].astype(jnp.float32)
                    else:
                        prev = outs[3 * (level - 2) + what]
                        a = prev[2 * q]
                        if what < 2:
                            a = a + prev[2 * q + 1]
                    t_ref[pl.ds(q * mj, mj), :width] = a

                for q in range(mi // 2):
                    gather(q)
                matrix = lane_matrix(width, "pair" if what < 2 else "pick")
                u_ref[pl.ds(0, rows), :] = dot32(t_ref[pl.ds(0, rows), :width], matrix)
                even = u_ref[pl.ds(0, rows // 2, stride=2), :]
                if what < 2:
                    even = 0.125 * (even + u_ref[pl.ds(1, rows // 2, stride=2), :])
                if level < LEVELS - 1:
                    outs[3 * (level - 1) + what][...] = even.reshape(mi // 2, mj // 2, LANES)
                else:
                    lanes = mk // 2
                    if what:
                        even = pltpu.roll(even, what * lanes, 1)
                    total = even if what == 0 else total + even
        packed[...] = total.reshape(shapes[-1][0], shapes[-1][1], LANES)
        mj = shapes[1][1]
        for what in range(3):
            one, two = outs[what], outs[3 + what]
            for e in range(w):
                to_previous[what * w + e] = one[e]
                to_next[what * w + e] = one[shapes[1][0] - w + e]
                n = what * w + e
                at = (3 * w + n // 2, pl.ds(n % 2 * (mj // 2), mj // 2))
                to_previous[at] = two[e]
                to_next[at] = two[shapes[2][0] - w + e]

    outs = []
    for level in range(1, LEVELS - 1):
        outs += [f32(*shapes[level][:2], LANES)] * 3
    outs += [f32(3 * w + 3 * w // 2, shapes[1][1], LANES)] * 2
    outs += [f32(*shapes[-1][:2], LANES)]
    scratch = [
        pltpu.VMEM((ni // 2 * nj, nk), jnp.float32),
        pltpu.VMEM((ni // 2 * nj, LANES), jnp.float32),
    ]
    args = (*tables, class_map, noise_seed)
    got = call(kernel, "coarse_statics", outs, args, [SMEM, SMEM, VMEM, VMEM], scratch)
    return got[:3], got[3:6], got[6], got[7], got[8]


def around(red_black, c, q, even, roll_rows, roll_lanes):
    ref = red_black[1 - c]
    mid, above, below = ref[q + 1], ref[q + 2], ref[q]
    beside = jnp.where(even, below, above) if c == 0 else jnp.where(even, above, below)
    return [
        mid,
        beside,
        pltpu.roll(mid, roll_rows - 1, 0),
        pltpu.roll(mid, 1, 0),
        pltpu.roll(mid, roll_lanes - 1, 1),
        pltpu.roll(mid, 1, 1),
    ]


class Stencil:
    def __init__(self, level, shape):
        self.rows, self.lanes = shape
        self.scale = 0.5 * 0.5**level
        self.lane = lax.broadcasted_iota(jnp.int32, shape, 1)
        self.even = checker(shape)

    def around(self, refs, c, q):
        return around(refs, c, q, self.even, self.rows, self.lanes)

    def weights(self, d_refs, mass, c, q):
        d = d_refs[c][q + 1]
        near = self.around(d_refs, c, q)
        at_end, at_start = self.lane == self.lanes - 1, self.lane == 0
        near[4] = jnp.where(at_end, 0.0, near[4])
        near[5] = jnp.where(at_start, 0.0, near[5])
        total = 6.0 * d
        for v in near:
            total = total + v
        inside = d > 0.0
        diagonal = jnp.where(inside, mass + self.scale * total, 0.0)
        inverse = jnp.where(inside, 1.0 / diagonal, 0.0)
        part = self.scale * inverse
        near[4] = jnp.where(at_end, -d, near[4])
        near[5] = jnp.where(at_start, -d, near[5])
        return diagonal, inverse, [part * (d + v) for v in near]

    def gathered(self, x_refs, w_ref, c, q):
        total = None
        for n, v in enumerate(self.around(x_refs, c, q)):
            term = w_ref[n, c, q] * v
            total = term if total is None else total + term
        return total

    def whole(self, red, black):
        return jnp.where(self.even, red, black), jnp.where(self.even, black, red)


def restricted(st, res_ref, first_pair, ni, nj, t_ref, u_ref, unroll):
    def gather(q):
        p = q + first_pair
        at, after = st.whole(res_ref[0, p], res_ref[1, p])
        _, before = st.whole(res_ref[0, p - 1], res_ref[1, p - 1])
        v = at + 0.5 * (before + after)
        v = v + 0.5 * (pltpu.roll(v, st.rows - 1, 0) + pltpu.roll(v, 1, 0))
        t_ref[pl.ds(pl.multiple_of(q * st.rows, 8), st.rows), :] = v

    loop(0, ni // 2, gather, unroll)
    u_ref[...] = dot32(t_ref[...], lane_matrix(st.lanes, "restrict"))
    size = ni // 2 * st.rows // 2
    coarse = u_ref[pl.ds(0, size, stride=2), :].reshape(ni // 2, st.rows // 2, LANES)
    return coarse[:, : nj // 2, :]


def restrict_scratch(ni, st_rows, nk):
    return [
        pltpu.VMEM((ni // 2 * st_rows, nk), jnp.float32),
        pltpu.VMEM((ni // 2 * st_rows, LANES), jnp.float32),
    ]


def own_noise(noise_seed):
    ni, nj, nk = noise_seed.shape

    def kernel(seed_ref, out):
        even = checker((nj, nk))

        def body(q):
            for c in range(2):
                for at in range(0, nj, 16):
                    rows = pl.ds(at, 16)
                    mask = even[at : at + 16]
                    seeds = (seed_ref[2 * q, rows], seed_ref[2 * q + 1, rows])
                    seed = jnp.where(mask, seeds[c], seeds[1 - c])
                    for t, g in enumerate(raw_noises(seed, 0)):
                        out[t, c, q, rows] = g

        loop(0, ni // 2, body)

    (out,) = call(kernel, "own_noise", [f32(SWEEPS, 2, ni // 2, nj, nk)], (noise_seed,))
    return out


def halo_noise(from_low, from_high):
    w = FINE_HALO
    nj, nk = from_low.shape[1:]

    def kernel(low, high, out_low, out_high):
        even = checker((nj, nk))
        for src, out in ((low, out_low), (high, out_high)):

            def body(q):
                for c in range(2):
                    for at in range(0, nj, 16):
                        rows = pl.ds(at, 16)
                        mask = even[at : at + 16]
                        seeds = (src[w + 2 * q, rows], src[w + 2 * q + 1, rows])
                        seed = jnp.where(mask, seeds[c], seeds[1 - c]).astype(jnp.int32)
                        for t, g in enumerate(raw_noises(seed, 0)):
                            out[t, c, q, rows] = g

            loop(0, w // 2, body)

    return call(kernel, "halo_noise", [f32(SWEEPS, 2, w // 2, nj, nk)] * 2, (from_low, from_high))


def fine_start(tables, own, noise, planes, plane_noise, rows, corners):
    class_map, mean_shift, sample_field = own
    ni, nj, nk = class_map.shape
    w = FINE_HALO
    h = w // 2
    count = ni + 2 * w
    pairs = count // 2
    count_j = nj + 2 * w

    def kernel(d_tab, m_tab, cls_ref, b_ref, sample, g_own, x_lo, x_hi, g_lo, g_hi, *refs):
        y_lo, y_hi, c_lo, c_hi = refs[:4]
        refs = refs[4:]
        w_ref, r3_ref, n3_ref, m_ref, xb_ref, to_next, to_previous = refs[:7]
        d0, d1, r_ref, x0, x1 = refs[7:]
        d_refs, x_refs = (d0, d1), (x0, x1)
        shape = (count_j, nk)
        st = Stencil(0, shape)
        even, own_even = st.even, st.even[:nj]
        edge_even = st.even[nj:]
        has_low, has_high = has_neighbours("gy")
        zero = jnp.zeros(shape, jnp.float32)
        for g in (0, pairs + 1):
            for ref in (*d_refs, *x_refs):
                ref[g] = zero

        def edge(a, n, where, mask=False):
            part = 2 if a == 3 else 1
            if where == 1:
                at, refs = a * ni + n - w // part, (y_hi, y_lo)
            elif where == 0:
                at, refs = a * w + n, (c_hi, c_lo)
            else:
                at, refs = 3 * w + h + a * w + n - (w + ni) // part, (c_hi, c_lo)
            hi, lo = refs[0][at], refs[1][at]
            if mask:
                hi, lo = hi * has_high, lo * has_low
            return jnp.concatenate([hi, lo], axis=0)

        def split(q, where):
            e = (2 * q, 2 * q + 1)
            if where == 1:
                mids = [(cls_ref[n - w] + 1).astype(jnp.float32) for n in e]
                bs = [b_ref[n - w] for n in e]
                x = jnp.where(own_even, sample[e[1] - w], sample[e[0] - w])
                g_ref, g_at = g_own, q - h
            else:
                src, g_ref = ((x_lo, g_lo) if where == 0 else (x_hi, g_hi))
                off = 0 if where == 0 else -(w + ni)
                mids = [src[n + off] for n in e]
                bs = [src[2 * w + n + off] for n in e]
                g_at = q + off // 2
                x = src[3 * w + g_at]
            cls = [jnp.concatenate([mids[c], edge(0, e[c], where, True)], axis=0) for c in range(2)]
            b = [jnp.concatenate([bs[c], edge(2, e[c], where)], axis=0) for c in range(2)]
            x1[q + 1] = jnp.concatenate([x, edge(3, q, where, True)], axis=0)
            seeds = [edge(1, e[c], where) for c in range(2)]
            for c in range(2):
                number = jnp.where(even, cls[c], cls[1 - c]).astype(jnp.int32)
                d, m = lookups(number, [d_tab, m_tab])
                d_refs[c][q + 1] = d
                m_ref[c, q] = m
                r_ref[0, c, q] = jnp.where(even, b[c], b[1 - c])
                seed = jnp.where(edge_even, seeds[c], seeds[1 - c]).astype(jnp.int32)
                for t, g in enumerate(raw_noises(seed, 0)):
                    out = n3_ref if t == SWEEPS - 1 else r_ref.at[t + 1]
                    out[c, q] = jnp.concatenate([g_ref[t, c, g_at], g], axis=0)

        loop(0, h, lambda q: split(q, 0))
        loop(h, h + ni // 2, lambda q: split(q, 1))
        loop(h + ni // 2, pairs, lambda q: split(q, 2))

        def prepare(q):
            for c in range(2):
                diagonal, inverse, weights = st.weights(d_refs, m_ref[c, q], c, q)
                m_ref[c, q] = diagonal
                for n in range(6):
                    w_ref[n, c, q] = weights[n]
                root = jnp.where(inverse > 0.0, lax.rsqrt(diagonal), 0.0)
                b = r_ref[0, c, q] * inverse
                noise = n3_ref[c, q] * root
                n3_ref[c, q] = noise
                r3_ref[c, q] = b + noise
                r_ref[0, c, q] = b + r_ref[1, c, q] * root
                r_ref[1, c, q] = b + r_ref[2, c, q] * root

        loop(0, pairs, prepare, 2)

        for half in range(2 * SWEEPS - 2):
            t, c = half // 2, half % 2

            def update(q, t=t, c=c):
                x_refs[c][q + 1] = r_ref[t, c, q] + st.gathered(x_refs, w_ref, c, q)

            loop((half + 1) // 2, pairs - (half + 1) // 2, update, UNROLL)

        def write(q):
            xb_ref[q] = x1[q + h + 1, :nj]

        loop(0, ni // 2, write, 4)
        for q in range(h):
            to_previous[q] = x1[q + h + 1, :nj]
            to_next[q] = x1[ni // 2 + q + 1, :nj]

    state = f32(2, pairs, count_j, nk)
    outs = [f32(6, 2, pairs, count_j, nk), state, state, state]
    outs += [f32(ni // 2, nj, nk), f32(h, nj, nk), f32(h, nj, nk)]
    scratch = [
        pltpu.VMEM((pairs + 2, count_j, nk), jnp.float32),
        pltpu.VMEM((pairs + 2, count_j, nk), jnp.float32),
        pltpu.VMEM((SWEEPS, 2, pairs, count_j, nk), jnp.float32),
        pltpu.VMEM((pairs + 2, count_j, nk), jnp.float32),
        pltpu.VMEM((pairs + 2, count_j, nk), jnp.float32),
    ]
    args = (*tables, class_map, mean_shift, sample_field, noise, *planes, *plane_noise, *rows, *corners)
    specs = [SMEM, SMEM] + [VMEM] * (len(args) - 2)
    return call(kernel, "fine_start", outs, args, specs, scratch, START_LIMIT)


def fine_finish(state, black, planes, rows):
    ni, nj, nk = black.shape[0] * 2, black.shape[1], black.shape[2]
    w = FINE_HALO
    h = w // 2
    pairs = (ni + 2 * w) // 2
    count_j = nj + 2 * w
    halo = HALO

    def kernel(w_ref, r3_ref, n3_ref, m_ref, xb_ref, x_lo, x_hi, y_lo, y_hi, *refs):
        fine, rhs, to_next, to_previous = refs[:4]
        x0, x1, res_ref, t_ref, u_ref = refs[4:]
        x_refs = (x0, x1)
        shape = (count_j, nk)
        st = Stencil(0, shape)
        has_low, has_high = has_neighbours("gy")
        has_x = has_neighbours("gx")
        zero = jnp.zeros(shape, jnp.float32)
        for g in (0, pairs + 1):
            for ref in x_refs:
                ref[g] = zero

        def join(q, mid, here=1.0):
            hi, lo = y_hi[q] * (has_high * here), y_lo[q] * (has_low * here)
            x1[q + 1] = jnp.concatenate([mid * here, hi, lo], axis=0)

        for q in range(h):
            join(q, x_lo[q], has_x[0])
            join(h + ni // 2 + q, x_hi[q], has_x[1])
        loop(0, ni // 2, lambda q: join(h + q, xb_ref[q]), 4)

        for c, (start, stop) in enumerate(((0, pairs - 1), (1, pairs - 1))):

            def update(q, c=c):
                x_refs[c][q + 1] = r3_ref[c, q] + st.gathered(x_refs, w_ref, c, q)

            loop(start, stop, update, UNROLL)

        def residual(q):
            red = r3_ref[0, q] - n3_ref[0, q] + st.gathered(x_refs, w_ref, 0, q) - x0[q + 1]
            res_ref[0, q] = m_ref[0, q] * red
            res_ref[1, q] = -m_ref[1, q] * n3_ref[1, q]

        loop(h - 1, h + ni // 2, residual, UNROLL)

        def write(q):
            both = st.whole(x0[q + h + 1], x1[q + h + 1])
            fine[2 * q] = both[0][:nj]
            fine[2 * q + 1] = both[1][:nj]

        loop(0, ni // 2, write, 4)
        coarse = restricted(st, res_ref, h, ni, nj, t_ref, u_ref, 2)
        rhs[...] = coarse
        to_previous[...] = coarse[:halo]
        to_next[...] = coarse[ni // 2 - halo :]

    outs = [f32(ni, nj, nk), f32(ni // 2, nj // 2, LANES)] + [f32(halo, nj // 2, LANES)] * 2
    scratch = [
        pltpu.VMEM((pairs + 2, count_j, nk), jnp.float32),
        pltpu.VMEM((pairs + 2, count_j, nk), jnp.float32),
        pltpu.VMEM((2, pairs, count_j, nk), jnp.float32),
    ] + restrict_scratch(ni, count_j, nk)
    args = (*state, black, *planes, *rows)
    return call(kernel, "fine_finish", outs, args, None, scratch, FINISH_LIMIT)


def level_sweeps(st, level, pairs, d_refs, m_ref, s_ref, r_ref, w_ref, x_refs, bounds, unroll):
    def prepare(q):
        for c in range(2):
            diagonal, inverse, weights = st.weights(d_refs, m_ref[c, q], c, q)
            m_ref[c, q] = diagonal
            for n in range(6):
                w_ref[n, c, q] = weights[n]
            root = jnp.where(inverse > 0.0, lax.rsqrt(diagonal), 0.0)
            b = r_ref[0, c, q] * inverse
            for t, g in enumerate(raw_noises(s_ref[c, q].astype(jnp.int32), level)):
                noise = g * root
                r_ref[t, c, q] = b + noise
            s_ref[c, q] = noise

    loop(0, pairs, prepare, min(unroll, 2))
    for half in range(2 * SWEEPS):
        t, c = half // 2, half % 2

        def update(q, t=t, c=c, half=half):
            if half == 0:
                x_refs[c][q + 1] = r_ref[t, c, q]
            else:
                x_refs[c][q + 1] = r_ref[t, c, q] + st.gathered(x_refs, w_ref, c, q)

        loop(*bounds(half), update, unroll)


def level_scratch(pairs, rows, lanes):
    guarded = pltpu.VMEM((pairs + 2, rows, lanes), jnp.float32)
    return [
        guarded,
        guarded,
        pltpu.VMEM((2, pairs, rows, lanes), jnp.float32),
        pltpu.VMEM((2, pairs, rows, lanes), jnp.float32),
        pltpu.VMEM((SWEEPS, 2, pairs, rows, lanes), jnp.float32),
        pltpu.VMEM((6, 2, pairs, rows, lanes), jnp.float32),
        guarded,
        guarded,
    ]


def middle_level(level, statics, static_planes, static_rows, rhs, rhs_planes, rhs_rows, tail=None):
    ni, nj, nk = rhs.shape
    w = HALO
    h = w // 2
    count, count_j = ni + 2 * w, nj + 2 * w
    pairs = count // 2
    to_coarsest = level == LEVELS - 2
    plane_base = 0 if level == 1 else 3 * w
    row_base = 0 if level == 1 else 3 * (2 * ni + 2 * w)

    def kernel(*refs):
        refs = list(refs)
        own = refs[:4]
        sx_lo, sx_hi, sy_lo, sy_hi, bx_lo, bx_hi, by_lo, by_hi = refs[4:12]
        at = 12
        if to_coarsest:
            tail_ref, out = refs[12:14]
            at = 14
        else:
            out, to_next, to_previous = refs[12:15]
            at = 15
        d0, d1, m_ref, s_ref, r_ref, w_ref, x0, x1, t_ref, u_ref = refs[at:]
        d_refs, x_refs = (d0, d1), (x0, x1)
        shape = (count_j, nk)
        st = Stencil(level, shape)
        x_has = has_neighbours("gx")
        y_has = has_neighbours("gy")
        zero = jnp.zeros(shape, jnp.float32)
        for g in (0, pairs + 1):
            for ref in (*d_refs, *x_refs):
                ref[g] = zero

        def static_plane(src, a, q, k):
            if level == 1:
                return src[a * w + 2 * q + k]
            return src[plane_base + a * h + q, pl.ds(k * nj, nj)]

        def fields(a, q, k, where):
            e = 2 * q + k
            if where == 1:
                mid = own[a][e - w]
            else:
                p = q if where == 0 else q - h - ni // 2
                if a < 3:
                    mid = static_plane((sx_lo, sx_hi)[where // 2], a, p, k)
                else:
                    mid = (bx_lo, bx_hi)[where // 2][2 * p + k]
                if a == 0:
                    mid = mid * x_has[where // 2]
            if a < 3:
                r = row_base + a * count + e
                hi, lo = sy_hi[r], sy_lo[r]
            else:
                hi, lo = by_hi[e], by_lo[e]
            if a == 0:
                hi, lo = hi * y_has[1], lo * y_has[0]
                if where != 1:
                    hi, lo = hi * x_has[where // 2], lo * x_has[where // 2]
            return jnp.concatenate([mid, hi, lo], axis=0)

        def split(q, where):
            for a in range(4):
                v = st.whole(fields(a, q, 0, where), fields(a, q, 1, where))
                for c in range(2):
                    if a == 0:
                        d_refs[c][q + 1] = v[c]
                    else:
                        (m_ref, s_ref, r_ref.at[0])[a - 1][c, q] = v[c]

        loop(0, h, lambda q: split(q, 0), 4)
        loop(h, h + ni // 2, lambda q: split(q, 1), 4)
        loop(h + ni // 2, pairs, lambda q: split(q, 2), 4)

        def bounds(half):
            return half // 2, (ni + w + 2 * SWEEPS - half) // 2 + 1

        level_sweeps(st, level, pairs, d_refs, m_ref, s_ref, r_ref, w_ref, x_refs, bounds, 4)

        def residual(q):
            red = r_ref[SWEEPS - 1, 0, q] - s_ref[0, q] + st.gathered(x_refs, w_ref, 0, q) - x0[q + 1]
            r_ref[0, 0, q] = m_ref[0, q] * red
            r_ref[0, 1, q] = -m_ref[1, q] * s_ref[1, q]

        loop(h - 1, h + ni // 2, residual, 4)
        coarse = restricted(st, r_ref.at[0], h, ni, nj, t_ref, u_ref, 4)
        if to_coarsest:
            lanes = nk // 4
            coarse = jnp.where(lax.broadcasted_iota(jnp.int32, coarse.shape, 2) < lanes, coarse, 0.0)
            out[...] = tail_ref[...] + pltpu.roll(coarse, 3 * lanes, 2)
        else:
            out[...] = coarse
            to_previous[...] = coarse[:w]
            to_next[...] = coarse[ni // 2 - w :]

    args = [*statics, rhs, *static_planes, *static_rows, *rhs_planes, *rhs_rows]
    if to_coarsest:
        args.append(tail)
        outs = [f32(ni // 2, nj // 2, LANES)]
    else:
        outs = [f32(ni // 2, nj // 2, LANES)] + [f32(w, nj // 2, LANES)] * 2
    scratch = level_scratch(pairs, count_j, nk) + restrict_scratch(ni, count_j, nk)
    return call(kernel, f"level_{level}", outs, args, None, scratch, LEVEL_LIMIT)


def coarsest_level(columns, reach, mi, lanes):
    mj = columns[0].shape[1]
    planes = columns[0].shape[0]
    pairs = planes // 2
    count_j = -(-len(columns) * mj // 8) * 8
    level = LEVELS - 1

    def kernel(*refs):
        blocks = refs[: len(columns)]
        out, d0, d1, m_ref, s_ref, r_ref, w_ref, x0, x1, t_ref = refs[len(columns) :]
        d_refs, x_refs = (d0, d1), (x0, x1)
        shape = (count_j, LANES)
        st = Stencil(level, shape)
        zero = jnp.zeros(shape, jnp.float32)
        for g in (0, pairs + 1):
            for ref in (*d_refs, *x_refs):
                ref[g] = zero
        t_ref[:, pl.ds(count_j - 8, 8), :] = jnp.zeros((planes, 8, LANES), jnp.float32)
        for g, block in enumerate(blocks):
            t_ref[:, pl.ds(g * mj, mj), :] = block[...]
        inside = st.lane < lanes
        first_i = (lax.axis_index("gx") - reach) * mi
        row = lax.broadcasted_iota(jnp.int32, shape, 0)
        j = row + (lax.axis_index("gy") - reach) * mj
        known = (j >= 0) & (j < lax.axis_size("gy") * mj) & (row < len(columns) * mj) & inside
        known = known.astype(jnp.float32)

        def split(q):
            i = first_i + 2 * q
            here = ((i >= 0) & (i < lax.axis_size("gx") * mi)).astype(jnp.float32)
            both = st.whole(t_ref[2 * q], t_ref[2 * q + 1])
            for c in range(2):
                d_refs[c][q + 1] = both[c] * (known * here)
                for a in range(1, 4):
                    v = pltpu.roll(both[c], LANES - a * lanes, 1)
                    (m_ref, s_ref, r_ref.at[0])[a - 1][c, q] = jnp.where(inside, v, 0.0)

        loop(0, pairs, split, pairs)

        def bounds(half):
            more = 2 * SWEEPS - 1 - half
            return (reach * mi - more) // 2, (reach * mi + mi - 1 + more) // 2 + 1

        level_sweeps(st, level, pairs, d_refs, m_ref, s_ref, r_ref, w_ref, x_refs, bounds, pairs)
        for n in range(mi // 2):
            p = reach * mi // 2 + n + 1
            for k, v in enumerate(st.whole(x0[p], x1[p])):
                out[2 * n + k] = v[reach * mj : reach * mj + mj, :lanes]

    scratch = level_scratch(pairs, count_j, LANES)
    scratch += [pltpu.VMEM((planes, count_j, LANES), jnp.float32)]
    outs = [f32(mi, mj, lanes)]
    (out,) = call(kernel, f"level_{level}", outs, columns, None, scratch, LEVEL_LIMIT)
    return out


def both_ways(to_next, to_previous, axis, ring=True):
    size = lax.axis_size(axis)
    up = [(i, (i + 1) % size) for i in range(size if ring else size - 1)]
    down = [(j, i) for i, j in up]
    return lax.ppermute(to_next, axis, up), lax.ppermute(to_previous, axis, down)


def window(block, axis, reach):
    size = lax.axis_size(axis)
    got = {0: block}
    for off in range(-reach, reach + 1):
        if off % size not in got:
            got[off % size] = lax.ppermute(block, axis, [(i, (i - off) % size) for i in range(size)])
    return [got[off % size] for off in range(-reach, reach + 1)]


def per_device(sample_field, mean_shift, class_map, noise_seed, diffusion_table, mass_table):
    tables = (diffusion_table, mass_table)
    nk = class_map.shape[2]
    arrays = (class_map, noise_seed, mean_shift, sample_field)

    planes = both_ways(*pack_planes(*arrays), "gx", False)
    *rows, classes, seed = lax.optimization_barrier(
        (*pack_rows_fine(*arrays), class_map, noise_seed)
    )
    rows = both_ways(*rows, "gy")
    statics1, statics2, static_next, static_previous, tail = coarse_statics(tables, classes, seed)
    seed, static_next, static_previous = lax.optimization_barrier(
        (noise_seed, static_next, static_previous)
    )
    static_planes = both_ways(static_next, static_previous, "gx", False)
    noise = own_noise(seed)
    *planes, noise = lax.optimization_barrier((*planes, noise))

    corners = both_ways(*pack_rows([planes], FINE_HALO, "pack_corners"), "gy")
    plane_noise = halo_noise(*planes)
    *early, low_noise, high_noise, static_low, static_high = lax.optimization_barrier(
        (*rows, *corners, *plane_noise, *static_planes)
    )
    static_planes = (static_low, static_high)
    *early, static_next, static_previous = lax.optimization_barrier(
        (*early, *pack_static_rows(static_planes, statics1, statics2))
    )
    rows, corners = early[:2], early[2:]
    static_rows = both_ways(static_next, static_previous, "gy")

    *state, black, to_next, to_previous = fine_start(
        tables, (class_map, mean_shift, sample_field), noise, planes, (low_noise, high_noise), rows, corners
    )
    planes = both_ways(to_next, to_previous, "gx")
    rows = both_ways(*pack_rows([(planes[0], black, planes[1])], FINE_HALO, "pack_rows_black"), "gy")

    fine, rhs, to_next, to_previous = fine_finish(state, black, planes, rows)
    for level in range(1, LEVELS - 1):
        planes = both_ways(to_next, to_previous, "gx")
        rows = both_ways(*pack_rows([(planes[0], rhs, planes[1])], HALO, f"pack_rows_{level}"), "gy")
        statics = (statics1, statics2)[level - 1]
        last = level == LEVELS - 2
        got = middle_level(
            level, statics, static_planes, static_rows, rhs, planes, rows, tail if last else None
        )
        if not last:
            rhs, to_next, to_previous = got
    (block,) = got
    mi, mj, _ = block.shape
    reach = -(-2 * SWEEPS // min(mi, mj))
    column = jnp.concatenate(window(block, "gx", reach))
    columns = window(column, "gy", reach)
    return fine, coarsest_level(columns, reach, mi, nk >> (LEVELS - 1))


def solution(mesh):
    spec = P("gx", "gy", None)
    return jax.shard_map(
        per_device,
        mesh=mesh,
        in_specs=(spec, spec, spec, spec, P(), P()),
        out_specs=(spec, spec),
        check_vma=False,
    )
```

```python
import functools

import jax
import jax.numpy as jnp
import numpy as np
from jax import lax
from jax.experimental import pallas as pl
from jax.experimental.pallas import tpu as pltpu
from jax.sharding import PartitionSpec as P

SWEEPS = 3
LEVELS = 4
LANES = 128
FINE_HALO = 4
PACK_LIMIT = 58
START_LIMIT = 14
FINISH_LIMIT = 8
LEVEL_LIMIT = 12
UNROLL = 4
HALO = 8
PRIMES = (65521, 65519)
FACTORS = (40503, 30011)
STEPS = (12347, 7919)


def sine_terms(count):
    nodes = 0.25 * np.cos(np.pi * (np.arange(64) + 0.5) / 64)
    design = np.stack([nodes ** (2 * n + 1) for n in range(count)], axis=1)
    fit = np.linalg.lstsq(design, np.sin(2 * np.pi * nodes), rcond=None)[0]
    return [float(c) for c in fit]


SINE = sine_terms(6)


def folded(seed, which):
    gap = 65536 - PRIMES[which]
    v = seed * FACTORS[which]
    v = (v >> 16) * gap + (v & 65535)
    return (v >> 16) * gap + (v & 65535)


def raw_noises(seed, level):
    prime1, prime2 = PRIMES
    base1 = folded(seed, 0)
    base1 = jnp.where(base1 >= prime1, base1 - prime1, base1).astype(jnp.float32)
    base2 = folded(seed, 1).astype(jnp.float32) * (1.0 / prime2) + 0.5 / prime2
    noises = []
    for t in range(SWEEPS):
        tag = level * SWEEPS + t
        h1 = base1 + float(((tag + 1) * STEPS[0]) % prime1 - prime1)
        h1 = jnp.where(h1 < 0.0, h1 + float(prime1), h1)
        u1 = h1 * (1.0 / prime1) + 0.5 / prime1
        v = -2.0 * jnp.log(u1)
        radius = v * lax.rsqrt(v)
        u2 = jnp.abs(base2 + (((tag + 1) * STEPS[1]) % prime2 / prime2 - 1.0))
        z = jnp.abs(u2 - 0.5) - 0.25
        zz = z * z
        poly = jnp.full_like(zz, SINE[-1])
        for term in SINE[-2::-1]:
            poly = poly * zz + term
        noises.append(radius * (poly * z))
    return noises


def dot32(a, b):
    return jnp.dot(a, b, preferred_element_type=jnp.float32, precision=lax.Precision.HIGHEST)


def lane_matrix(rows, kind):
    k = lax.broadcasted_iota(jnp.int32, (rows, LANES), 0)
    half = 2 * lax.broadcasted_iota(jnp.int32, (rows, LANES), 1)
    if kind == "pick":
        return (k == half).astype(jnp.float32)
    if kind == "pair":
        return ((k == half) | (k == half + 1)).astype(jnp.float32)
    near = (k == half - 1) | (k == half + 1)
    return jnp.where(k == half, 0.25, jnp.where(near, 0.125, 0.0))


def lookups(numbers, tables):
    results = [jnp.zeros(numbers.shape, jnp.float32) for _ in tables]
    for n in range(tables[0].shape[0]):
        hit = numbers == n + 1
        results = [jnp.where(hit, table[n], result) for table, result in zip(tables, results)]
    return results


def loop(start, stop, body, unroll=1):
    if stop - start <= unroll:
        for q in range(start, stop):
            body(q)
        return

    def step(n, carry):
        for u in range(unroll):
            body(start + n * unroll + u)
        return carry

    whole = (stop - start) // unroll
    lax.fori_loop(0, whole, step, 0)
    for q in range(start + whole * unroll, stop):
        body(q)


def checker(shape):
    return ((lax.broadcasted_iota(jnp.int32, shape, 0) + lax.broadcasted_iota(jnp.int32, shape, 1)) & 1) == 0


def has_neighbours(axis):
    at = lax.axis_index(axis)
    last = lax.axis_size(axis) - 1
    return (at > 0).astype(jnp.float32), (at < last).astype(jnp.float32)


VMEM = pl.BlockSpec(memory_space=pltpu.VMEM)
SMEM = pl.BlockSpec(memory_space=pltpu.SMEM)


def f32(*shape):
    return jax.ShapeDtypeStruct(shape, jnp.float32)


def call(kernel, name, outs, args, specs=None, scratch=(), limit=None):
    return pl.pallas_call(
        kernel,
        out_shape=tuple(outs),
        in_specs=specs or [VMEM] * len(args),
        out_specs=tuple([VMEM] * len(outs)),
        scratch_shapes=list(scratch),
        compiler_params=pltpu.CompilerParams(vmem_limit_bytes=(limit or 4) * 1024 * 1024),
        name=name,
    )(*args)


def pack_planes(class_map, noise_seed, mean_shift, sample_field):
    ni, nj, nk = class_map.shape
    w = FINE_HALO
    arrays = (class_map, noise_seed, mean_shift, sample_field)

    def kernel(*refs):
        sources, outs, (whole_ref, real_ref, sems) = refs[:4], refs[4:6], refs[6:]
        copies = []
        for side, start in enumerate((ni - w, 0)):
            for a, source in enumerate(sources):
                target = (whole_ref, real_ref)[a // 2].at[side, a % 2]
                copy = pltpu.make_async_copy(source.at[pl.ds(start, w)], target, sems.at[side, a])
                copy.start()
                copies.append(copy)
        for copy in copies:
            copy.wait()
        even = checker((nj, nk))
        for side, out in enumerate(outs):
            for e in range(w):
                out[e] = (whole_ref[side, 0, e] + 1).astype(jnp.float32)
                out[w + e] = whole_ref[side, 1, e].astype(jnp.float32)
                out[2 * w + e] = real_ref[side, 0, e]
            for q in range(w // 2):
                out[3 * w + q] = jnp.where(even, real_ref[side, 1, 2 * q + 1], real_ref[side, 1, 2 * q])

    scratch = [
        pltpu.VMEM((2, 2, w, nj, nk), jnp.int32),
        pltpu.VMEM((2, 2, w, nj, nk), jnp.float32),
        pltpu.SemaphoreType.DMA((2, 4)),
    ]
    outs = [f32(3 * w + w // 2, nj, nk)] * 2
    specs = [pl.BlockSpec(memory_space=pltpu.HBM)] * 4
    return call(kernel, "pack_planes", outs, arrays, specs, scratch, PACK_LIMIT)


def pack_rows_fine(class_map, noise_seed, mean_shift, sample_field):
    ni, nj, nk = class_map.shape
    w = FINE_HALO

    def kernel(*refs):
        own, (to_next, to_previous) = refs[:4], refs[4:]
        even = checker((nj, nk))
        for out, start in ((to_previous, 0), (to_next, nj - w)):
            rows = pl.ds(start, w)
            mask = even[start : start + w]
            for e in range(ni):
                out[e] = (own[0][e, rows] + 1).astype(jnp.float32)
                out[ni + e] = own[1][e, rows].astype(jnp.float32)
                out[2 * ni + e] = own[2][e, rows]
            for q in range(ni // 2):
                out[3 * ni + q] = jnp.where(mask, own[3][2 * q + 1, rows], own[3][2 * q, rows])

    args = (class_map, noise_seed, mean_shift, sample_field)
    return call(kernel, "pack_rows_fine", [f32(3 * ni + ni // 2, w, nk)] * 2, args)


def pack_rows(triples, w, name):
    parts = [a for triple in triples for a in triple]
    nk = parts[0].shape[2]
    total = sum(p.shape[0] for p in parts)

    def kernel(*refs):
        to_next, to_previous = refs[-2:]
        at = 0
        for n, part in enumerate(parts):
            size, nj, _ = part.shape
            to_previous[pl.ds(at, size)] = refs[n][:, pl.ds(0, w)]
            to_next[pl.ds(at, size)] = refs[n][:, pl.ds(nj - w, w)]
            at += size

    return call(kernel, name, [f32(total, w, nk)] * 2, parts)


def pack_static_rows(static_planes, statics1, statics2):
    w = HALO
    h = w // 2
    sizes = (statics1[0].shape, statics2[0].shape)
    total = 3 * sum(s[0] + 2 * w for s in sizes)

    def kernel(low, high, *refs):
        to_next, to_previous = refs[-2:]
        at = 0
        for level in range(2):
            ni, nj, _ = sizes[level]
            for a in range(3):
                own = refs[3 * level + a]
                for out, start in ((to_previous, 0), (to_next, nj - w)):
                    for src, base in ((low, 0), (high, w + ni)):
                        for e in range(w):
                            if level == 0:
                                v = src[a * w + e, pl.ds(start, w)]
                            else:
                                v = src[3 * w + a * h + e // 2, pl.ds(e % 2 * nj + start, w)]
                            out[at + base + e] = v
                    for e in range(ni):
                        out[at + w + e] = own[e, pl.ds(start, w)]
                at += ni + 2 * w

    args = (*static_planes, *statics1, *statics2)
    return call(kernel, "pack_rows_static", [f32(total, w, LANES)] * 2, args)


def coarse_statics(tables, class_map, noise_seed):
    ni, nj, nk = class_map.shape
    shapes = [(ni >> n, nj >> n, nk >> n) for n in range(LEVELS)]
    w = HALO

    def kernel(d_tab, m_tab, cls_ref, seed_ref, *refs):
        outs, (to_next, to_previous, packed), (t_ref, u_ref) = refs[:6], refs[6:9], refs[9:]
        for level in range(1, LEVELS):
            mi, mj, mk = shapes[level - 1]
            rows = mi // 2 * mj
            width = max(mk, LANES)
            for what in range(3):

                def gather(q):
                    if level == 1:
                        if what < 2:
                            tab = (d_tab, m_tab)[what]
                            (a,) = lookups(cls_ref[2 * q] + 1, [tab])
                            (b,) = lookups(cls_ref[2 * q + 1] + 1, [tab])
                            a = a + b
                        else:
                            a = seed_ref[2 * q].astype(jnp.float32)
                    else:
                        prev = outs[3 * (level - 2) + what]
                        a = prev[2 * q]
                        if what < 2:
                            a = a + prev[2 * q + 1]
                    t_ref[pl.ds(q * mj, mj), :width] = a

                for q in range(mi // 2):
                    gather(q)
                matrix = lane_matrix(width, "pair" if what < 2 else "pick")
                u_ref[pl.ds(0, rows), :] = dot32(t_ref[pl.ds(0, rows), :width], matrix)
                even = u_ref[pl.ds(0, rows // 2, stride=2), :]
                if what < 2:
                    even = 0.125 * (even + u_ref[pl.ds(1, rows // 2, stride=2), :])
                if level < LEVELS - 1:
                    outs[3 * (level - 1) + what][...] = even.reshape(mi // 2, mj // 2, LANES)
                else:
                    lanes = mk // 2
                    if what:
                        even = pltpu.roll(even, what * lanes, 1)
                    total = even if what == 0 else total + even
        packed[...] = total.reshape(shapes[-1][0], shapes[-1][1], LANES)
        mj = shapes[1][1]
        for what in range(3):
            one, two = outs[what], outs[3 + what]
            for e in range(w):
                to_previous[what * w + e] = one[e]
                to_next[what * w + e] = one[shapes[1][0] - w + e]
                n = what * w + e
                at = (3 * w + n // 2, pl.ds(n % 2 * (mj // 2), mj // 2))
                to_previous[at] = two[e]
                to_next[at] = two[shapes[2][0] - w + e]

    outs = []
    for level in range(1, LEVELS - 1):
        outs += [f32(*shapes[level][:2], LANES)] * 3
    outs += [f32(3 * w + 3 * w // 2, shapes[1][1], LANES)] * 2
    outs += [f32(*shapes[-1][:2], LANES)]
    scratch = [
        pltpu.VMEM((ni // 2 * nj, nk), jnp.float32),
        pltpu.VMEM((ni // 2 * nj, LANES), jnp.float32),
    ]
    args = (*tables, class_map, noise_seed)
    got = call(kernel, "coarse_statics", outs, args, [SMEM, SMEM, VMEM, VMEM], scratch)
    return got[:3], got[3:6], got[6], got[7], got[8]


def around(red_black, c, q, even, roll_rows, roll_lanes):
    ref = red_black[1 - c]
    mid, above, below = ref[q + 1], ref[q + 2], ref[q]
    beside = jnp.where(even, below, above) if c == 0 else jnp.where(even, above, below)
    return [
        mid,
        beside,
        pltpu.roll(mid, roll_rows - 1, 0),
        pltpu.roll(mid, 1, 0),
        pltpu.roll(mid, roll_lanes - 1, 1),
        pltpu.roll(mid, 1, 1),
    ]


class Stencil:
    def __init__(self, level, shape):
        self.rows, self.lanes = shape
        self.scale = 0.5 * 0.5**level
        self.lane = lax.broadcasted_iota(jnp.int32, shape, 1)
        self.even = checker(shape)

    def around(self, refs, c, q):
        return around(refs, c, q, self.even, self.rows, self.lanes)

    def weights(self, d_refs, mass, c, q):
        d = d_refs[c][q + 1]
        near = self.around(d_refs, c, q)
        at_end, at_start = self.lane == self.lanes - 1, self.lane == 0
        near[4] = jnp.where(at_end, 0.0, near[4])
        near[5] = jnp.where(at_start, 0.0, near[5])
        total = 6.0 * d
        for v in near:
            total = total + v
        inside = d > 0.0
        diagonal = jnp.where(inside, mass + self.scale * total, 0.0)
        inverse = jnp.where(inside, 1.0 / diagonal, 0.0)
        part = self.scale * inverse
        near[4] = jnp.where(at_end, -d, near[4])
        near[5] = jnp.where(at_start, -d, near[5])
        return diagonal, inverse, [part * (d + v) for v in near]

    def gathered(self, x_refs, w_ref, c, q):
        total = None
        for n, v in enumerate(self.around(x_refs, c, q)):
            term = w_ref[n, c, q] * v
            total = term if total is None else total + term
        return total

    def whole(self, red, black):
        return jnp.where(self.even, red, black), jnp.where(self.even, black, red)


def restricted(st, res_ref, first_pair, ni, nj, t_ref, u_ref, unroll):
    def gather(q):
        p = q + first_pair
        at, after = st.whole(res_ref[0, p], res_ref[1, p])
        _, before = st.whole(res_ref[0, p - 1], res_ref[1, p - 1])
        v = at + 0.5 * (before + after)
        v = v + 0.5 * (pltpu.roll(v, st.rows - 1, 0) + pltpu.roll(v, 1, 0))
        t_ref[pl.ds(pl.multiple_of(q * st.rows, 8), st.rows), :] = v

    loop(0, ni // 2, gather, unroll)
    u_ref[...] = dot32(t_ref[...], lane_matrix(st.lanes, "restrict"))
    size = ni // 2 * st.rows // 2
    coarse = u_ref[pl.ds(0, size, stride=2), :].reshape(ni // 2, st.rows // 2, LANES)
    return coarse[:, : nj // 2, :]


def restrict_scratch(ni, st_rows, nk):
    return [
        pltpu.VMEM((ni // 2 * st_rows, nk), jnp.float32),
        pltpu.VMEM((ni // 2 * st_rows, LANES), jnp.float32),
    ]


def own_noise(noise_seed):
    ni, nj, nk = noise_seed.shape

    def kernel(seed_ref, out):
        even = checker((nj, nk))

        def body(q):
            for c in range(2):
                for at in range(0, nj, 16):
                    rows = pl.ds(at, 16)
                    mask = even[at : at + 16]
                    seeds = (seed_ref[2 * q, rows], seed_ref[2 * q + 1, rows])
                    seed = jnp.where(mask, seeds[c], seeds[1 - c])
                    for t, g in enumerate(raw_noises(seed, 0)):
                        out[t, c, q, rows] = g

        loop(0, ni // 2, body)

    (out,) = call(kernel, "own_noise", [f32(SWEEPS, 2, ni // 2, nj, nk)], (noise_seed,))
    return out


def halo_noise(from_low, from_high):
    w = FINE_HALO
    nj, nk = from_low.shape[1:]

    def kernel(low, high, out_low, out_high):
        even = checker((nj, nk))
        for src, out in ((low, out_low), (high, out_high)):

            def body(q):
                for c in range(2):
                    for at in range(0, nj, 16):
                        rows = pl.ds(at, 16)
                        mask = even[at : at + 16]
                        seeds = (src[w + 2 * q, rows], src[w + 2 * q + 1, rows])
                        seed = jnp.where(mask, seeds[c], seeds[1 - c]).astype(jnp.int32)
                        for t, g in enumerate(raw_noises(seed, 0)):
                            out[t, c, q, rows] = g

            loop(0, w // 2, body)

    return call(kernel, "halo_noise", [f32(SWEEPS, 2, w // 2, nj, nk)] * 2, (from_low, from_high))


def fine_start(tables, own, noise, planes, plane_noise, rows, corners):
    class_map, mean_shift, sample_field = own
    ni, nj, nk = class_map.shape
    w = FINE_HALO
    h = w // 2
    count = ni + 2 * w
    pairs = count // 2
    count_j = nj + 2 * w

    def kernel(d_tab, m_tab, cls_ref, b_ref, sample, g_own, x_lo, x_hi, g_lo, g_hi, *refs):
        y_lo, y_hi, c_lo, c_hi = refs[:4]
        refs = refs[4:]
        w_ref, r3_ref, n3_ref, m_ref, xb_ref, to_next, to_previous = refs[:7]
        d0, d1, r_ref, x0, x1 = refs[7:]
        d_refs, x_refs = (d0, d1), (x0, x1)
        shape = (count_j, nk)
        st = Stencil(0, shape)
        even, own_even = st.even, st.even[:nj]
        edge_even = st.even[nj:]
        has_low, has_high = has_neighbours("gy")
        zero = jnp.zeros(shape, jnp.float32)
        for g in (0, pairs + 1):
            for ref in (*d_refs, *x_refs):
                ref[g] = zero

        def edge(a, n, where, mask=False):
            part = 2 if a == 3 else 1
            if where == 1:
                at, refs = a * ni + n - w // part, (y_hi, y_lo)
            elif where == 0:
                at, refs = a * w + n, (c_hi, c_lo)
            else:
                at, refs = 3 * w + h + a * w + n - (w + ni) // part, (c_hi, c_lo)
            hi, lo = refs[0][at], refs[1][at]
            if mask:
                hi, lo = hi * has_high, lo * has_low
            return jnp.concatenate([hi, lo], axis=0)

        def split(q, where):
            e = (2 * q, 2 * q + 1)
            if where == 1:
                mids = [(cls_ref[n - w] + 1).astype(jnp.float32) for n in e]
                bs = [b_ref[n - w] for n in e]
                x = jnp.where(own_even, sample[e[1] - w], sample[e[0] - w])
                g_ref, g_at = g_own, q - h
            else:
                src, g_ref = ((x_lo, g_lo) if where == 0 else (x_hi, g_hi))
                off = 0 if where == 0 else -(w + ni)
                mids = [src[n + off] for n in e]
                bs = [src[2 * w + n + off] for n in e]
                g_at = q + off // 2
                x = src[3 * w + g_at]
            cls = [jnp.concatenate([mids[c], edge(0, e[c], where, True)], axis=0) for c in range(2)]
            b = [jnp.concatenate([bs[c], edge(2, e[c], where)], axis=0) for c in range(2)]
            x1[q + 1] = jnp.concatenate([x, edge(3, q, where, True)], axis=0)
            seeds = [edge(1, e[c], where) for c in range(2)]
            for c in range(2):
                number = jnp.where(even, cls[c], cls[1 - c]).astype(jnp.int32)
                d, m = lookups(number, [d_tab, m_tab])
                d_refs[c][q + 1] = d
                m_ref[c, q] = m
                r_ref[0, c, q] = jnp.where(even, b[c], b[1 - c])
                seed = jnp.where(edge_even, seeds[c], seeds[1 - c]).astype(jnp.int32)
                for t, g in enumerate(raw_noises(seed, 0)):
                    out = n3_ref if t == SWEEPS - 1 else r_ref.at[t + 1]
                    out[c, q] = jnp.concatenate([g_ref[t, c, g_at], g], axis=0)

        loop(0, h, lambda q: split(q, 0))
        loop(h, h + ni // 2, lambda q: split(q, 1))
        loop(h + ni // 2, pairs, lambda q: split(q, 2))

        def prepare(q):
            for c in range(2):
                diagonal, inverse, weights = st.weights(d_refs, m_ref[c, q], c, q)
                m_ref[c, q] = diagonal
                for n in range(6):
                    w_ref[n, c, q] = weights[n]
                root = jnp.where(inverse > 0.0, lax.rsqrt(diagonal), 0.0)
                b = r_ref[0, c, q] * inverse
                noise = n3_ref[c, q] * root
                n3_ref[c, q] = noise
                r3_ref[c, q] = b + noise
                r_ref[0, c, q] = b + r_ref[1, c, q] * root
                r_ref[1, c, q] = b + r_ref[2, c, q] * root

        loop(0, pairs, prepare, 2)

        for half in range(2 * SWEEPS - 2):
            t, c = half // 2, half % 2

            def update(q, t=t, c=c):
                x_refs[c][q + 1] = r_ref[t, c, q] + st.gathered(x_refs, w_ref, c, q)

            loop((half + 1) // 2, pairs - (half + 1) // 2, update, UNROLL)

        def write(q):
            xb_ref[q] = x1[q + h + 1, :nj]

        loop(0, ni // 2, write, 4)
        for q in range(h):
            to_previous[q] = x1[q + h + 1, :nj]
            to_next[q] = x1[ni // 2 + q + 1, :nj]

    state = f32(2, pairs, count_j, nk)
    outs = [f32(6, 2, pairs, count_j, nk), state, state, state]
    outs += [f32(ni // 2, nj, nk), f32(h, nj, nk), f32(h, nj, nk)]
    scratch = [
        pltpu.VMEM((pairs + 2, count_j, nk), jnp.float32),
        pltpu.VMEM((pairs + 2, count_j, nk), jnp.float32),
        pltpu.VMEM((SWEEPS, 2, pairs, count_j, nk), jnp.float32),
        pltpu.VMEM((pairs + 2, count_j, nk), jnp.float32),
        pltpu.VMEM((pairs + 2, count_j, nk), jnp.float32),
    ]
    args = (*tables, class_map, mean_shift, sample_field, noise, *planes, *plane_noise, *rows, *corners)
    specs = [SMEM, SMEM] + [VMEM] * (len(args) - 2)
    return call(kernel, "fine_start", outs, args, specs, scratch, START_LIMIT)


def fine_finish(state, black, planes, rows):
    ni, nj, nk = black.shape[0] * 2, black.shape[1], black.shape[2]
    w = FINE_HALO
    h = w // 2
    pairs = (ni + 2 * w) // 2
    count_j = nj + 2 * w
    halo = HALO

    def kernel(w_ref, r3_ref, n3_ref, m_ref, xb_ref, x_lo, x_hi, y_lo, y_hi, *refs):
        fine, rhs, to_next, to_previous = refs[:4]
        x0, x1, res_ref, t_ref, u_ref = refs[4:]
        x_refs = (x0, x1)
        shape = (count_j, nk)
        st = Stencil(0, shape)
        has_low, has_high = has_neighbours("gy")
        has_x = has_neighbours("gx")
        zero = jnp.zeros(shape, jnp.float32)
        for g in (0, pairs + 1):
            for ref in x_refs:
                ref[g] = zero

        def join(q, mid, here=1.0):
            hi, lo = y_hi[q] * (has_high * here), y_lo[q] * (has_low * here)
            x1[q + 1] = jnp.concatenate([mid * here, hi, lo], axis=0)

        for q in range(h):
            join(q, x_lo[q], has_x[0])
            join(h + ni // 2 + q, x_hi[q], has_x[1])
        loop(0, ni // 2, lambda q: join(h + q, xb_ref[q]), 4)

        for c, (start, stop) in enumerate(((0, pairs - 1), (1, pairs - 1))):

            def update(q, c=c):
                x_refs[c][q + 1] = r3_ref[c, q] + st.gathered(x_refs, w_ref, c, q)

            loop(start, stop, update, UNROLL)

        def residual(q):
            red = r3_ref[0, q] - n3_ref[0, q] + st.gathered(x_refs, w_ref, 0, q) - x0[q + 1]
            res_ref[0, q] = m_ref[0, q] * red
            res_ref[1, q] = -m_ref[1, q] * n3_ref[1, q]

        loop(h - 1, h + ni // 2, residual, UNROLL)

        def write(q):
            both = st.whole(x0[q + h + 1], x1[q + h + 1])
            fine[2 * q] = both[0][:nj]
            fine[2 * q + 1] = both[1][:nj]

        loop(0, ni // 2, write, 4)
        coarse = restricted(st, res_ref, h, ni, nj, t_ref, u_ref, 2)
        rhs[...] = coarse
        to_previous[...] = coarse[:halo]
        to_next[...] = coarse[ni // 2 - halo :]

    outs = [f32(ni, nj, nk), f32(ni // 2, nj // 2, LANES)] + [f32(halo, nj // 2, LANES)] * 2
    scratch = [
        pltpu.VMEM((pairs + 2, count_j, nk), jnp.float32),
        pltpu.VMEM((pairs + 2, count_j, nk), jnp.float32),
        pltpu.VMEM((2, pairs, count_j, nk), jnp.float32),
    ] + restrict_scratch(ni, count_j, nk)
    args = (*state, black, *planes, *rows)
    return call(kernel, "fine_finish", outs, args, None, scratch, FINISH_LIMIT)


def prepared(st, level, pairs, d_refs, m_ref, s_ref, v_ref, n_ref, w_ref, unroll):
    def prepare(q):
        for c in range(2):
            diagonal, inverse, weights = st.weights(d_refs, m_ref[c, q], c, q)
            m_ref[c, q] = diagonal
            v_ref[c, q] = inverse
            for n in range(6):
                w_ref[n, c, q] = weights[n]
            root = jnp.where(inverse > 0.0, lax.rsqrt(diagonal), 0.0)
            for t, g in enumerate(raw_noises(s_ref[c, q].astype(jnp.int32), level)):
                n_ref[t, c, q] = g * root

    loop(0, pairs, prepare, unroll)


def swept(st, pairs, b_ref, v_ref, n_ref, w_ref, x_refs, bounds, unroll):
    def update(q, t, c, half):
        if t == 0:
            b_ref[c, q] = b_ref[c, q] * v_ref[c, q]
        total = b_ref[c, q] + n_ref[t, c, q]
        if half:
            total = total + st.gathered(x_refs, w_ref, c, q)
        x_refs[c][q + 1] = total

    for half in range(2 * SWEEPS):
        t, c = half // 2, half % 2
        loop(*bounds(half), functools.partial(update, t=t, c=c, half=half), unroll)


def middle_static(level, statics, static_planes, static_rows):
    ni, nj, nk = statics[0].shape
    w = HALO
    h = w // 2
    count, count_j = ni + 2 * w, nj + 2 * w
    pairs = count // 2
    plane_base = 0 if level == 1 else 3 * w
    row_base = 0 if level == 1 else 3 * (2 * ni + 2 * w)

    def kernel(*refs):
        own, (x_lo, x_hi, y_lo, y_hi), refs = refs[:3], refs[3:7], refs[7:]
        m_ref, v_ref, n_ref, w_ref, d0, d1, s_ref = refs
        d_refs = (d0, d1)
        shape = (count_j, nk)
        st = Stencil(level, shape)
        x_has, y_has = has_neighbours("gx"), has_neighbours("gy")
        zero = jnp.zeros(shape, jnp.float32)
        for g in (0, pairs + 1):
            for ref in d_refs:
                ref[g] = zero

        def plane(src, a, q, k):
            if level == 1:
                return src[a * w + 2 * q + k]
            return src[plane_base + a * h + q, pl.ds(k * nj, nj)]

        def field(a, q, k, where):
            e = 2 * q + k
            if where == 1:
                mid = own[a][e - w]
            else:
                mid = plane((x_lo, x_hi)[where // 2], a, q if where == 0 else q - h - ni // 2, k)
            r = row_base + a * count + e
            hi, lo = y_hi[r], y_lo[r]
            if a == 0:
                hi, lo = hi * y_has[1], lo * y_has[0]
                if where != 1:
                    mid, hi, lo = [v * x_has[where // 2] for v in (mid, hi, lo)]
            return jnp.concatenate([mid, hi, lo], axis=0)

        def split(q, where):
            for a in range(3):
                v = st.whole(field(a, q, 0, where), field(a, q, 1, where))
                for c in range(2):
                    if a == 0:
                        d_refs[c][q + 1] = v[c]
                    else:
                        (m_ref, s_ref)[a - 1][c, q] = v[c]

        loop(0, h, lambda q: split(q, 0), 4)
        loop(h, h + ni // 2, lambda q: split(q, 1), 4)
        loop(h + ni // 2, pairs, lambda q: split(q, 2), 4)
        prepared(st, level, pairs, d_refs, m_ref, s_ref, v_ref, n_ref, w_ref, 2)

    field_shape = (2, pairs, count_j, nk)
    outs = [f32(*field_shape), f32(*field_shape), f32(SWEEPS, *field_shape), f32(6, *field_shape)]
    scratch = [pltpu.VMEM((pairs + 2, count_j, nk), jnp.float32)] * 2
    scratch += [pltpu.VMEM(field_shape, jnp.float32)]
    args = [*statics, *static_planes, *static_rows]
    return call(kernel, f"static_{level}", outs, args, None, scratch)


def middle_level(level, state, rhs, planes, rows, tail=None):
    ni, nj, nk = rhs.shape
    w = HALO
    h = w // 2
    count_j = nj + 2 * w
    pairs = (ni + 2 * w) // 2
    to_coarsest = level == LEVELS - 2

    def kernel(m_ref, v_ref, n_ref, w_ref, own, x_lo, x_hi, y_lo, y_hi, *refs):
        if to_coarsest:
            tail_ref, out, *refs = refs
        else:
            out, to_next, to_previous, *refs = refs
        b_ref, x0, x1, t_ref, u_ref = refs
        x_refs = (x0, x1)
        shape = (count_j, nk)
        st = Stencil(level, shape)
        zero = jnp.zeros(shape, jnp.float32)
        for g in (0, pairs + 1):
            for ref in x_refs:
                ref[g] = zero

        def split(q, where):
            both = []
            for e in (2 * q, 2 * q + 1):
                mid = own[e - w] if where == 1 else (x_lo[e] if where == 0 else x_hi[e - w - ni])
                both.append(jnp.concatenate([mid, y_hi[e], y_lo[e]], axis=0))
            b_ref[0, q], b_ref[1, q] = st.whole(*both)

        loop(0, h, lambda q: split(q, 0), 4)
        loop(h, h + ni // 2, lambda q: split(q, 1), 4)
        loop(h + ni // 2, pairs, lambda q: split(q, 2), 4)

        def bounds(half):
            return half // 2, (ni + w + 2 * SWEEPS - half) // 2 + 1

        swept(st, pairs, b_ref, v_ref, n_ref, w_ref, x_refs, bounds, 4)
        last = SWEEPS - 1

        def residual(q):
            red = b_ref[0, q] + st.gathered(x_refs, w_ref, 0, q) - x0[q + 1]
            b_ref[0, q] = m_ref[0, q] * red
            b_ref[1, q] = -m_ref[1, q] * n_ref[last, 1, q]

        loop(h - 1, h + ni // 2, residual, 4)
        coarse = restricted(st, b_ref, h, ni, nj, t_ref, u_ref, 4)
        if to_coarsest:
            lanes = nk // 4
            coarse = jnp.where(lax.broadcasted_iota(jnp.int32, coarse.shape, 2) < lanes, coarse, 0.0)
            out[...] = tail_ref[...] + pltpu.roll(coarse, 3 * lanes, 2)
        else:
            out[...] = coarse
            to_previous[...] = coarse[:w]
            to_next[...] = coarse[ni // 2 - w :]

    args = [*state, rhs, *planes, *rows]
    outs = [f32(ni // 2, nj // 2, LANES)]
    if to_coarsest:
        args.append(tail)
    else:
        outs += [f32(w, nj // 2, LANES)] * 2
    guarded = pltpu.VMEM((pairs + 2, count_j, nk), jnp.float32)
    scratch = [pltpu.VMEM((2, pairs, count_j, nk), jnp.float32), guarded, guarded]
    scratch += restrict_scratch(ni, count_j, nk)
    return call(kernel, f"level_{level}", outs, args, None, scratch)


def coarsest_level(columns, reach, mi, lanes):
    mj = columns[0].shape[1]
    planes = columns[0].shape[0]
    pairs = planes // 2
    count_j = -(-len(columns) * mj // 8) * 8
    level = LEVELS - 1

    def kernel(*refs):
        blocks = refs[: len(columns)]
        out, d0, d1, m_ref, s_ref, b_ref, v_ref, n_ref, w_ref, x0, x1, t_ref = refs[len(columns) :]
        d_refs, x_refs = (d0, d1), (x0, x1)
        shape = (count_j, LANES)
        st = Stencil(level, shape)
        zero = jnp.zeros(shape, jnp.float32)
        for g in (0, pairs + 1):
            for ref in (*d_refs, *x_refs):
                ref[g] = zero
        t_ref[:, pl.ds(count_j - 8, 8), :] = jnp.zeros((planes, 8, LANES), jnp.float32)
        for g, block in enumerate(blocks):
            t_ref[:, pl.ds(g * mj, mj), :] = block[...]
        inside = st.lane < lanes
        first_i = (lax.axis_index("gx") - reach) * mi
        row = lax.broadcasted_iota(jnp.int32, shape, 0)
        j = row + (lax.axis_index("gy") - reach) * mj
        known = (j >= 0) & (j < lax.axis_size("gy") * mj) & (row < len(columns) * mj) & inside
        known = known.astype(jnp.float32)

        def split(q):
            i = first_i + 2 * q
            here = ((i >= 0) & (i < lax.axis_size("gx") * mi)).astype(jnp.float32)
            both = st.whole(t_ref[2 * q], t_ref[2 * q + 1])
            for c in range(2):
                d_refs[c][q + 1] = both[c] * (known * here)
                for a in range(1, 4):
                    v = pltpu.roll(both[c], LANES - a * lanes, 1)
                    (m_ref, s_ref, b_ref)[a - 1][c, q] = jnp.where(inside, v, 0.0)

        loop(0, pairs, split, pairs)

        def bounds(half):
            more = 2 * SWEEPS - 1 - half
            return (reach * mi - more) // 2, (reach * mi + mi - 1 + more) // 2 + 1

        prepared(st, level, pairs, d_refs, m_ref, s_ref, v_ref, n_ref, w_ref, 2)
        swept(st, pairs, b_ref, v_ref, n_ref, w_ref, x_refs, bounds, pairs)
        for n in range(mi // 2):
            p = reach * mi // 2 + n + 1
            for k, v in enumerate(st.whole(x0[p], x1[p])):
                out[2 * n + k] = v[reach * mj : reach * mj + mj, :lanes]

    guarded = pltpu.VMEM((pairs + 2, count_j, LANES), jnp.float32)
    fields = [(2,), (2,), (2,), (2,), (SWEEPS, 2), (6, 2)]
    scratch = [guarded, guarded]
    scratch += [pltpu.VMEM((*lead, pairs, count_j, LANES), jnp.float32) for lead in fields]
    scratch += [guarded, guarded, pltpu.VMEM((planes, count_j, LANES), jnp.float32)]
    outs = [f32(mi, mj, lanes)]
    (out,) = call(kernel, f"level_{level}", outs, columns, None, scratch, LEVEL_LIMIT)
    return out


def both_ways(to_next, to_previous, axis, ring=True):
    size = lax.axis_size(axis)
    up = [(i, (i + 1) % size) for i in range(size if ring else size - 1)]
    down = [(j, i) for i, j in up]
    return lax.ppermute(to_next, axis, up), lax.ppermute(to_previous, axis, down)


def window(block, axis, reach):
    size = lax.axis_size(axis)
    got = {0: block}
    for off in range(-reach, reach + 1):
        if off % size not in got:
            got[off % size] = lax.ppermute(block, axis, [(i, (i - off) % size) for i in range(size)])
    return [got[off % size] for off in range(-reach, reach + 1)]


def per_device(sample_field, mean_shift, class_map, noise_seed, diffusion_table, mass_table):
    tables = (diffusion_table, mass_table)
    nk = class_map.shape[2]
    arrays = (class_map, noise_seed, mean_shift, sample_field)

    planes = both_ways(*pack_planes(*arrays), "gx", False)
    *rows, classes, seed = lax.optimization_barrier(
        (*pack_rows_fine(*arrays), class_map, noise_seed)
    )
    rows = both_ways(*rows, "gy")
    statics1, statics2, static_next, static_previous, tail = coarse_statics(tables, classes, seed)
    seed, static_next, static_previous = lax.optimization_barrier(
        (noise_seed, static_next, static_previous)
    )
    static_planes = both_ways(static_next, static_previous, "gx", False)
    noise = own_noise(seed)
    *planes, noise = lax.optimization_barrier((*planes, noise))

    corners = both_ways(*pack_rows([planes], FINE_HALO, "pack_corners"), "gy")
    plane_noise = halo_noise(*planes)
    *early, low_noise, high_noise, static_low, static_high = lax.optimization_barrier(
        (*rows, *corners, *plane_noise, *static_planes)
    )
    static_planes = (static_low, static_high)
    *early, static_next, static_previous = lax.optimization_barrier(
        (*early, *pack_static_rows(static_planes, statics1, statics2))
    )
    rows, corners = early[:2], early[2:]
    static_rows = both_ways(static_next, static_previous, "gy")

    *state, black, to_next, to_previous = fine_start(
        tables, (class_map, mean_shift, sample_field), noise, planes, (low_noise, high_noise), rows, corners
    )
    planes = both_ways(to_next, to_previous, "gx")
    messages = pack_rows([(planes[0], black, planes[1])], FINE_HALO, "pack_rows_black")
    *messages, early, late = lax.optimization_barrier((*messages, *static_rows))
    static_rows = (early, late)
    rows = both_ways(*messages, "gy")
    state1 = middle_static(1, statics1, static_planes, static_rows)
    *rows, s0, s1, s2, s3 = lax.optimization_barrier((*rows, *state1))
    states = [(s0, s1, s2, s3)]

    fine, rhs, to_next, to_previous = fine_finish(state, black, planes, rows)
    to_next, to_previous, early, late = lax.optimization_barrier(
        (to_next, to_previous, *static_rows)
    )
    for level in range(1, LEVELS - 1):
        planes = both_ways(to_next, to_previous, "gx")
        if level == 1:
            state2 = middle_static(2, statics2, static_planes, (early, late))
            *planes, s0, s1, s2, s3 = lax.optimization_barrier((*planes, *state2))
            states.append((s0, s1, s2, s3))
        rows = both_ways(*pack_rows([(planes[0], rhs, planes[1])], HALO, f"pack_rows_{level}"), "gy")
        last = level == LEVELS - 2
        got = middle_level(level, states[level - 1], rhs, planes, rows, tail if last else None)
        if not last:
            rhs, to_next, to_previous = got
    (block,) = got
    mi, mj, _ = block.shape
    reach = -(-2 * SWEEPS // min(mi, mj))
    column = jnp.concatenate(window(block, "gx", reach))
    columns = window(column, "gy", reach)
    return fine, coarsest_level(columns, reach, mi, nk >> (LEVELS - 1))


def solution(mesh):
    spec = P("gx", "gy", None)
    return jax.shard_map(
        per_device,
        mesh=mesh,
        in_specs=(spec, spec, spec, spec, P(), P()),
        out_specs=(spec, spec),
        check_vma=False,
    )
```

```python
import functools

import jax
import jax.numpy as jnp
import numpy as np
from jax import lax
from jax.experimental import pallas as pl
from jax.experimental.pallas import tpu as pltpu
from jax.sharding import PartitionSpec as P

SWEEPS = 3
LEVELS = 4
LANES = 128
FINE_HALO = 4
PACK_LIMIT = 58
START_LIMIT = 14
FINISH_LIMIT = 8
LEVEL_LIMIT = 12
UNROLL = 4
HALO = 8
PRIMES = (65521, 65519)
FACTORS = (40503, 30011)
STEPS = (12347, 7919)


def sine_terms(count):
    nodes = 0.25 * np.cos(np.pi * (np.arange(64) + 0.5) / 64)
    design = np.stack([nodes ** (2 * n + 1) for n in range(count)], axis=1)
    fit = np.linalg.lstsq(design, np.sin(2 * np.pi * nodes), rcond=None)[0]
    return [float(c) for c in fit]


SINE = sine_terms(6)


def folded(seed, which):
    gap = 65536 - PRIMES[which]
    v = seed * FACTORS[which]
    v = (v >> 16) * gap + (v & 65535)
    return (v >> 16) * gap + (v & 65535)


def raw_noises(seed, level):
    prime1, prime2 = PRIMES
    base1 = folded(seed, 0)
    base1 = jnp.where(base1 >= prime1, base1 - prime1, base1).astype(jnp.float32)
    base2 = folded(seed, 1).astype(jnp.float32) * (1.0 / prime2) + 0.5 / prime2
    noises = []
    for t in range(SWEEPS):
        tag = level * SWEEPS + t
        h1 = base1 + float(((tag + 1) * STEPS[0]) % prime1 - prime1)
        h1 = jnp.where(h1 < 0.0, h1 + float(prime1), h1)
        u1 = h1 * (1.0 / prime1) + 0.5 / prime1
        v = -2.0 * jnp.log(u1)
        radius = v * lax.rsqrt(v)
        u2 = jnp.abs(base2 + (((tag + 1) * STEPS[1]) % prime2 / prime2 - 1.0))
        z = jnp.abs(u2 - 0.5) - 0.25
        zz = z * z
        poly = jnp.full_like(zz, SINE[-1])
        for term in SINE[-2::-1]:
            poly = poly * zz + term
        noises.append(radius * (poly * z))
    return noises


def dot32(a, b):
    return jnp.dot(a, b, preferred_element_type=jnp.float32, precision=lax.Precision.HIGHEST)


def lane_matrix(rows, kind):
    k = lax.broadcasted_iota(jnp.int32, (rows, LANES), 0)
    half = 2 * lax.broadcasted_iota(jnp.int32, (rows, LANES), 1)
    if kind == "pick":
        return (k == half).astype(jnp.float32)
    if kind == "pair":
        return ((k == half) | (k == half + 1)).astype(jnp.float32)
    near = (k == half - 1) | (k == half + 1)
    return jnp.where(k == half, 0.25, jnp.where(near, 0.125, 0.0))


def spread_table(table, rows):
    lane = lax.broadcasted_iota(jnp.int32, (rows, LANES), 1)
    result = jnp.zeros((rows, LANES), jnp.float32)
    for n in range(table.shape[0]):
        result = jnp.where(lane == n + 1, table[n], result)
    return result


def lookup(numbers, lanes_table):
    parts = []
    for at in range(0, numbers.shape[1], LANES):
        index = numbers[:, at : at + LANES]
        parts.append(jnp.take_along_axis(lanes_table, index, axis=1, mode="promise_in_bounds"))
    return jnp.concatenate(parts, axis=1)


def selected(numbers, tables):
    results = [jnp.zeros(numbers.shape, jnp.float32) for _ in tables]
    for n in range(tables[0].shape[0]):
        hit = numbers == n + 1
        results = [jnp.where(hit, table[n], result) for table, result in zip(tables, results)]
    return results


def loop(start, stop, body, unroll=1):
    if stop - start <= unroll:
        for q in range(start, stop):
            body(q)
        return

    def step(n, carry):
        for u in range(unroll):
            body(start + n * unroll + u)
        return carry

    whole = (stop - start) // unroll
    lax.fori_loop(0, whole, step, 0)
    for q in range(start + whole * unroll, stop):
        body(q)


def checker(shape):
    return ((lax.broadcasted_iota(jnp.int32, shape, 0) + lax.broadcasted_iota(jnp.int32, shape, 1)) & 1) == 0


def swap_starts(axis, length, w):
    even = lax.axis_index(axis) % 2 == 0
    return jnp.where(even, length - w, 0), jnp.where(even, 0, length - w)


def has_neighbours(axis):
    at = lax.axis_index(axis)
    last = lax.axis_size(axis) - 1
    return (at > 0).astype(jnp.float32), (at < last).astype(jnp.float32)


VMEM = pl.BlockSpec(memory_space=pltpu.VMEM)
SMEM = pl.BlockSpec(memory_space=pltpu.SMEM)


def f32(*shape):
    return jax.ShapeDtypeStruct(shape, jnp.float32)


def call(kernel, name, outs, args, specs=None, scratch=(), limit=None):
    return pl.pallas_call(
        kernel,
        out_shape=tuple(outs),
        in_specs=specs or [VMEM] * len(args),
        out_specs=tuple([VMEM] * len(outs)),
        scratch_shapes=list(scratch),
        compiler_params=pltpu.CompilerParams(vmem_limit_bytes=(limit or 4) * 1024 * 1024),
        name=name,
    )(*args)


def pack_planes(class_map, noise_seed, mean_shift, sample_field):
    ni, nj, nk = class_map.shape
    w = FINE_HALO
    arrays = (class_map, noise_seed, mean_shift, sample_field)

    def kernel(*refs):
        sources, outs, (whole_ref, real_ref, sems) = refs[:4], refs[4:6], refs[6:]
        copies = []
        for side, start in enumerate(swap_starts("gx", ni, w)):
            for a, source in enumerate(sources):
                target = (whole_ref, real_ref)[a // 2].at[side, a % 2]
                copy = pltpu.make_async_copy(source.at[pl.ds(start, w)], target, sems.at[side, a])
                copy.start()
                copies.append(copy)
        for copy in copies:
            copy.wait()
        even = checker((nj, nk))
        for side, out in enumerate(outs):
            for e in range(w):
                out[e] = (whole_ref[side, 0, e] + 1).astype(jnp.float32)
                out[w + e] = whole_ref[side, 1, e].astype(jnp.float32)
                out[2 * w + e] = real_ref[side, 0, e]
            for q in range(w // 2):
                out[3 * w + q] = jnp.where(even, real_ref[side, 1, 2 * q + 1], real_ref[side, 1, 2 * q])

    scratch = [
        pltpu.VMEM((2, 2, w, nj, nk), jnp.int32),
        pltpu.VMEM((2, 2, w, nj, nk), jnp.float32),
        pltpu.SemaphoreType.DMA((2, 4)),
    ]
    outs = [f32(3 * w + w // 2, nj, nk)] * 2
    specs = [pl.BlockSpec(memory_space=pltpu.HBM)] * 4
    return call(kernel, "pack_planes", outs, arrays, specs, scratch, PACK_LIMIT)


def pack_rows_fine(class_map, noise_seed, mean_shift, sample_field):
    ni, nj, nk = class_map.shape
    w = FINE_HALO

    def kernel(*refs):
        own, (to_next, to_previous) = refs[:4], refs[4:]
        even = checker((nj, nk))
        for out, start in ((to_previous, 0), (to_next, nj - w)):
            rows = pl.ds(start, w)
            mask = even[start : start + w]
            for e in range(ni):
                out[e] = (own[0][e, rows] + 1).astype(jnp.float32)
                out[ni + e] = own[1][e, rows].astype(jnp.float32)
                out[2 * ni + e] = own[2][e, rows]
            for q in range(ni // 2):
                out[3 * ni + q] = jnp.where(mask, own[3][2 * q + 1, rows], own[3][2 * q, rows])

    args = (class_map, noise_seed, mean_shift, sample_field)
    return call(kernel, "pack_rows_fine", [f32(3 * ni + ni // 2, w, nk)] * 2, args)


def pack_rows(triples, w, name):
    parts = [a for triple in triples for a in triple]
    nk = parts[0].shape[2]
    total = sum(p.shape[0] for p in parts)

    def kernel(*refs):
        to_next, to_previous = refs[-2:]
        at = 0
        for n, part in enumerate(parts):
            size, nj, _ = part.shape
            to_previous[pl.ds(at, size)] = refs[n][:, pl.ds(0, w)]
            to_next[pl.ds(at, size)] = refs[n][:, pl.ds(nj - w, w)]
            at += size

    return call(kernel, name, [f32(total, w, nk)] * 2, parts)


def pack_static_rows(static_planes, statics1, statics2):
    w = HALO
    h = w // 2
    sizes = (statics1[0].shape, statics2[0].shape)
    total = 3 * sum(s[0] + 2 * w for s in sizes)

    def kernel(low, high, *refs):
        to_next, to_previous = refs[-2:]
        at = 0
        for level in range(2):
            ni, nj, _ = sizes[level]
            for a in range(3):
                own = refs[3 * level + a]
                for out, start in ((to_previous, 0), (to_next, nj - w)):
                    for src, base in ((low, 0), (high, w + ni)):
                        for e in range(w):
                            if level == 0:
                                v = src[a * w + e, pl.ds(start, w)]
                            else:
                                v = src[3 * w + a * h + e // 2, pl.ds(e % 2 * nj + start, w)]
                            out[at + base + e] = v
                    for e in range(ni):
                        out[at + w + e] = own[e, pl.ds(start, w)]
                at += ni + 2 * w

    args = (*static_planes, *statics1, *statics2)
    return call(kernel, "pack_rows_static", [f32(total, w, LANES)] * 2, args)


def coarse_statics(tables, class_map, noise_seed):
    ni, nj, nk = class_map.shape
    shapes = [(ni >> n, nj >> n, nk >> n) for n in range(LEVELS)]
    w = HALO

    def kernel(d_tab, m_tab, cls_ref, seed_ref, *refs):
        outs, (to_even, to_odd, packed), (t_ref, u_ref) = refs[:6], refs[6:9], refs[9:]
        spread = [spread_table(table, nj) for table in (d_tab, m_tab)]
        for level in range(1, LEVELS):
            mi, mj, mk = shapes[level - 1]
            rows = mi // 2 * mj
            width = max(mk, LANES)
            for what in range(3):

                def gather(q):
                    if level == 1:
                        if what < 2:
                            a = lookup(cls_ref[2 * q] + 1, spread[what])
                            a = a + lookup(cls_ref[2 * q + 1] + 1, spread[what])
                        else:
                            a = seed_ref[2 * q].astype(jnp.float32)
                    else:
                        prev = outs[3 * (level - 2) + what]
                        a = prev[2 * q]
                        if what < 2:
                            a = a + prev[2 * q + 1]
                    t_ref[pl.ds(q * mj, mj), :width] = a

                for q in range(mi // 2):
                    gather(q)
                matrix = lane_matrix(width, "pair" if what < 2 else "pick")
                u_ref[pl.ds(0, rows), :] = dot32(t_ref[pl.ds(0, rows), :width], matrix)
                even = u_ref[pl.ds(0, rows // 2, stride=2), :]
                if what < 2:
                    even = 0.125 * (even + u_ref[pl.ds(1, rows // 2, stride=2), :])
                if level < LEVELS - 1:
                    outs[3 * (level - 1) + what][...] = even.reshape(mi // 2, mj // 2, LANES)
                else:
                    lanes = mk // 2
                    if what:
                        even = pltpu.roll(even, what * lanes, 1)
                    total = even if what == 0 else total + even
        packed[...] = total.reshape(shapes[-1][0], shapes[-1][1], LANES)
        mj = shapes[1][1]
        starts1 = swap_starts("gx", shapes[1][0], w)
        starts2 = swap_starts("gx", shapes[2][0], w)
        for what in range(3):
            one, two = outs[what], outs[3 + what]
            for out, start1, start2 in zip((to_even, to_odd), starts1, starts2):
                for e in range(w):
                    out[what * w + e] = one[start1 + e]
                    n = what * w + e
                    at = (3 * w + n // 2, pl.ds(n % 2 * (mj // 2), mj // 2))
                    out[at] = two[start2 + e]

    outs = []
    for level in range(1, LEVELS - 1):
        outs += [f32(*shapes[level][:2], LANES)] * 3
    outs += [f32(3 * w + 3 * w // 2, shapes[1][1], LANES)] * 2
    outs += [f32(*shapes[-1][:2], LANES)]
    scratch = [
        pltpu.VMEM((ni // 2 * nj, nk), jnp.float32),
        pltpu.VMEM((ni // 2 * nj, LANES), jnp.float32),
    ]
    args = (*tables, class_map, noise_seed)
    got = call(kernel, "coarse_statics", outs, args, [SMEM, SMEM, VMEM, VMEM], scratch)
    return got[:3], got[3:6], got[6], got[7], got[8]


def around(red_black, c, q, even, roll_rows, roll_lanes):
    ref = red_black[1 - c]
    mid, above, below = ref[q + 1], ref[q + 2], ref[q]
    beside = jnp.where(even, below, above) if c == 0 else jnp.where(even, above, below)
    return [
        mid,
        beside,
        pltpu.roll(mid, roll_rows - 1, 0),
        pltpu.roll(mid, 1, 0),
        pltpu.roll(mid, roll_lanes - 1, 1),
        pltpu.roll(mid, 1, 1),
    ]


class Stencil:
    def __init__(self, level, shape):
        self.rows, self.lanes = shape
        self.scale = 0.5 * 0.5**level
        self.lane = lax.broadcasted_iota(jnp.int32, shape, 1)
        self.even = checker(shape)

    def around(self, refs, c, q):
        return around(refs, c, q, self.even, self.rows, self.lanes)

    def weights(self, d_refs, mass, c, q):
        d = d_refs[c][q + 1]
        near = self.around(d_refs, c, q)
        at_end, at_start = self.lane == self.lanes - 1, self.lane == 0
        near[4] = jnp.where(at_end, 0.0, near[4])
        near[5] = jnp.where(at_start, 0.0, near[5])
        total = 6.0 * d
        for v in near:
            total = total + v
        inside = d > 0.0
        diagonal = jnp.where(inside, mass + self.scale * total, 0.0)
        inverse = jnp.where(inside, 1.0 / diagonal, 0.0)
        part = self.scale * inverse
        near[4] = jnp.where(at_end, -d, near[4])
        near[5] = jnp.where(at_start, -d, near[5])
        return diagonal, inverse, [part * (d + v) for v in near]

    def gathered(self, x_refs, w_ref, c, q):
        total = None
        for n, v in enumerate(self.around(x_refs, c, q)):
            term = w_ref[n, c, q] * v
            total = term if total is None else total + term
        return total

    def whole(self, red, black):
        return jnp.where(self.even, red, black), jnp.where(self.even, black, red)


def restricted(st, res_ref, first_pair, ni, nj, t_ref, u_ref, unroll):
    def gather(q):
        p = q + first_pair
        at, after = st.whole(res_ref[0, p], res_ref[1, p])
        _, before = st.whole(res_ref[0, p - 1], res_ref[1, p - 1])
        v = at + 0.5 * (before + after)
        v = v + 0.5 * (pltpu.roll(v, st.rows - 1, 0) + pltpu.roll(v, 1, 0))
        t_ref[pl.ds(pl.multiple_of(q * st.rows, 8), st.rows), :] = v

    loop(0, ni // 2, gather, unroll)
    u_ref[...] = dot32(t_ref[...], lane_matrix(st.lanes, "restrict"))
    size = ni // 2 * st.rows // 2
    coarse = u_ref[pl.ds(0, size, stride=2), :].reshape(ni // 2, st.rows // 2, LANES)
    return coarse[:, : nj // 2, :]


def restrict_scratch(ni, st_rows, nk):
    return [
        pltpu.VMEM((ni // 2 * st_rows, nk), jnp.float32),
        pltpu.VMEM((ni // 2 * st_rows, LANES), jnp.float32),
    ]


def own_noise(noise_seed):
    ni, nj, nk = noise_seed.shape

    def kernel(seed_ref, out):
        even = checker((nj, nk))

        def body(q):
            for c in range(2):
                for at in range(0, nj, 16):
                    rows = pl.ds(at, 16)
                    mask = even[at : at + 16]
                    seeds = (seed_ref[2 * q, rows], seed_ref[2 * q + 1, rows])
                    seed = jnp.where(mask, seeds[c], seeds[1 - c])
                    for t, g in enumerate(raw_noises(seed, 0)):
                        out[t, c, q, rows] = g

        loop(0, ni // 2, body)

    (out,) = call(kernel, "own_noise", [f32(SWEEPS, 2, ni // 2, nj, nk)], (noise_seed,))
    return out


def halo_noise(from_low, from_high):
    w = FINE_HALO
    nj, nk = from_low.shape[1:]

    def kernel(low, high, out_low, out_high):
        even = checker((nj, nk))
        for src, out in ((low, out_low), (high, out_high)):

            def body(q):
                for c in range(2):
                    for at in range(0, nj, 16):
                        rows = pl.ds(at, 16)
                        mask = even[at : at + 16]
                        seeds = (src[w + 2 * q, rows], src[w + 2 * q + 1, rows])
                        seed = jnp.where(mask, seeds[c], seeds[1 - c]).astype(jnp.int32)
                        for t, g in enumerate(raw_noises(seed, 0)):
                            out[t, c, q, rows] = g

            loop(0, w // 2, body)

    return call(kernel, "halo_noise", [f32(SWEEPS, 2, w // 2, nj, nk)] * 2, (from_low, from_high))


def fine_start(tables, own, noise, planes, plane_noise, rows, corners):
    class_map, mean_shift, sample_field = own
    ni, nj, nk = class_map.shape
    w = FINE_HALO
    h = w // 2
    count = ni + 2 * w
    pairs = count // 2
    count_j = nj + 2 * w

    def kernel(d_tab, m_tab, cls_ref, b_ref, sample, g_own, x_lo, x_hi, g_lo, g_hi, *refs):
        y_lo, y_hi, c_lo, c_hi = refs[:4]
        refs = refs[4:]
        w_ref, r3_ref, n3_ref, m_ref, xb_ref, to_next, to_previous = refs[:7]
        d0, d1, r_ref, x0, x1 = refs[7:]
        d_refs, x_refs = (d0, d1), (x0, x1)
        shape = (count_j, nk)
        st = Stencil(0, shape)
        even, own_even = st.even, st.even[:nj]
        edge_even = st.even[nj:]
        has_low, has_high = has_neighbours("gy")
        zero = jnp.zeros(shape, jnp.float32)
        for g in (0, pairs + 1):
            for ref in (*d_refs, *x_refs):
                ref[g] = zero

        def edge(a, n, where, mask=False):
            part = 2 if a == 3 else 1
            if where == 1:
                at, refs = a * ni + n - w // part, (y_hi, y_lo)
            elif where == 0:
                at, refs = a * w + n, (c_hi, c_lo)
            else:
                at, refs = 3 * w + h + a * w + n - (w + ni) // part, (c_hi, c_lo)
            hi, lo = refs[0][at], refs[1][at]
            if mask:
                hi, lo = hi * has_high, lo * has_low
            return jnp.concatenate([hi, lo], axis=0)

        def split(q, where):
            e = (2 * q, 2 * q + 1)
            if where == 1:
                mids = [(cls_ref[n - w] + 1).astype(jnp.float32) for n in e]
                bs = [b_ref[n - w] for n in e]
                x = jnp.where(own_even, sample[e[1] - w], sample[e[0] - w])
                g_ref, g_at = g_own, q - h
            else:
                src, g_ref = ((x_lo, g_lo) if where == 0 else (x_hi, g_hi))
                off = 0 if where == 0 else -(w + ni)
                mids = [src[n + off] for n in e]
                bs = [src[2 * w + n + off] for n in e]
                g_at = q + off // 2
                x = src[3 * w + g_at]
            cls = [jnp.concatenate([mids[c], edge(0, e[c], where, True)], axis=0) for c in range(2)]
            b = [jnp.concatenate([bs[c], edge(2, e[c], where)], axis=0) for c in range(2)]
            x1[q + 1] = jnp.concatenate([x, edge(3, q, where, True)], axis=0)
            seeds = [edge(1, e[c], where) for c in range(2)]
            for c in range(2):
                number = jnp.where(even, cls[c], cls[1 - c]).astype(jnp.int32)
                d, m = selected(number, (d_tab, m_tab))
                d_refs[c][q + 1] = d
                m_ref[c, q] = m
                r_ref[0, c, q] = jnp.where(even, b[c], b[1 - c])
                seed = jnp.where(edge_even, seeds[c], seeds[1 - c]).astype(jnp.int32)
                for t, g in enumerate(raw_noises(seed, 0)):
                    out = n3_ref if t == SWEEPS - 1 else r_ref.at[t + 1]
                    out[c, q] = jnp.concatenate([g_ref[t, c, g_at], g], axis=0)

        loop(0, h, lambda q: split(q, 0))
        loop(h, h + ni // 2, lambda q: split(q, 1))
        loop(h + ni // 2, pairs, lambda q: split(q, 2))

        def prepare(q):
            for c in range(2):
                diagonal, inverse, weights = st.weights(d_refs, m_ref[c, q], c, q)
                m_ref[c, q] = diagonal
                for n in range(6):
                    w_ref[n, c, q] = weights[n]
                root = jnp.where(inverse > 0.0, lax.rsqrt(diagonal), 0.0)
                b = r_ref[0, c, q] * inverse
                noise = n3_ref[c, q] * root
                n3_ref[c, q] = noise
                r3_ref[c, q] = b + noise
                r_ref[0, c, q] = b + r_ref[1, c, q] * root
                r_ref[1, c, q] = b + r_ref[2, c, q] * root

        loop(0, pairs, prepare, 2)

        for half in range(2 * SWEEPS - 2):
            t, c = half // 2, half % 2

            def update(q, t=t, c=c):
                x_refs[c][q + 1] = r_ref[t, c, q] + st.gathered(x_refs, w_ref, c, q)

            loop((half + 1) // 2, pairs - (half + 1) // 2, update, UNROLL)

        def write(q):
            xb_ref[q] = x1[q + h + 1, :nj]

        loop(0, ni // 2, write, 4)
        for q in range(h):
            to_previous[q] = x1[q + h + 1, :nj]
            to_next[q] = x1[ni // 2 + q + 1, :nj]

    state = f32(2, pairs, count_j, nk)
    outs = [f32(6, 2, pairs, count_j, nk), state, state, state]
    outs += [f32(ni // 2, nj, nk), f32(h, nj, nk), f32(h, nj, nk)]
    scratch = [
        pltpu.VMEM((pairs + 2, count_j, nk), jnp.float32),
        pltpu.VMEM((pairs + 2, count_j, nk), jnp.float32),
        pltpu.VMEM((SWEEPS, 2, pairs, count_j, nk), jnp.float32),
        pltpu.VMEM((pairs + 2, count_j, nk), jnp.float32),
        pltpu.VMEM((pairs + 2, count_j, nk), jnp.float32),
    ]
    args = (*tables, class_map, mean_shift, sample_field, noise, *planes, *plane_noise, *rows, *corners)
    specs = [SMEM, SMEM] + [VMEM] * (len(args) - 2)
    return call(kernel, "fine_start", outs, args, specs, scratch, START_LIMIT)


def fine_finish(state, black, planes, rows):
    ni, nj, nk = black.shape[0] * 2, black.shape[1], black.shape[2]
    w = FINE_HALO
    h = w // 2
    pairs = (ni + 2 * w) // 2
    count_j = nj + 2 * w
    halo = HALO

    def kernel(w_ref, r3_ref, n3_ref, m_ref, xb_ref, x_lo, x_hi, y_lo, y_hi, *refs):
        fine, rhs, to_next, to_previous = refs[:4]
        x0, x1, res_ref, t_ref, u_ref = refs[4:]
        x_refs = (x0, x1)
        shape = (count_j, nk)
        st = Stencil(0, shape)
        has_low, has_high = has_neighbours("gy")
        has_x = has_neighbours("gx")
        zero = jnp.zeros(shape, jnp.float32)
        for g in (0, pairs + 1):
            for ref in x_refs:
                ref[g] = zero

        def join(q, mid, here=1.0):
            hi, lo = y_hi[q] * (has_high * here), y_lo[q] * (has_low * here)
            x1[q + 1] = jnp.concatenate([mid * here, hi, lo], axis=0)

        for q in range(h):
            join(q, x_lo[q], has_x[0])
            join(h + ni // 2 + q, x_hi[q], has_x[1])
        loop(0, ni // 2, lambda q: join(h + q, xb_ref[q]), 4)

        for c, (start, stop) in enumerate(((0, pairs - 1), (1, pairs - 1))):

            def update(q, c=c):
                x_refs[c][q + 1] = r3_ref[c, q] + st.gathered(x_refs, w_ref, c, q)

            loop(start, stop, update, UNROLL)

        def residual(q):
            red = r3_ref[0, q] - n3_ref[0, q] + st.gathered(x_refs, w_ref, 0, q) - x0[q + 1]
            res_ref[0, q] = m_ref[0, q] * red
            res_ref[1, q] = -m_ref[1, q] * n3_ref[1, q]

        loop(h - 1, h + ni // 2, residual, UNROLL)

        def write(q):
            both = st.whole(x0[q + h + 1], x1[q + h + 1])
            fine[2 * q] = both[0][:nj]
            fine[2 * q + 1] = both[1][:nj]

        loop(0, ni // 2, write, 4)
        coarse = restricted(st, res_ref, h, ni, nj, t_ref, u_ref, 2)
        rhs[...] = coarse
        to_previous[...] = coarse[:halo]
        to_next[...] = coarse[ni // 2 - halo :]

    outs = [f32(ni, nj, nk), f32(ni // 2, nj // 2, LANES)] + [f32(halo, nj // 2, LANES)] * 2
    scratch = [
        pltpu.VMEM((pairs + 2, count_j, nk), jnp.float32),
        pltpu.VMEM((pairs + 2, count_j, nk), jnp.float32),
        pltpu.VMEM((2, pairs, count_j, nk), jnp.float32),
    ] + restrict_scratch(ni, count_j, nk)
    args = (*state, black, *planes, *rows)
    return call(kernel, "fine_finish", outs, args, None, scratch, FINISH_LIMIT)


def prepared(st, level, pairs, d_refs, m_ref, s_ref, v_ref, n_ref, w_ref, unroll):
    def prepare(q):
        for c in range(2):
            diagonal, inverse, weights = st.weights(d_refs, m_ref[c, q], c, q)
            m_ref[c, q] = diagonal
            v_ref[c, q] = inverse
            for n in range(6):
                w_ref[n, c, q] = weights[n]
            root = jnp.where(inverse > 0.0, lax.rsqrt(diagonal), 0.0)
            for t, g in enumerate(raw_noises(s_ref[c, q].astype(jnp.int32), level)):
                n_ref[t, c, q] = g * root

    loop(0, pairs, prepare, unroll)


def swept(st, pairs, b_ref, v_ref, n_ref, w_ref, x_refs, bounds, unroll):
    def update(q, t, c, half):
        if t == 0:
            b_ref[c, q] = b_ref[c, q] * v_ref[c, q]
        total = b_ref[c, q] + n_ref[t, c, q]
        if half:
            total = total + st.gathered(x_refs, w_ref, c, q)
        x_refs[c][q + 1] = total

    for half in range(2 * SWEEPS):
        t, c = half // 2, half % 2
        loop(*bounds(half), functools.partial(update, t=t, c=c, half=half), unroll)


def middle_static(level, statics, static_planes, static_rows):
    ni, nj, nk = statics[0].shape
    w = HALO
    h = w // 2
    count, count_j = ni + 2 * w, nj + 2 * w
    pairs = count // 2
    plane_base = 0 if level == 1 else 3 * w
    row_base = 0 if level == 1 else 3 * (2 * ni + 2 * w)

    def kernel(*refs):
        own, (x_lo, x_hi, y_lo, y_hi), refs = refs[:3], refs[3:7], refs[7:]
        m_ref, v_ref, n_ref, w_ref, d0, d1, s_ref = refs
        d_refs = (d0, d1)
        shape = (count_j, nk)
        st = Stencil(level, shape)
        x_has, y_has = has_neighbours("gx"), has_neighbours("gy")
        zero = jnp.zeros(shape, jnp.float32)
        for g in (0, pairs + 1):
            for ref in d_refs:
                ref[g] = zero

        def plane(src, a, q, k):
            if level == 1:
                return src[a * w + 2 * q + k]
            return src[plane_base + a * h + q, pl.ds(k * nj, nj)]

        def field(a, q, k, where):
            e = 2 * q + k
            if where == 1:
                mid = own[a][e - w]
            else:
                mid = plane((x_lo, x_hi)[where // 2], a, q if where == 0 else q - h - ni // 2, k)
            r = row_base + a * count + e
            hi, lo = y_hi[r], y_lo[r]
            if a == 0:
                hi, lo = hi * y_has[1], lo * y_has[0]
                if where != 1:
                    mid, hi, lo = [v * x_has[where // 2] for v in (mid, hi, lo)]
            return jnp.concatenate([mid, hi, lo], axis=0)

        def split(q, where):
            for a in range(3):
                v = st.whole(field(a, q, 0, where), field(a, q, 1, where))
                for c in range(2):
                    if a == 0:
                        d_refs[c][q + 1] = v[c]
                    else:
                        (m_ref, s_ref)[a - 1][c, q] = v[c]

        loop(0, h, lambda q: split(q, 0), 4)
        loop(h, h + ni // 2, lambda q: split(q, 1), 4)
        loop(h + ni // 2, pairs, lambda q: split(q, 2), 4)
        prepared(st, level, pairs, d_refs, m_ref, s_ref, v_ref, n_ref, w_ref, 2)

    field_shape = (2, pairs, count_j, nk)
    outs = [f32(*field_shape), f32(*field_shape), f32(SWEEPS, *field_shape), f32(6, *field_shape)]
    scratch = [pltpu.VMEM((pairs + 2, count_j, nk), jnp.float32)] * 2
    scratch += [pltpu.VMEM(field_shape, jnp.float32)]
    args = [*statics, *static_planes, *static_rows]
    return call(kernel, f"static_{level}", outs, args, None, scratch)


def middle_level(level, state, rhs, planes, rows, tail=None):
    ni, nj, nk = rhs.shape
    w = HALO
    h = w // 2
    count_j = nj + 2 * w
    pairs = (ni + 2 * w) // 2
    to_coarsest = level == LEVELS - 2

    def kernel(m_ref, v_ref, n_ref, w_ref, own, x_lo, x_hi, y_lo, y_hi, *refs):
        if to_coarsest:
            tail_ref, out, *refs = refs
        else:
            out, to_next, to_previous, *refs = refs
        b_ref, x0, x1, t_ref, u_ref = refs
        x_refs = (x0, x1)
        shape = (count_j, nk)
        st = Stencil(level, shape)
        zero = jnp.zeros(shape, jnp.float32)
        for g in (0, pairs + 1):
            for ref in x_refs:
                ref[g] = zero

        def split(q, where):
            both = []
            for e in (2 * q, 2 * q + 1):
                mid = own[e - w] if where == 1 else (x_lo[e] if where == 0 else x_hi[e - w - ni])
                both.append(jnp.concatenate([mid, y_hi[e], y_lo[e]], axis=0))
            b_ref[0, q], b_ref[1, q] = st.whole(*both)

        loop(0, h, lambda q: split(q, 0), 4)
        loop(h, h + ni // 2, lambda q: split(q, 1), 4)
        loop(h + ni // 2, pairs, lambda q: split(q, 2), 4)

        def bounds(half):
            return half // 2, (ni + w + 2 * SWEEPS - half) // 2 + 1

        swept(st, pairs, b_ref, v_ref, n_ref, w_ref, x_refs, bounds, 4)
        last = SWEEPS - 1

        def residual(q):
            red = b_ref[0, q] + st.gathered(x_refs, w_ref, 0, q) - x0[q + 1]
            b_ref[0, q] = m_ref[0, q] * red
            b_ref[1, q] = -m_ref[1, q] * n_ref[last, 1, q]

        loop(h - 1, h + ni // 2, residual, 4)
        coarse = restricted(st, b_ref, h, ni, nj, t_ref, u_ref, 4)
        if to_coarsest:
            lanes = nk // 4
            coarse = jnp.where(lax.broadcasted_iota(jnp.int32, coarse.shape, 2) < lanes, coarse, 0.0)
            out[...] = tail_ref[...] + pltpu.roll(coarse, 3 * lanes, 2)
        else:
            out[...] = coarse
            to_previous[...] = coarse[:w]
            to_next[...] = coarse[ni // 2 - w :]

    args = [*state, rhs, *planes, *rows]
    outs = [f32(ni // 2, nj // 2, LANES)]
    if to_coarsest:
        args.append(tail)
    else:
        outs += [f32(w, nj // 2, LANES)] * 2
    guarded = pltpu.VMEM((pairs + 2, count_j, nk), jnp.float32)
    scratch = [pltpu.VMEM((2, pairs, count_j, nk), jnp.float32), guarded, guarded]
    scratch += restrict_scratch(ni, count_j, nk)
    return call(kernel, f"level_{level}", outs, args, None, scratch)


def coarsest_level(columns, reach, mi, lanes):
    mj = columns[0].shape[1]
    planes = columns[0].shape[0]
    pairs = planes // 2
    count_j = -(-len(columns) * mj // 8) * 8
    level = LEVELS - 1

    def kernel(*refs):
        blocks = refs[: len(columns)]
        out, d0, d1, m_ref, s_ref, b_ref, v_ref, n_ref, w_ref, x0, x1, t_ref = refs[len(columns) :]
        d_refs, x_refs = (d0, d1), (x0, x1)
        shape = (count_j, LANES)
        st = Stencil(level, shape)
        zero = jnp.zeros(shape, jnp.float32)
        for g in (0, pairs + 1):
            for ref in (*d_refs, *x_refs):
                ref[g] = zero
        t_ref[:, pl.ds(count_j - 8, 8), :] = jnp.zeros((planes, 8, LANES), jnp.float32)
        for g, block in enumerate(blocks):
            t_ref[:, pl.ds(g * mj, mj), :] = block[...]
        inside = st.lane < lanes
        first_i = (lax.axis_index("gx") - reach) * mi
        row = lax.broadcasted_iota(jnp.int32, shape, 0)
        j = row + (lax.axis_index("gy") - reach) * mj
        known = (j >= 0) & (j < lax.axis_size("gy") * mj) & (row < len(columns) * mj) & inside
        known = known.astype(jnp.float32)

        def split(q):
            i = first_i + 2 * q
            here = ((i >= 0) & (i < lax.axis_size("gx") * mi)).astype(jnp.float32)
            both = st.whole(t_ref[2 * q], t_ref[2 * q + 1])
            for c in range(2):
                d_refs[c][q + 1] = both[c] * (known * here)
                for a in range(1, 4):
                    v = pltpu.roll(both[c], LANES - a * lanes, 1)
                    (m_ref, s_ref, b_ref)[a - 1][c, q] = jnp.where(inside, v, 0.0)

        loop(0, pairs, split, pairs)

        def bounds(half):
            more = 2 * SWEEPS - 1 - half
            return (reach * mi - more) // 2, (reach * mi + mi - 1 + more) // 2 + 1

        prepared(st, level, pairs, d_refs, m_ref, s_ref, v_ref, n_ref, w_ref, 2)
        swept(st, pairs, b_ref, v_ref, n_ref, w_ref, x_refs, bounds, pairs)
        for n in range(mi // 2):
            p = reach * mi // 2 + n + 1
            for k, v in enumerate(st.whole(x0[p], x1[p])):
                out[2 * n + k] = v[reach * mj : reach * mj + mj, :lanes]

    guarded = pltpu.VMEM((pairs + 2, count_j, LANES), jnp.float32)
    fields = [(2,), (2,), (2,), (2,), (SWEEPS, 2), (6, 2)]
    scratch = [guarded, guarded]
    scratch += [pltpu.VMEM((*lead, pairs, count_j, LANES), jnp.float32) for lead in fields]
    scratch += [guarded, guarded, pltpu.VMEM((planes, count_j, LANES), jnp.float32)]
    outs = [f32(mi, mj, lanes)]
    (out,) = call(kernel, f"level_{level}", outs, columns, None, scratch, LEVEL_LIMIT)
    return out


def both_ways(to_next, to_previous, axis, ring=True):
    size = lax.axis_size(axis)
    up = [(i, (i + 1) % size) for i in range(size if ring else size - 1)]
    down = [(j, i) for i, j in up]
    return lax.ppermute(to_next, axis, up), lax.ppermute(to_previous, axis, down)


def swapped(first, second, axis):
    size = lax.axis_size(axis)

    def partner(i, start):
        j = i + 1 if i % 2 == start else i - 1
        return j if 0 <= j < size else i

    got = [
        lax.ppermute(block, axis, [(i, partner(i, start)) for i in range(size)])
        for start, block in enumerate((first, second))
    ]

    def kernel(a, b, low, high):
        even = lax.axis_index(axis) % 2 == 0
        has_low, has_high = has_neighbours(axis)
        up = jnp.where(even, 1.0, 0.0)

        def body(n):
            one, two = a[n], b[n]
            low[n] = jnp.where(up > 0.0, two, one) * has_low
            high[n] = jnp.where(up > 0.0, one, two) * has_high

        loop(0, first.shape[0], body, 2)

    return got, lambda pair: call(kernel, "put_in_order", [f32(*first.shape)] * 2, pair)


def window(block, axis, reach):
    size = lax.axis_size(axis)
    got = {0: block}
    for off in range(-reach, reach + 1):
        if off % size not in got:
            got[off % size] = lax.ppermute(block, axis, [(i, (i - off) % size) for i in range(size)])
    return [got[off % size] for off in range(-reach, reach + 1)]


def per_device(sample_field, mean_shift, class_map, noise_seed, diffusion_table, mass_table):
    tables = (diffusion_table, mass_table)
    nk = class_map.shape[2]
    arrays = (class_map, noise_seed, mean_shift, sample_field)

    planes, in_order = swapped(*pack_planes(*arrays), "gx")
    *rows, classes, seed = lax.optimization_barrier(
        (*pack_rows_fine(*arrays), class_map, noise_seed)
    )
    rows = both_ways(*rows, "gy")
    statics1, statics2, static_next, static_previous, tail = coarse_statics(tables, classes, seed)
    seed, static_next, static_previous = lax.optimization_barrier(
        (noise_seed, static_next, static_previous)
    )
    static_planes, static_in_order = swapped(static_next, static_previous, "gx")
    noise = own_noise(seed)
    *planes, noise = lax.optimization_barrier((*planes, noise))
    planes = in_order(planes)

    corners = both_ways(*pack_rows([planes], FINE_HALO, "pack_corners"), "gy")
    plane_noise = halo_noise(*planes)
    *early, low_noise, high_noise, static_low, static_high = lax.optimization_barrier(
        (*rows, *corners, *plane_noise, *static_planes)
    )
    static_planes = static_in_order((static_low, static_high))
    *early, static_next, static_previous = lax.optimization_barrier(
        (*early, *pack_static_rows(static_planes, statics1, statics2))
    )
    rows, corners = early[:2], early[2:]
    static_rows = both_ways(static_next, static_previous, "gy")

    *state, black, to_next, to_previous = fine_start(
        tables, (class_map, mean_shift, sample_field), noise, planes, (low_noise, high_noise), rows, corners
    )
    planes = both_ways(to_next, to_previous, "gx")
    messages = pack_rows([(planes[0], black, planes[1])], FINE_HALO, "pack_rows_black")
    *messages, early, late = lax.optimization_barrier((*messages, *static_rows))
    static_rows = (early, late)
    rows = both_ways(*messages, "gy")
    state1 = middle_static(1, statics1, static_planes, static_rows)
    *rows, s0, s1, s2, s3 = lax.optimization_barrier((*rows, *state1))
    states = [(s0, s1, s2, s3)]

    fine, rhs, to_next, to_previous = fine_finish(state, black, planes, rows)
    to_next, to_previous, early, late = lax.optimization_barrier(
        (to_next, to_previous, *static_rows)
    )
    for level in range(1, LEVELS - 1):
        planes = both_ways(to_next, to_previous, "gx")
        if level == 1:
            state2 = middle_static(2, statics2, static_planes, (early, late))
            *planes, s0, s1, s2, s3 = lax.optimization_barrier((*planes, *state2))
            states.append((s0, s1, s2, s3))
        rows = both_ways(*pack_rows([(planes[0], rhs, planes[1])], HALO, f"pack_rows_{level}"), "gy")
        last = level == LEVELS - 2
        got = middle_level(level, states[level - 1], rhs, planes, rows, tail if last else None)
        if not last:
            rhs, to_next, to_previous = got
    (block,) = got
    mi, mj, _ = block.shape
    reach = -(-2 * SWEEPS // min(mi, mj))
    column = jnp.concatenate(window(block, "gx", reach))
    columns = window(column, "gy", reach)
    return fine, coarsest_level(columns, reach, mi, nk >> (LEVELS - 1))


def solution(mesh):
    spec = P("gx", "gy", None)
    return jax.shard_map(
        per_device,
        mesh=mesh,
        in_specs=(spec, spec, spec, spec, P(), P()),
        out_specs=(spec, spec),
        check_vma=False,
    )
```
